32 devices in a mesh: seq: 4 (over y, x), batch: 8 (over z, core).
Axes of the slice: x: 2, y: 2, z: 4, core: 2. Of those that a mesh axis runs over, the one named last changes fastest.
Arguments:
- tokens: bfloat16 [8, 1024, 2048], P('batch', 'seq'), may hold values from -48 to 48
- seq_count: int32 [8], P('batch'), may hold values from 1 to 4, as said below
- query_weight: bfloat16 [2048, 2048], P(None, 'seq'), may hold values from -0.125 to 0.125
- key_weight: bfloat16 [2048, 256], P(None, 'seq'), may hold values from -0.125 to 0.125
- value_weight: bfloat16 [2048, 256], P(None, 'seq'), may hold values from -0.125 to 0.125
- out_weight: bfloat16 [2048, 2048], P('seq'), may hold values from -0.5 to 0.5
- gate_weight: bfloat16 [2048, 5632], P(None, 'seq'), may hold values from -0.125 to 0.125
- up_weight: bfloat16 [2048, 5632], P(None, 'seq'), may hold values from -0.125 to 0.125
- down_weight: bfloat16 [5632, 2048], P('seq'), may hold values from -0.078125 to 0.078125
- attention_gain: float32 [2048], replicated, may hold values from 0.5 to 1.5
- feedforward_gain: float32 [2048], replicated, may hold values from 0.5 to 1.5
- cotangent: bfloat16 [8, 1024, 2048], P('batch', 'seq'), may hold values from -6 to 6
Outputs:
- layer_out: bfloat16 [8, 1024, 2048], P('batch', 'seq')
- input_grad: float32 [8, 1024, 2048], P('batch', 'seq')
- query_grad: float32 [2048, 2048], P('batch', 'seq')
- key_grad: float32 [2048, 256], P('batch', 'seq')
- value_grad: float32 [2048, 256], P('batch', 'seq')
- out_grad: float32 [2048, 2048], P(('seq', 'batch'))
- gate_grad: float32 [2048, 5632], P('batch', 'seq')
- up_grad: float32 [2048, 5632], P('batch', 'seq')
- down_grad: float32 [5632, 2048], P(('seq', 'batch'))
- attention_gain_grad: float32 [2048], P(('seq', 'batch'))
- feedforward_gain_grad: float32 [2048], P(('seq', 'batch'))
The draws below stay inside these ranges and needn't reach their ends.
Inputs may be any that keep to these rules, and one draw needn't show every extreme that they name: `seq_count`: the 1024 tokens of a group form this many sequences of equal length, one after another; the values are 1, 2 and 4, and each of them occurs in some group.
All inputs are finite; a program needn't handle non-finite values.
Results may differ from the reference program's by a relative error of at most 0.02.
Values may be sent and summed in bfloat16 or wider, within the bound.
No kernel may reach another device: no remote copies, remote signals or barrier semaphores. Data moves between devices by JAX's collectives and lax.ppermute only.
A program may use at most 192 MiB of HBM per device.

```python
import math
import jax
import jax.numpy as jnp
from jax import lax

D = 2048
FF = 5632
H = 32
KVH = 4
HD = 64
GROUPS = 8
GROUP_TOK = 1024
QB = 512
KVD = 256


def draw_tokens(key, part):
    key_values, key_rows, key_columns = jax.random.split(key, 3)
    values = jax.random.truncated_normal(key_values, -4.0, 4.0, (GROUPS, GROUP_TOK, D), jnp.float32)
    row_scale = jnp.exp(jax.random.uniform(key_rows, (GROUPS, GROUP_TOK, 1), jnp.float32, math.log(0.3), math.log(3.0)))
    column_scale = jnp.exp(jax.random.uniform(key_columns, (1, 1, D), jnp.float32, math.log(0.4), math.log(3.0)))
    return (values * row_scale * column_scale).astype(jnp.bfloat16)


def draw_seq_count(key, part):
    key_kind, key_place = jax.random.split(key)
    kinds = jax.random.randint(key_kind, (GROUPS,), 0, 3, dtype=jnp.int32)
    order = jax.random.permutation(key_place, GROUPS)
    forced = jnp.zeros((GROUPS,), jnp.int32).at[order[:3]].set(jnp.arange(3, dtype=jnp.int32))
    marked = jnp.zeros((GROUPS,), jnp.int32).at[order[:3]].set(1)
    kinds = jnp.where(marked > 0, forced, kinds)
    return jnp.left_shift(jnp.ones((GROUPS,), jnp.int32), kinds)


def steps_of(stream_key, dims, pieces, low, largest):
    factor_of = 1.0
    for axis_at, blocks in pieces:
        heights = jax.random.uniform(jax.random.fold_in(jax.random.fold_in(stream_key, 6), axis_at), (blocks,), jnp.float32, low / len(pieces), largest / len(pieces))
        factor_of = factor_of * jnp.repeat(jnp.exp(heights), dims[axis_at] // blocks).reshape((-1,) + (1,) * (len(dims) - 1 - axis_at))
    return factor_of


def centred(stream_key, shape, scale, reach, pieces=(), held_as=jnp.bfloat16):
    level = steps_of(stream_key, shape, pieces, -0.22, 0.18) if pieces else 1.0
    drawn = jax.random.normal(stream_key, shape, jnp.float32) * scale * level
    return jnp.minimum(jnp.maximum(drawn, -reach), reach).astype(held_as)


def setup_inputs(seed: int = 0) -> dict:
    streams_of = jax.random.split(jax.random.key(seed), 13)
    tokens = draw_tokens(jax.random.fold_in(streams_of[12], 71), 0)
    seq_count = draw_seq_count(jax.random.fold_in(streams_of[12], 71), 0)
    query_weight = centred(streams_of[2], (D, D), D ** -0.5, 0.125, ((1, 4),))
    key_weight = centred(streams_of[3], (D, KVD), D ** -0.5, 0.125, ((1, 4),))
    value_weight = centred(streams_of[4], (D, KVD), D ** -0.5, 0.125, ((1, 4),))
    out_weight = centred(streams_of[5], (D, D), (D // 16) ** -0.5, 0.5, ((0, 4),))
    gate_weight = centred(streams_of[6], (D, FF), D ** -0.5, 0.125, ((1, 4),))
    up_weight = centred(streams_of[7], (D, FF), D ** -0.5, 0.125, ((1, 4),))
    down_weight = centred(streams_of[8], (FF, D), FF ** -0.5, 0.078125, ((0, 4),))
    attention_gain = jnp.clip(1.0 + 0.1 * jax.random.normal(streams_of[9], (D,), jnp.float32), 0.5, 1.5)
    feedforward_gain = jnp.clip(1.0 + 0.1 * jax.random.normal(streams_of[10], (D,), jnp.float32), 0.5, 1.5)
    cotangent = centred(streams_of[11], (GROUPS, GROUP_TOK, D), 1.0, 6.0, ((0, 8), (1, 4)))
    return {"tokens": tokens, "seq_count": seq_count, "query_weight": query_weight, "key_weight": key_weight, "value_weight": value_weight, "out_weight": out_weight, "gate_weight": gate_weight, "up_weight": up_weight, "down_weight": down_weight, "attention_gain": attention_gain, "feedforward_gain": feedforward_gain, "cotangent": cotangent}


EPS = 1e-05
NEG = -1e+30

@jax.custom_vjp
def low(v):
    return lax.optimization_barrier(v.astype(jnp.bfloat16)).astype(jnp.float32)

@jax.custom_vjp
def low_back(v):
    return v

def low_keep(v):
    return (low(v), None)

def low_pass(kept, grad):
    return (grad,)

def back_keep(v):
    return (v, None)

def back_low(kept, grad):
    return (low(grad),)
low.defvjp(low_keep, low_pass)
low_back.defvjp(back_keep, back_low)

def highest(left, right):
    return jnp.dot(left, right, precision=lax.Precision.HIGHEST, preferred_element_type=jnp.float32)

def rms_norm(values, gain):
    inverse = lax.rsqrt(lax.optimization_barrier(jnp.mean(values * values, axis=-1, keepdims=True)) + EPS)
    return values * inverse * gain

def rotation(positions):
    freq_index = jnp.arange(HD // 2, dtype=jnp.float32)
    inverse = jnp.exp(freq_index * (-2.0 * math.log(10000.0) / HD))
    angles = positions.astype(jnp.float32)[:, None] * inverse[None, :]
    return (jnp.cos(angles)[:, None, :], jnp.sin(angles)[:, None, :])

def rotate(values, cosine_table, sine_table):
    half_width = HD // 2
    first_half = values[..., :half_width]
    second_half = values[..., half_width:]
    return jnp.concatenate([first_half * cosine_table - second_half * sine_table, second_half * cosine_table + first_half * sine_table], axis=-1)

def attention(queries, keys, values_all, starts):
    score_scale = 1.0 / math.sqrt(HD)
    key_index = jnp.arange(GROUP_TOK, dtype=jnp.int32)

    def one_block(block_index):
        row_first = block_index * QB
        query_block = lax.dynamic_slice_in_dim(queries, row_first, QB, 0)
        query_index = row_first + jnp.arange(QB, dtype=jnp.int32)
        query_starts = lax.dynamic_slice_in_dim(starts, row_first, QB, 0)
        raw_scores = jnp.einsum('qngd,knd->ngqk', query_block, keys, precision=lax.Precision.HIGHEST)
        allowed = (key_index[None, :] <= query_index[:, None]) & (key_index[None, :] >= query_starts[:, None])
        scores = low_back(jnp.where(allowed, raw_scores * score_scale, NEG))
        row_max = lax.optimization_barrier(jnp.max(scores, axis=-1, keepdims=True))
        exponent = jnp.exp(scores - row_max)
        soft_probs = exponent / lax.optimization_barrier(jnp.sum(exponent, axis=-1, keepdims=True))
        return jnp.einsum('ngqk,knd->qngd', low(soft_probs), values_all, precision=lax.Precision.HIGHEST)
    blocks = lax.map(jax.checkpoint(one_block), jnp.arange(GROUP_TOK // QB, dtype=jnp.int32))
    return blocks.reshape(GROUP_TOK, H * HD)

def layer(inputs, weights, seq_number):
    query_weight, key_weight, value_weight, out_weight, gate_weight, up_weight, down_weight, attention_gain, feedforward_gain = weights
    token_index = jnp.arange(GROUP_TOK, dtype=jnp.int32)
    seq_length = GROUP_TOK // seq_number
    starts = token_index // seq_length * seq_length
    cosine_table, sine_table = rotation(token_index - starts)
    normed_one = low(rms_norm(inputs, attention_gain))
    query_pre = low_back(highest(normed_one, query_weight)).reshape(GROUP_TOK, H, HD)
    key_pre = low_back(highest(normed_one, key_weight)).reshape(GROUP_TOK, KVH, HD)
    value_heads = low(low_back(highest(normed_one, value_weight))).reshape(GROUP_TOK, KVH, HD)
    query_heads = low(low_back(rotate(query_pre, cosine_table, sine_table))).reshape(GROUP_TOK, KVH, H // KVH, HD)
    key_heads = low(low_back(rotate(key_pre, cosine_table, sine_table)))
    attended = low(low_back(attention(query_heads, key_heads, value_heads, starts)))
    branch = low_back(highest(attended, out_weight))
    hidden = inputs + branch
    normed_two = low(rms_norm(hidden, feedforward_gain))
    gate = low_back(highest(normed_two, gate_weight))
    upward = low_back(highest(normed_two, up_weight))
    mixed = low(jax.nn.silu(gate) * upward)
    return hidden + low_back(highest(mixed, down_weight))

def reference(tokens, seq_count, query_weight, key_weight, value_weight, out_weight, gate_weight, up_weight, down_weight, attention_gain, feedforward_gain, cotangent):
    params = (query_weight.astype(jnp.float32), key_weight.astype(jnp.float32), value_weight.astype(jnp.float32), out_weight.astype(jnp.float32), gate_weight.astype(jnp.float32), up_weight.astype(jnp.float32), down_weight.astype(jnp.float32), attention_gain.astype(jnp.float32), feedforward_gain.astype(jnp.float32))

    def step(totals, item):
        group_tokens, seq_number, group_cotangent = item
        result, pullback = jax.vjp(lambda inputs, weights: layer(inputs, weights, seq_number), group_tokens.astype(jnp.float32), params)
        input_part, weight_parts = pullback(group_cotangent.astype(jnp.float32))
        new_totals = jax.tree.map(lambda left, right: left + right, totals, weight_parts)
        return (new_totals, (result.astype(jnp.bfloat16), input_part))
    zeros = jax.tree.map(lambda array: jnp.zeros(array.shape, jnp.float32), params)
    totals, (outputs, input_grads) = lax.scan(step, zeros, (tokens, seq_count, cotangent))
    return (outputs, input_grads, totals[0], totals[1], totals[2], totals[3], totals[4], totals[5], totals[6], totals[7], totals[8])
```

```python
import math

import jax
import jax.numpy as jnp
from jax import lax
from jax.experimental import pallas as pl
from jax.experimental.pallas import tpu as pltpu
from jax.sharding import PartitionSpec as P

HD = 64
EPS = 1e-05
NEG = -1e30
F32 = jnp.float32
BF16 = jnp.bfloat16


def mm(a, b):
    return lax.dot_general(a, b, (((1,), (0,)), ((), ())), preferred_element_type=F32)


def mm_nt(a, b):
    return lax.dot_general(a, b, (((1,), (1,)), ((), ())), preferred_element_type=F32)


def mm_tn(a, b):
    return lax.dot_general(a, b, (((0,), (0,)), ((), ())), preferred_element_type=F32)


def exchange(values, even_mask, odd_mask):
    seq_parts = lax.axis_size("seq")
    batch_parts = lax.axis_size("batch")
    pairs = []
    for part in range(seq_parts):
        for group in range(batch_parts):
            mask = even_mask if group % 2 == 0 else odd_mask
            pairs.append((part * batch_parts + group, (part ^ mask) * batch_parts + group))
    return lax.ppermute(values, ("seq", "batch"), pairs)


def first_swap(values):
    return exchange(values, 1, 2)


def second_swap(values):
    return exchange(values, 2, 1)


def gather_blocks(block):
    near = first_swap(block)
    side = second_swap(block)
    far = second_swap(near)
    return [block, near, side, far]


def scatter_sum(upper, lower):
    rows = lower.shape[0] // 2
    arrived = second_swap(upper)
    passed = (lower[rows:].astype(F32) + arrived[rows:].astype(F32)).astype(BF16)
    last = first_swap(passed)
    return lower[:rows].astype(F32) + arrived[:rows].astype(F32) + last.astype(F32)


def swap_halves(values):
    lane = lax.broadcasted_iota(jnp.int32, values.shape, 1)
    ahead = pltpu.roll(values, values.shape[1] - HD // 2, 1)
    behind = pltpu.roll(values, HD // 2, 1)
    return jnp.where(lane % HD < HD // 2, ahead, behind)


def padded_keys(keys_values):
    lane = lax.broadcasted_iota(jnp.int32, keys_values.shape, 1)
    zero = jnp.zeros_like(keys_values)
    left = jnp.where(lane < HD, keys_values, zero)
    right = pltpu.roll(left, HD, 1)
    return jnp.concatenate([left, right], axis=0)


def padded_values(keys_values):
    lane = lax.broadcasted_iota(jnp.int32, keys_values.shape, 1)
    zero = jnp.zeros_like(keys_values)
    right = jnp.where(lane >= HD, keys_values, zero)
    left = pltpu.roll(right, HD, 1)
    return jnp.concatenate([left, right], axis=0)


def attention_forward_kernel(
    info, query_ref, kv_ref, cos_ref, sin_ref, cos_all, sin_all,
    attended_ref, rotated_ref, kv_out, lse_ref, keys_s, values_s, acc_s, max_s,
):
    step = pl.program_id(0)
    rows = query_ref.shape[0]
    pairs = query_ref.shape[1] // 128
    blocks = kv_ref.shape[0] // rows

    @pl.when(step == 0)
    def _():
        for part in range(blocks):
            here = pl.ds(part * rows, rows)
            kv = kv_ref[here, :]
            lane = lax.broadcasted_iota(jnp.int32, kv.shape, 1)
            turned = kv * cos_all[here, :] + swap_halves(kv) * sin_all[here, :]
            kv = jnp.where(lane < HD, turned, kv).astype(BF16).astype(F32)
            kv_out[here, :] = kv.astype(BF16)
            keys_s[part] = (padded_keys(kv) * (1.0 / math.sqrt(HD))).astype(BF16)
            both = padded_values(kv)
            lane2 = lax.broadcasted_iota(jnp.int32, both.shape, 1)
            row2 = lax.broadcasted_iota(jnp.int32, both.shape, 0)
            ones = jnp.where((lane2 < HD) == (row2 < rows), 1.0, 0.0)
            values_s[part] = jnp.concatenate([both, ones], axis=1).astype(BF16)

    own = info[step]
    low = info[2 * blocks + step]
    row = lax.broadcasted_iota(jnp.int32, (rows, rows), 0)
    column = lax.broadcasted_iota(jnp.int32, (rows, rows), 1)
    allowed = column <= row
    left_half = lax.broadcasted_iota(jnp.int32, (rows, 2 * 128), 1) % 128 < HD
    at = info[blocks + own]
    for pair in range(pairs):
        cols = pl.ds(pair * 128, 128)
        query = query_ref[:, cols]
        query = (query * cos_ref[...] + swap_halves(query) * sin_ref[...]).astype(BF16)
        rotated_ref[:, cols] = query
        scores = mm_nt(query, keys_s[at])
        probs = []
        for head in range(2):
            part = jnp.where(allowed, scores[:, head * rows : (head + 1) * rows], NEG)
            top = jnp.max(part, axis=1, keepdims=True)
            probs.append(jnp.exp(part - top))
            max_s[2 * pair + head] = jnp.broadcast_to(top, (rows, 128))
        acc_s[pair] = mm(jnp.concatenate(probs, axis=1).astype(BF16), values_s[at])

    for back in range(1, blocks):

        @pl.when(own - back >= low)
        def _():
            where_ = info[blocks + jnp.maximum(own - back, 0)]
            for pair in range(pairs):
                query = rotated_ref[:, pl.ds(pair * 128, 128)]
                scores = mm_nt(query, keys_s[where_])
                probs = []
                scale = []
                for head in range(2):
                    part = scores[:, head * rows : (head + 1) * rows]
                    before = max_s[2 * pair + head][:, :1]
                    top = jnp.maximum(before, jnp.max(part, axis=1, keepdims=True))
                    probs.append(jnp.exp(part - top))
                    scale.append(jnp.exp(before - top))
                    max_s[2 * pair + head] = jnp.broadcast_to(top, (rows, 128))
                factor = jnp.where(left_half, scale[0], scale[1])
                acc_s[pair] = acc_s[pair] * factor + mm(
                    jnp.concatenate(probs, axis=1).astype(BF16), values_s[where_]
                )

    lane = lax.broadcasted_iota(jnp.int32, (rows, 128), 1)
    logs = jnp.zeros((rows, 128), F32)
    for pair in range(pairs):
        total = acc_s[pair][:, 128:]
        attended_ref[:, pl.ds(pair * 128, 128)] = (acc_s[pair][:, :128] / total).astype(BF16)
        log_total = jnp.log(total)
        for head in range(2):
            value = max_s[2 * pair + head] + jnp.broadcast_to(
                log_total[:, head * HD : head * HD + 1], (rows, 128)
            )
            logs = jnp.where(lane == 2 * pair + head, value, logs)
    lse_ref[...] = jnp.transpose(logs)[: 2 * pairs, :]


def attention_forward(info, qkv, cosine, sine, rows):
    total, width = qkv.shape
    blocks = total // rows
    query_width = width - 2 * HD
    pairs = query_width // 128
    last = query_width // 128
    return pl.pallas_call(
        attention_forward_kernel,
        grid_spec=pltpu.PrefetchScalarGridSpec(
            num_scalar_prefetch=1,
            grid=(blocks,),
            in_specs=[
                pl.BlockSpec((rows, query_width), lambda j, info: (j, 0)),
                pl.BlockSpec((total, 128), lambda j, info: (0, last)),
                pl.BlockSpec((rows, 128), lambda j, info: (j, 0)),
                pl.BlockSpec((rows, 128), lambda j, info: (j, 0)),
                pl.BlockSpec((total, 128), lambda j, info: (0, 0)),
                pl.BlockSpec((total, 128), lambda j, info: (0, 0)),
            ],
            out_specs=[
                pl.BlockSpec((rows, query_width), lambda j, info: (j, 0)),
                pl.BlockSpec((rows, query_width), lambda j, info: (j, 0)),
                pl.BlockSpec((total, 128), lambda j, info: (0, 0)),
                pl.BlockSpec((2 * pairs, rows), lambda j, info: (0, j)),
            ],
            scratch_shapes=[
                pltpu.VMEM((blocks, 2 * rows, 128), BF16),
                pltpu.VMEM((blocks, 2 * rows, 256), BF16),
                pltpu.VMEM((pairs, rows, 256), F32),
                pltpu.VMEM((2 * pairs, rows, 128), F32),
            ],
        ),
        out_shape=[
            jax.ShapeDtypeStruct((total, query_width), BF16),
            jax.ShapeDtypeStruct((total, query_width), BF16),
            jax.ShapeDtypeStruct((total, 128), BF16),
            jax.ShapeDtypeStruct((2 * pairs, total), F32),
        ],
        name="attention_forward",
    )(info, qkv, qkv, cosine, sine, cosine, sine)


def attention_backward_kernel(
    info, query_ref, att_ref, grad_ref, lse_ref, kv_ref, cos_ref, sin_ref, cos_all, sin_all,
    out_ref, keys_s, values_s, key_acc, value_acc, query_acc, delta_s,
):
    step = pl.program_id(0)
    rows = query_ref.shape[0]
    query_width = query_ref.shape[1]
    pairs = query_width // 128
    blocks = kv_ref.shape[0] // rows

    @pl.when(step == 0)
    def _():
        for part in range(blocks):
            kv = kv_ref[pl.ds(part * rows, rows), :].astype(F32)
            keys_s[part] = (padded_keys(kv) * (1.0 / math.sqrt(HD))).astype(BF16)
            values_s[part] = padded_values(kv).astype(BF16)
        key_acc[...] = jnp.zeros_like(key_acc)
        value_acc[...] = jnp.zeros_like(value_acc)

    own = info[step]
    low = info[2 * blocks + step]
    at = info[blocks + own]
    key_index = lax.broadcasted_iota(jnp.int32, (2 * rows, rows), 0) % rows
    query_index = lax.broadcasted_iota(jnp.int32, (2 * rows, rows), 1)
    allowed = key_index <= query_index
    top_half = lax.broadcasted_iota(jnp.int32, (2 * rows, rows), 0) < rows

    products = att_ref[...].astype(F32) * grad_ref[...].astype(F32)
    head_row = lax.broadcasted_iota(jnp.int32, (2 * pairs, query_width), 0)
    head_col = lax.broadcasted_iota(jnp.int32, (2 * pairs, query_width), 1) // HD
    picker = jnp.where(head_row == head_col, 1.0, 0.0)
    delta_s[...] = lax.dot_general(
        picker, products, (((1,), (1,)), ((), ())),
        precision=lax.Precision.HIGHEST, preferred_element_type=F32,
    )

    def one_block(where_, masked):
        keys = keys_s[where_]
        values = values_s[where_]
        for pair in range(pairs):
            cols = pl.ds(pair * 128, 128)
            query = query_ref[:, cols]
            grad = grad_ref[:, cols]
            lse = jnp.where(
                top_half, lse_ref[2 * pair : 2 * pair + 1, :], lse_ref[2 * pair + 1 : 2 * pair + 2, :]
            )
            delta = jnp.where(
                top_half, delta_s[2 * pair : 2 * pair + 1, :], delta_s[2 * pair + 1 : 2 * pair + 2, :]
            )
            scores = mm_nt(keys, query) - lse
            if masked:
                scores = jnp.where(allowed, scores, NEG)
            probs = jnp.exp(scores)
            grad_probs = mm_nt(values, grad)
            grad_scores = (probs * (grad_probs - delta)).astype(BF16)
            value_acc[where_] += mm(probs.astype(BF16), grad)
            key_acc[where_] += mm(grad_scores, query)
            part = mm_tn(grad_scores, keys)
            if masked:
                query_acc[:, cols] = part
            else:
                query_acc[:, cols] += part

    one_block(at, True)
    for back in range(1, blocks):

        @pl.when(own - back >= low)
        def _():
            one_block(info[blocks + jnp.maximum(own - back, 0)], False)

    here = pl.ds(pl.multiple_of(step * rows, rows), rows)
    for pair in range(pairs):
        cols = pl.ds(pair * 128, 128)
        grad = query_acc[:, cols].astype(BF16).astype(F32)
        out_ref[here, cols] = (grad * cos_ref[...] - swap_halves(grad) * sin_ref[...]).astype(BF16)

    @pl.when(step == pl.num_programs(0) - 1)
    def _():
        lane = lax.broadcasted_iota(jnp.int32, (rows, 128), 1)
        for part in range(blocks):
            spot = pl.ds(part * rows, rows)
            key_grad = key_acc[part]
            key_grad = key_grad[:rows] + pltpu.roll(key_grad[rows:], HD, 1)
            key_grad = (key_grad * (1.0 / math.sqrt(HD))).astype(BF16).astype(F32)
            value_grad = value_acc[part]
            value_grad = pltpu.roll(value_grad[:rows], HD, 1) + value_grad[rows:]
            turned = key_grad * cos_all[spot, :] - swap_halves(key_grad) * sin_all[spot, :]
            out_ref[spot, pl.ds(query_width, 128)] = jnp.where(lane < HD, turned, value_grad).astype(BF16)


def attention_backward(info, query, attended, grad, lse, kv, cosine, sine, rows):
    total, query_width = query.shape
    blocks = total // rows
    pairs = query_width // 128
    row_block = pl.BlockSpec((rows, query_width), lambda j, info: (j, 0))
    table_block = pl.BlockSpec((rows, 128), lambda j, info: (j, 0))
    whole = pl.BlockSpec((total, 128), lambda j, info: (0, 0))
    return pl.pallas_call(
        attention_backward_kernel,
        grid_spec=pltpu.PrefetchScalarGridSpec(
            num_scalar_prefetch=1,
            grid=(blocks,),
            in_specs=[
                row_block, row_block, row_block,
                pl.BlockSpec((2 * pairs, rows), lambda j, info: (0, j)),
                whole, table_block, table_block, whole, whole,
            ],
            out_specs=pl.BlockSpec((total, query_width + 128), lambda j, info: (0, 0)),
            scratch_shapes=[
                pltpu.VMEM((blocks, 2 * rows, 128), BF16),
                pltpu.VMEM((blocks, 2 * rows, 128), BF16),
                pltpu.VMEM((blocks, 2 * rows, 128), F32),
                pltpu.VMEM((blocks, 2 * rows, 128), F32),
                pltpu.VMEM((rows, query_width), F32),
                pltpu.VMEM((2 * pairs, rows), F32),
            ],
        ),
        out_shape=jax.ShapeDtypeStruct((total, query_width + 128), BF16),
        name="attention_backward",
    )(info, query, attended, grad, lse, kv, cosine, sine, cosine, sine)


def norm_scale(values):
    return lax.rsqrt(jnp.mean(values * values, axis=-1, keepdims=True) + EPS)


def norm_backward(values, scale, gain, grads):
    weighted = grads * gain
    gain_grad = jnp.sum(grads * values * scale, axis=0)
    cubed = scale * scale * scale
    value_grad = scale * weighted - values * cubed * jnp.mean(weighted * values, axis=-1, keepdims=True)
    return gain_grad, value_grad


def over_batch(term):
    return lax.psum_scatter(term.astype(BF16), "batch", scatter_dimension=0, tiled=True).astype(F32)


def shards(
    tokens, seq_count, query_weight, key_weight, value_weight, out_weight,
    gate_weight, up_weight, down_weight, attention_gain, feedforward_gain, cotangent,
):
    seq_parts = lax.axis_size("seq")
    batch_parts = lax.axis_size("batch")
    part = lax.axis_index("seq")
    parity = lax.axis_index("batch") % 2
    rows = tokens.shape[1]
    group_rows = rows * seq_parts
    width = tokens.shape[2]

    order = jnp.arange(seq_parts, dtype=jnp.int32)
    swapped = ((order & 1) << 1) | (order >> 1)
    masks = jnp.where(parity == 0, order, swapped)
    owners = part ^ masks
    other = part ^ order
    spots = jnp.where(parity == 0, other, ((other & 1) << 1) | (other >> 1))
    seq_length = group_rows // seq_count[0]
    firsts = (owners * rows) // seq_length * seq_length // rows
    info = jnp.concatenate([owners, spots, firsts]).astype(jnp.int32)

    index = (owners[:, None] * rows + jnp.arange(rows, dtype=jnp.int32)[None, :]).reshape(-1)
    places = index - index // seq_length * seq_length
    lane = jnp.arange(128, dtype=jnp.int32)
    inverse = jnp.exp((lane % (HD // 2)).astype(F32) * (-2.0 * math.log(10000.0) / HD))
    angles = places.astype(F32)[:, None] * inverse[None, :]
    cosine = jnp.cos(angles)
    sine = jnp.sin(angles) * jnp.where(lane % HD < HD // 2, -1.0, 1.0)[None, :]

    inputs = tokens[0].astype(F32)
    scale_one = norm_scale(inputs)
    normed_one = (inputs * scale_one * attention_gain).astype(BF16)
    qkv_weight = jnp.concatenate([query_weight, key_weight, value_weight], axis=1)
    normed_one_blocks = gather_blocks(normed_one)
    qkv = jnp.concatenate([mm(block, qkv_weight) for block in normed_one_blocks], axis=0)
    cotangent_blocks = gather_blocks(cotangent[0])

    attended, query, kv, lse = attention_forward(info, qkv, cosine, sine, rows)
    half = group_rows // 2
    branch_upper = mm(attended[half:], out_weight).astype(BF16)
    branch_lower = mm(attended[:half], out_weight).astype(BF16)
    hidden = inputs + scatter_sum(branch_upper, branch_lower)

    grad_rows = jnp.concatenate(cotangent_blocks, axis=0)
    grad_mixed = mm_nt(grad_rows, down_weight)

    scale_two = norm_scale(hidden)
    normed_two = (hidden * scale_two * feedforward_gain).astype(BF16)
    normed_two_rows = jnp.concatenate(gather_blocks(normed_two), axis=0)
    gate = mm(normed_two_rows, gate_weight)
    upward = mm(normed_two_rows, up_weight)
    sigmoid_gate = jax.nn.sigmoid(gate)
    activated = gate * sigmoid_gate
    mixed = (activated * upward).astype(BF16)
    grad_gate = (grad_mixed * upward * sigmoid_gate * (1.0 + gate * (1.0 - sigmoid_gate))).astype(BF16)
    grad_upward = (grad_mixed * activated).astype(BF16)

    def back_rows(first, last):
        return (
            mm_nt(grad_gate[first:last], gate_weight) + mm_nt(grad_upward[first:last], up_weight)
        ).astype(BF16)

    grad_normed_two = scatter_sum(back_rows(half, group_rows), back_rows(0, half))
    down_grad = over_batch(mm_tn(mixed, grad_rows))
    gate_grad = over_batch(mm_tn(normed_two_rows, grad_gate))
    up_grad = over_batch(mm_tn(normed_two_rows, grad_upward))

    grad_out = cotangent[0].astype(F32)
    feed_gain_term, grad_hidden_norm = norm_backward(hidden, scale_two, feedforward_gain, grad_normed_two)
    grad_hidden = grad_out + grad_hidden_norm
    grad_branch_blocks = gather_blocks(grad_hidden.astype(BF16))
    grad_branch_rows = jnp.concatenate(grad_branch_blocks, axis=0)
    grad_attended = mm_nt(grad_branch_rows, out_weight).astype(BF16)
    out_grad = over_batch(mm_tn(attended, grad_branch_rows))

    ffn_upper = mm(mixed[half:], down_weight).astype(BF16)
    ffn_lower = mm(mixed[:half], down_weight).astype(BF16)
    layer_out = (hidden + scatter_sum(ffn_upper, ffn_lower)).astype(BF16)

    grad_qkv = attention_backward(info, query, attended, grad_attended, lse, kv, cosine, sine, rows)
    normed_one_rows = jnp.concatenate(normed_one_blocks, axis=0)
    grad_normed_one = scatter_sum(
        mm_nt(grad_qkv[half:], qkv_weight).astype(BF16), mm_nt(grad_qkv[:half], qkv_weight).astype(BF16)
    )
    qkv_grad = over_batch(mm_tn(normed_one_rows, grad_qkv))
    attention_gain_term, grad_inputs_norm = norm_backward(inputs, scale_one, attention_gain, grad_normed_one)
    input_grad = grad_hidden + grad_inputs_norm

    devices = seq_parts * batch_parts
    gains = jnp.concatenate(
        [attention_gain_term.reshape(devices, -1), feed_gain_term.reshape(devices, -1)], axis=1
    )
    gains = jnp.sum(lax.all_to_all(gains, ("seq", "batch"), 0, 0, tiled=True), axis=0)
    share = width // devices
    query_width = query_weight.shape[1]
    key_width = key_weight.shape[1]
    return (
        layer_out[None],
        input_grad[None],
        qkv_grad[:, :query_width],
        qkv_grad[:, query_width : query_width + key_width],
        qkv_grad[:, query_width + key_width :],
        out_grad,
        gate_grad,
        up_grad,
        down_grad,
        gains[:share],
        gains[share:],
    )


def solution(mesh):
    return jax.shard_map(
        shards,
        mesh=mesh,
        in_specs=(
            P("batch", "seq", None),
            P("batch"),
            P(None, "seq"),
            P(None, "seq"),
            P(None, "seq"),
            P("seq", None),
            P(None, "seq"),
            P(None, "seq"),
            P("seq", None),
            P(),
            P(),
            P("batch", "seq", None),
        ),
        out_specs=(
            P("batch", "seq", None),
            P("batch", "seq", None),
            P("batch", "seq"),
            P("batch", "seq"),
            P("batch", "seq"),
            P(("seq", "batch"), None),
            P("batch", "seq"),
            P("batch", "seq"),
            P(("seq", "batch"), None),
            P(("seq", "batch")),
            P(("seq", "batch")),
        ),
        check_vma=False,
    )
```

```python
import functools
import math

import jax
import jax.numpy as jnp
from jax import lax
from jax.experimental import pallas as pl
from jax.experimental.pallas import tpu as pltpu
from jax.sharding import PartitionSpec as P

HD = 64
EPS = 1e-05
NEG = -1e30
F32 = jnp.float32
BF16 = jnp.bfloat16


def mm(a, b):
    return lax.dot_general(a, b, (((1,), (0,)), ((), ())), preferred_element_type=F32)


def mm_nt(a, b):
    return lax.dot_general(a, b, (((1,), (1,)), ((), ())), preferred_element_type=F32)


def mm_tn(a, b):
    return lax.dot_general(a, b, (((0,), (0,)), ((), ())), preferred_element_type=F32)


def exchange(values, even_mask, odd_mask):
    seq_parts = lax.axis_size("seq")
    batch_parts = lax.axis_size("batch")
    pairs = []
    for part in range(seq_parts):
        for group in range(batch_parts):
            mask = even_mask if group % 2 == 0 else odd_mask
            pairs.append((part * batch_parts + group, (part ^ mask) * batch_parts + group))
    return lax.ppermute(values, ("seq", "batch"), pairs)


def after(value, *others):
    return lax.optimization_barrier((value, *others))[0]


def first_swap(values):
    return exchange(values, 1, 2)


def second_swap(values):
    return exchange(values, 2, 1)


def split_sum(lower, arrived):
    rows = lower.shape[0] // 2
    total = lower.astype(F32) + arrived.astype(F32)
    return total[:rows], total[rows:].astype(BF16)


def swap_halves(values):
    lane = lax.broadcasted_iota(jnp.int32, values.shape, 1)
    ahead = pltpu.roll(values, values.shape[1] - HD // 2, 1)
    behind = pltpu.roll(values, HD // 2, 1)
    return jnp.where(lane % HD < HD // 2, ahead, behind)


def padded_keys(keys_values):
    lane = lax.broadcasted_iota(jnp.int32, keys_values.shape, 1)
    zero = jnp.zeros_like(keys_values)
    left = jnp.where(lane < HD, keys_values, zero)
    right = pltpu.roll(left, HD, 1)
    return jnp.concatenate([left, right], axis=0)


def padded_values(keys_values):
    lane = lax.broadcasted_iota(jnp.int32, keys_values.shape, 1)
    zero = jnp.zeros_like(keys_values)
    right = jnp.where(lane >= HD, keys_values, zero)
    left = pltpu.roll(right, HD, 1)
    return jnp.concatenate([left, right], axis=0)


def attention_forward_kernel(
    first, info, query_ref, kv_ref, cos_ref, sin_ref, cos_all, sin_all,
    attended_ref, rotated_ref, kv_out, lse_ref, keys_s, values_s, acc_s, max_s,
):
    step = pl.program_id(0) + first
    rows = query_ref.shape[0]
    pairs = query_ref.shape[1] // 128
    blocks = kv_ref.shape[0] // rows

    @pl.when(step == first)
    def _():
        for part in range(blocks):
            here = pl.ds(part * rows, rows)
            kv = kv_ref[here, :]
            lane = lax.broadcasted_iota(jnp.int32, kv.shape, 1)
            turned = kv * cos_all[here, :] + swap_halves(kv) * sin_all[here, :]
            kv = jnp.where(lane < HD, turned, kv).astype(BF16).astype(F32)
            kv_out[here, :] = kv.astype(BF16)
            keys_s[part] = (padded_keys(kv) * (1.0 / math.sqrt(HD))).astype(BF16)
            both = jnp.transpose(padded_values(kv))
            feature = lax.broadcasted_iota(jnp.int32, both.shape, 0)
            key = lax.broadcasted_iota(jnp.int32, both.shape, 1)
            ones = jnp.where((feature < HD) == (key < rows), 1.0, 0.0)
            values_s[part] = jnp.concatenate([both, ones], axis=0).astype(BF16)

    own = info[step]
    low = info[2 * blocks + step]
    key_index = lax.broadcasted_iota(jnp.int32, (2 * rows, rows), 0) % rows
    query_index = lax.broadcasted_iota(jnp.int32, (2 * rows, rows), 1)
    allowed = key_index <= query_index
    at = info[blocks + own]

    def spread(upper, lower, height):
        return jnp.concatenate(
            [jnp.broadcast_to(upper, (height, rows)), jnp.broadcast_to(lower, (height, rows))], axis=0
        )

    for pair in range(pairs):
        cols = pl.ds(pair * 128, 128)
        query = query_ref[:, cols]
        query = (query * cos_ref[...] + swap_halves(query) * sin_ref[...]).astype(BF16)
        rotated_ref[:, cols] = query
        scores = jnp.where(allowed, mm_nt(keys_s[at], query), NEG)
        tops = [jnp.max(scores[i * rows : (i + 1) * rows], axis=0, keepdims=True) for i in range(2)]
        probs = jnp.exp(scores - spread(*tops, rows)).astype(BF16)
        for i in range(2):
            max_s[2 * pair + i : 2 * pair + i + 1, :] = tops[i]
        acc_s[pair] = mm(values_s[at], probs)

    for back in range(1, blocks):

        @pl.when(own - back >= low)
        def _():
            there = info[blocks + jnp.maximum(own - back, 0)]
            for pair in range(pairs):
                query = rotated_ref[:, pl.ds(pair * 128, 128)]
                scores = mm_nt(keys_s[there], query)
                tops, scales = [], []
                for i in range(2):
                    before = max_s[2 * pair + i : 2 * pair + i + 1, :]
                    top = jnp.maximum(
                        before, jnp.max(scores[i * rows : (i + 1) * rows], axis=0, keepdims=True)
                    )
                    tops.append(top)
                    scales.append(jnp.exp(before - top))
                    max_s[2 * pair + i : 2 * pair + i + 1, :] = top
                probs = jnp.exp(scores - spread(*tops, rows)).astype(BF16)
                factor = spread(*scales, HD)
                factor = jnp.concatenate([factor, factor], axis=0)
                acc_s[pair] = acc_s[pair] * factor + mm(values_s[there], probs)

    for pair in range(pairs):
        total = acc_s[pair][128:, :]
        result = acc_s[pair][:128, :] / total
        attended_ref[:, pl.ds(pair * 128, 128)] = jnp.transpose(result).astype(BF16)
        for i in range(2):
            spot = slice(2 * pair + i, 2 * pair + i + 1)
            lse_ref[spot, :] = max_s[spot, :] + jnp.log(total[i * HD : i * HD + 1, :])


def attention_forward(info, qkv, cosine, sine, rows, first, count):
    total, width = qkv.shape
    blocks = total // rows
    query_width = width - 2 * HD
    pairs = query_width // 128
    last = query_width // 128
    return pl.pallas_call(
        functools.partial(attention_forward_kernel, first),
        grid_spec=pltpu.PrefetchScalarGridSpec(
            num_scalar_prefetch=1,
            grid=(count,),
            in_specs=[
                pl.BlockSpec((rows, query_width), lambda j, info: (j + first, 0)),
                pl.BlockSpec((total, 128), lambda j, info: (0, last)),
                pl.BlockSpec((rows, 128), lambda j, info: (j + first, 0)),
                pl.BlockSpec((rows, 128), lambda j, info: (j + first, 0)),
                pl.BlockSpec((total, 128), lambda j, info: (0, 0)),
                pl.BlockSpec((total, 128), lambda j, info: (0, 0)),
            ],
            out_specs=[
                pl.BlockSpec((rows, query_width), lambda j, info: (j, 0)),
                pl.BlockSpec((rows, query_width), lambda j, info: (j, 0)),
                pl.BlockSpec((total, 128), lambda j, info: (0, 0)),
                pl.BlockSpec((2 * pairs, rows), lambda j, info: (0, j)),
            ],
            scratch_shapes=[
                pltpu.VMEM((blocks, 2 * rows, 128), BF16),
                pltpu.VMEM((blocks, 256, 2 * rows), BF16),
                pltpu.VMEM((pairs, 256, rows), F32),
                pltpu.VMEM((2 * pairs, rows), F32),
            ],
        ),
        cost_estimate=pl.CostEstimate(flops=count * 4 * 10**9, bytes_accessed=count * 10**6, transcendentals=0),
        out_shape=[
            jax.ShapeDtypeStruct((count * rows, query_width), BF16),
            jax.ShapeDtypeStruct((count * rows, query_width), BF16),
            jax.ShapeDtypeStruct((total, 128), BF16),
            jax.ShapeDtypeStruct((2 * pairs, count * rows), F32),
        ],
        name="attention_forward",
    )(info, qkv, qkv, cosine, sine, cosine, sine)


def attention_backward_kernel(
    first, final, info, query_ref, att_ref, grad_ref, lse_ref, kv_ref, cos_ref, sin_ref, cos_all, sin_all, *refs
):
    if first:
        refs = refs[1:]
        key_in, value_in = refs[:2]
        refs = refs[2:]
    else:
        key_in = value_in = None
    out_ref, key_acc, value_acc = refs[:3]
    refs = refs[3:]
    if final:
        kv_out = refs[0]
        refs = refs[1:]
    keys_s, values_s, query_acc, delta_s = refs
    step = pl.program_id(0) + first
    rows = query_ref.shape[0]
    query_width = query_ref.shape[1]
    pairs = query_width // 128
    blocks = kv_ref.shape[0] // rows

    @pl.when(step == first)
    def _():
        for part in range(blocks):
            kv = kv_ref[pl.ds(part * rows, rows), :].astype(F32)
            keys_s[part] = (padded_keys(kv) * (1.0 / math.sqrt(HD))).astype(BF16)
            values_s[part] = padded_values(kv).astype(BF16)
        if first:
            key_acc[...] = key_in[...]
            value_acc[...] = value_in[...]
        else:
            key_acc[...] = jnp.zeros_like(key_acc)
            value_acc[...] = jnp.zeros_like(value_acc)

    own = info[step]
    low = info[2 * blocks + step]
    at = info[blocks + own]
    key_index = lax.broadcasted_iota(jnp.int32, (2 * rows, rows), 0) % rows
    query_index = lax.broadcasted_iota(jnp.int32, (2 * rows, rows), 1)
    allowed = key_index <= query_index
    top_half = lax.broadcasted_iota(jnp.int32, (2 * rows, rows), 0) < rows

    products = att_ref[...].astype(F32) * grad_ref[...].astype(F32)
    head_row = lax.broadcasted_iota(jnp.int32, (2 * pairs, query_width), 0)
    head_col = lax.broadcasted_iota(jnp.int32, (2 * pairs, query_width), 1) // HD
    picker = jnp.where(head_row == head_col, 1.0, 0.0)
    delta_s[...] = lax.dot_general(
        picker, products, (((1,), (1,)), ((), ())),
        precision=lax.Precision.HIGHEST, preferred_element_type=F32,
    )

    def one_block(where_, masked):
        keys = keys_s[where_]
        values = values_s[where_]
        for pair in range(pairs):
            cols = pl.ds(pair * 128, 128)
            query = query_ref[:, cols]
            grad = grad_ref[:, cols]
            lse = jnp.where(
                top_half, lse_ref[2 * pair : 2 * pair + 1, :], lse_ref[2 * pair + 1 : 2 * pair + 2, :]
            )
            delta = jnp.where(
                top_half, delta_s[2 * pair : 2 * pair + 1, :], delta_s[2 * pair + 1 : 2 * pair + 2, :]
            )
            scores = mm_nt(keys, query) - lse
            if masked:
                scores = jnp.where(allowed, scores, NEG)
            probs = jnp.exp(scores)
            grad_probs = mm_nt(values, grad)
            grad_scores = (probs * (grad_probs - delta)).astype(BF16)
            value_acc[where_] += mm(probs.astype(BF16), grad)
            key_acc[where_] += mm(grad_scores, query)
            part = mm_tn(grad_scores, keys)
            if masked:
                query_acc[:, cols] = part
            else:
                query_acc[:, cols] += part

    one_block(at, True)
    for back in range(1, blocks):

        @pl.when(own - back >= low)
        def _():
            one_block(info[blocks + jnp.maximum(own - back, 0)], False)

    for pair in range(pairs):
        cols = pl.ds(pair * 128, 128)
        grad = query_acc[:, cols].astype(BF16).astype(F32)
        out_ref[:, cols] = (grad * cos_ref[...] - swap_halves(grad) * sin_ref[...]).astype(BF16)

    if final:

        @pl.when(step == first + pl.num_programs(0) - 1)
        def _():
            lane = lax.broadcasted_iota(jnp.int32, (rows, 128), 1)
            for part in range(blocks):
                spot = pl.ds(part * rows, rows)
                key_grad = key_acc[part]
                key_grad = key_grad[:rows] + pltpu.roll(key_grad[rows:], HD, 1)
                key_grad = (key_grad * (1.0 / math.sqrt(HD))).astype(BF16).astype(F32)
                value_grad = value_acc[part]
                value_grad = pltpu.roll(value_grad[:rows], HD, 1) + value_grad[rows:]
                turned = key_grad * cos_all[spot, :] - swap_halves(key_grad) * sin_all[spot, :]
                kv_out[spot, :] = jnp.where(lane < HD, turned, value_grad).astype(BF16)


def attention_backward(info, query, attended, grad, lse, kv, cosine, sine, rows, first, count, carried):
    total, query_width = query.shape
    blocks = total // rows
    pairs = query_width // 128
    final = first + count == blocks
    row_block = pl.BlockSpec((rows, query_width), lambda j, info: (j + first, 0))
    table_block = pl.BlockSpec((rows, 128), lambda j, info: (j + first, 0))
    whole = pl.BlockSpec((total, 128), lambda j, info: (0, 0))
    sums = pl.BlockSpec((blocks, 2 * rows, 128), lambda j, info: (0, 0, 0))
    sums_shape = jax.ShapeDtypeStruct((blocks, 2 * rows, 128), F32)
    in_specs = [
        row_block, row_block,
        pl.BlockSpec((rows, query_width), lambda j, info: (j, 0)),
        pl.BlockSpec((2 * pairs, rows), lambda j, info: (0, j + first)),
        whole, table_block, table_block, whole, whole,
    ]
    operands = [info, query, attended, grad, lse, kv, cosine, sine, cosine, sine]
    aliases = {}
    if first:
        aliases = {len(operands): 0, len(operands) + 1: 1, len(operands) + 2: 2}
        operands += carried
        in_specs += [pl.BlockSpec(memory_space=pl.ANY), sums, sums]
    out_specs = [row_block, sums, sums]
    out_shape = [jax.ShapeDtypeStruct((total, query_width + 128), BF16), sums_shape, sums_shape]
    if final:
        out_specs.append(whole)
        out_shape.append(jax.ShapeDtypeStruct((total, 128), BF16))
    return pl.pallas_call(
        functools.partial(attention_backward_kernel, first, final),
        grid_spec=pltpu.PrefetchScalarGridSpec(
            num_scalar_prefetch=1,
            grid=(count,),
            in_specs=in_specs,
            out_specs=out_specs,
            scratch_shapes=[
                pltpu.VMEM((blocks, 2 * rows, 128), BF16),
                pltpu.VMEM((blocks, 2 * rows, 128), BF16),
                pltpu.VMEM((rows, query_width), F32),
                pltpu.VMEM((2 * pairs, rows), F32),
            ],
        ),
        out_shape=out_shape,
        input_output_aliases=aliases,
        cost_estimate=pl.CostEstimate(flops=count * 6 * 10**9, bytes_accessed=count * 10**6, transcendentals=0),
        name="attention_backward",
    )(*operands)


def feed_forward_kernel(values_ref, grad_ref, gate_w, up_w, *refs):
    rows_out, mixed_ref, gate_ref, up_ref, back_ref = refs[-5:]
    width = values_ref.shape[1]
    hidden = gate_w.shape[1]
    rows_out[...] = values_ref[...]

    def columns(first, size):
        cols = pl.ds(first, size)
        values = values_ref[...]
        gate = mm(values, gate_w[:, cols])
        upward = mm(values, up_w[:, cols])
        grad = grad_ref[:, cols]
        sigma = 1.0 / (1.0 + jnp.exp(-gate))
        activated = gate * sigma
        mixed_ref[:, cols] = (activated * upward).astype(BF16)
        gate_ref[:, cols] = (grad * upward * sigma * (1.0 + gate * (1.0 - sigma))).astype(BF16)
        up_ref[:, cols] = (grad * activated).astype(BF16)

    step = min(256, hidden)

    @pl.loop(0, hidden // step)
    def _(index):
        columns(pl.multiple_of(index * step, step), step)

    if hidden % step:
        columns(hidden - hidden % step, hidden % step)

    part = min(256, width)

    @pl.loop(0, width // part)
    def _(index):
        here = pl.ds(pl.multiple_of(index * part, part), part)
        back_ref[:, here] = (
            mm_nt(gate_ref[...], gate_w[here, :]) + mm_nt(up_ref[...], up_w[here, :])
        ).astype(BF16)


def feed_forward(values, grad_mixed, gate_weight, up_weight, block, blocks, carried):
    rows, width = values.shape
    hidden = gate_weight.shape[1]
    here = pl.BlockSpec((rows, hidden), lambda i: (block, 0))
    resident = pl.BlockSpec(memory_space=pltpu.VMEM)
    operands = [values, grad_mixed, gate_weight, up_weight, *carried]
    whole = jax.ShapeDtypeStruct((blocks * rows, hidden), BF16)
    return pl.pallas_call(
        feed_forward_kernel,
        grid=(1,),
        in_specs=[
            pl.BlockSpec((rows, width), lambda i: (0, 0)), here, resident, resident,
            *[pl.BlockSpec(memory_space=pl.ANY)] * len(carried),
        ],
        out_specs=[
            pl.BlockSpec((rows, width), lambda i: (block, 0)), here, here, here,
            pl.BlockSpec((rows, width), lambda i: (0, 0)),
        ],
        out_shape=[
            jax.ShapeDtypeStruct((blocks * rows, width), BF16), whole, whole, whole,
            jax.ShapeDtypeStruct((rows, width), BF16),
        ],
        input_output_aliases={4 + i: i for i in range(len(carried))},
        cost_estimate=pl.CostEstimate(flops=6 * 10**9, bytes_accessed=10**6, transcendentals=0),
        name="feed_forward",
    )(*operands)


def norm_scale(values):
    return lax.rsqrt(jnp.mean(values * values, axis=-1, keepdims=True) + EPS)


def norm_backward(values, scale, gain, grads):
    weighted = grads * gain
    gain_grad = jnp.sum(grads * values * scale, axis=0)
    cubed = scale * scale * scale
    value_grad = scale * weighted - values * cubed * jnp.mean(weighted * values, axis=-1, keepdims=True)
    return gain_grad, value_grad


def over_batch(term):
    return lax.psum_scatter(term, "batch", scatter_dimension=0, tiled=True).astype(F32)


def pick(parts, index, axis):
    return lax.dynamic_index_in_dim(parts, index, axis, keepdims=False)


def line_sum(term):
    batch_parts = lax.axis_size("batch")
    line = batch_parts // 2
    index = lax.axis_index("batch")
    core, place = index % 2, index // 2
    parts = term.reshape(line, 2, term.shape[0] // batch_parts, term.shape[1])
    swap = [(i, i ^ 1) for i in range(batch_parts)]
    arrived = lax.ppermute(pick(parts, 1 - core, 1), "batch", swap)
    parts = (pick(parts, core, 1).astype(F32) + arrived.astype(F32)).astype(BF16)
    up = down = None
    for step in range(1, line):
        rising = pick(parts, jnp.minimum(place + line - step, line - 1), 0)
        falling = pick(parts, jnp.maximum(place - line + step, 0), 0)
        if up is not None:
            rising = (rising.astype(F32) + up.astype(F32)).astype(BF16)
            falling = (falling.astype(F32) + down.astype(F32)).astype(BF16)
        up = lax.ppermute(rising, "batch", [(i, i + 2) for i in range(2 * step)])
        down = lax.ppermute(
            falling, "batch", [(i, i - 2) for i in range(batch_parts - 2 * step, batch_parts)]
        )
    total = pick(parts, place, 0).astype(F32)
    if up is not None:
        total = total + up.astype(F32) + down.astype(F32)
    return total


def shards(
    tokens, seq_count, query_weight, key_weight, value_weight, out_weight,
    gate_weight, up_weight, down_weight, attention_gain, feedforward_gain, cotangent,
):
    seq_parts = lax.axis_size("seq")
    batch_parts = lax.axis_size("batch")
    part = lax.axis_index("seq")
    parity = lax.axis_index("batch") % 2
    rows = tokens.shape[1]
    group_rows = rows * seq_parts
    width = tokens.shape[2]

    order = jnp.arange(seq_parts, dtype=jnp.int32)
    swapped = ((order & 1) << 1) | (order >> 1)
    masks = jnp.where(parity == 0, order, swapped)
    owners = part ^ masks
    other = part ^ order
    spots = jnp.where(parity == 0, other, ((other & 1) << 1) | (other >> 1))
    seq_length = group_rows // seq_count[0]
    firsts = (owners * rows) // seq_length * seq_length // rows
    info = jnp.concatenate([owners, spots, firsts]).astype(jnp.int32)

    index = (owners[:, None] * rows + jnp.arange(rows, dtype=jnp.int32)[None, :]).reshape(-1)
    places = index - index // seq_length * seq_length
    lane = jnp.arange(128, dtype=jnp.int32)
    inverse = jnp.exp((lane % (HD // 2)).astype(F32) * (-2.0 * math.log(10000.0) / HD))
    angles = places.astype(F32)[:, None] * inverse[None, :]
    cosine = jnp.cos(angles)
    sine = jnp.sin(angles) * jnp.where(lane % HD < HD // 2, -1.0, 1.0)[None, :]

    inputs = tokens[0].astype(F32)
    scale_one = norm_scale(inputs)
    normed_one = (inputs * scale_one * attention_gain).astype(BF16)
    qkv_weight = jnp.concatenate([query_weight, key_weight, value_weight], axis=1)
    half = group_rows // 2

    near = first_swap(normed_one)
    side = second_swap(normed_one)
    qkv_own = mm(normed_one, qkv_weight)
    far = second_swap(after(near, qkv_own))
    normed_one_blocks = [normed_one, near, side, far]
    qkv = jnp.concatenate([qkv_own, *(mm(block, qkv_weight) for block in normed_one_blocks[1:])], axis=0)

    grad_ffn = after(cotangent[0], far)
    grad_near = first_swap(grad_ffn)
    grad_side = second_swap(grad_ffn)

    att_upper, query_upper, kv, lse_upper = attention_forward(info, qkv, cosine, sine, rows, seq_parts // 2, seq_parts // 2)
    branch_upper = mm(att_upper, out_weight).astype(BF16)
    arrived = second_swap(branch_upper)
    later_qkv, grad_near, grad_side = lax.optimization_barrier((after(qkv, branch_upper), grad_near, grad_side))
    grad_far = second_swap(grad_near)
    att_lower, query_lower, _, lse_lower = attention_forward(info, later_qkv, cosine, sine, rows, 0, seq_parts // 2)
    branch_lower = mm(att_lower, out_weight).astype(BF16)
    attended = jnp.concatenate([att_lower, att_upper], axis=0)
    query = jnp.concatenate([query_lower, query_upper], axis=0)
    lse = jnp.concatenate([lse_lower, lse_upper], axis=1)
    branch, passed = split_sum(branch_lower, after(arrived, branch_lower))
    passed = first_swap(after(passed, grad_far))
    grad_rows = jnp.concatenate([cotangent[0], grad_near, grad_side, grad_far], axis=0)
    grad_mixed = mm_nt(grad_rows, down_weight)
    hidden = inputs + branch + after(passed, grad_mixed).astype(F32)

    scale_two = norm_scale(hidden)
    normed_two = (hidden * scale_two * feedforward_gain).astype(BF16)
    near = first_swap(normed_two)
    side = second_swap(normed_two)
    *carried, back_own = feed_forward(normed_two, grad_mixed, gate_weight, up_weight, 0, seq_parts, [])
    near, side, *carried = lax.optimization_barrier((near, side, *carried))
    far = second_swap(near)
    *carried, back_near = feed_forward(near, grad_mixed, gate_weight, up_weight, 1, seq_parts, carried)
    *carried, back_side = feed_forward(side, grad_mixed, gate_weight, up_weight, 2, seq_parts, carried)
    sum_side = second_swap(back_side)
    *carried, back_far = feed_forward(far, grad_mixed, gate_weight, up_weight, 3, seq_parts, carried)
    normed_two_rows, mixed, grad_gate, grad_upward = carried
    sum_far = second_swap(back_far)
    down_term = mm_tn(mixed, after(grad_rows, back_far)).astype(BF16)
    passed = (back_near.astype(F32) + after(sum_far, down_term).astype(F32)).astype(BF16)
    passed = first_swap(passed)
    gate_term = mm_tn(normed_two_rows, after(grad_gate, down_term)).astype(BF16)
    grad_normed_two = back_own.astype(F32) + sum_side.astype(F32) + after(passed, gate_term).astype(F32)
    down_grad = over_batch(down_term)
    gate_grad = over_batch(gate_term)

    grad_out = cotangent[0].astype(F32)
    feed_gain_term, grad_hidden_norm = norm_backward(hidden, scale_two, feedforward_gain, grad_normed_two)
    grad_hidden = grad_out + grad_hidden_norm
    grad_branch = grad_hidden.astype(BF16)
    near = first_swap(grad_branch)
    side = second_swap(grad_branch)
    up_term = mm_tn(normed_two_rows, after(grad_upward, gate_term)).astype(BF16)
    up_grad = over_batch(up_term)

    def attended_grad(block):
        return mm_nt(block, out_weight).astype(BF16)

    def backward(grad, first, count, carried):
        return attention_backward(
            info, query, attended, grad, lse, kv, cosine, sine, rows, first, count, carried
        )

    ffn_upper = mm(after(mixed, up_term)[half:], down_weight).astype(BF16)
    carried = backward(after(attended_grad(grad_branch), ffn_upper), 0, 1, [])
    near, side, *carried = lax.optimization_barrier((near, side, *carried))
    far = second_swap(near)
    middle = attended_grad(jnp.concatenate([near, side], axis=0))
    carried = backward(middle, 1, 2, carried)
    far = after(far, *carried)
    ffn_arrived = second_swap(after(ffn_upper, far))
    grad_qkv, _, _, grad_kv = backward(attended_grad(far), 3, 1, carried)
    grad_qkv = lax.dynamic_update_slice(grad_qkv, grad_kv, (0, grad_qkv.shape[1] - grad_kv.shape[1]))
    upper = mm_nt(grad_qkv[half:], qkv_weight).astype(BF16)
    arrived = second_swap(after(upper, ffn_arrived))
    lower = mm_nt(grad_qkv[:half], qkv_weight).astype(BF16)
    grad_branch_rows = jnp.concatenate([grad_branch, near, side, far], axis=0)
    out_term = mm_tn(attended, after(grad_branch_rows, upper)).astype(BF16)
    normed_one_rows = jnp.concatenate(normed_one_blocks, axis=0)
    qkv_term = mm_tn(normed_one_rows, after(grad_qkv, upper)).astype(BF16)
    out_grad = line_sum(out_term)
    qkv_grad = line_sum(qkv_term)
    kept, passed = split_sum(lower, after(arrived, qkv_term, lower))
    passed = first_swap(passed)
    ffn_lower = mm(after(mixed, upper)[:half], down_weight).astype(BF16)
    ffn_kept, ffn_passed = split_sum(ffn_lower, ffn_arrived)
    ffn_passed = first_swap(ffn_passed)
    grad_normed_one = kept + passed.astype(F32)
    attention_gain_term, grad_inputs_norm = norm_backward(inputs, scale_one, attention_gain, grad_normed_one)
    input_grad = grad_hidden + grad_inputs_norm
    layer_out = (hidden + ffn_kept + ffn_passed.astype(F32)).astype(BF16)

    devices = seq_parts * batch_parts
    gains = jnp.concatenate(
        [attention_gain_term.reshape(devices, -1), feed_gain_term.reshape(devices, -1)], axis=1
    )
    gains = jnp.sum(lax.all_to_all(gains, ("seq", "batch"), 0, 0, tiled=True), axis=0)
    share = width // devices
    query_width = query_weight.shape[1]
    key_width = key_weight.shape[1]
    return (
        layer_out[None],
        input_grad[None],
        qkv_grad[:, :query_width],
        qkv_grad[:, query_width : query_width + key_width],
        qkv_grad[:, query_width + key_width :],
        out_grad,
        gate_grad,
        up_grad,
        down_grad,
        gains[:share],
        gains[share:],
    )


def solution(mesh):
    return jax.shard_map(
        shards,
        mesh=mesh,
        in_specs=(
            P("batch", "seq", None),
            P("batch"),
            P(None, "seq"),
            P(None, "seq"),
            P(None, "seq"),
            P("seq", None),
            P(None, "seq"),
            P(None, "seq"),
            P("seq", None),
            P(),
            P(),
            P("batch", "seq", None),
        ),
        out_specs=(
            P("batch", "seq", None),
            P("batch", "seq", None),
            P("batch", "seq"),
            P("batch", "seq"),
            P("batch", "seq"),
            P(("seq", "batch"), None),
            P("batch", "seq"),
            P("batch", "seq"),
            P(("seq", "batch"), None),
            P(("seq", "batch")),
            P(("seq", "batch")),
        ),
        check_vma=False,
    )
```

```python
import functools
import math

import jax
import jax.numpy as jnp
from jax import lax
from jax.experimental import pallas as pl
from jax.experimental.pallas import tpu as pltpu
from jax.sharding import PartitionSpec as P

HD = 64
EPS = 1e-05
NEG = -1e30
F32 = jnp.float32
BF16 = jnp.bfloat16


def mm(a, b):
    return lax.dot_general(a, b, (((1,), (0,)), ((), ())), preferred_element_type=F32)


def mm_nt(a, b):
    return lax.dot_general(a, b, (((1,), (1,)), ((), ())), preferred_element_type=F32)


def mm_tn(a, b):
    return lax.dot_general(a, b, (((0,), (0,)), ((), ())), preferred_element_type=F32)


def exchange(values, even_mask, odd_mask):
    seq_parts = lax.axis_size("seq")
    batch_parts = lax.axis_size("batch")
    pairs = []
    for part in range(seq_parts):
        for group in range(batch_parts):
            mask = even_mask if group % 2 == 0 else odd_mask
            pairs.append((part * batch_parts + group, (part ^ mask) * batch_parts + group))
    return lax.ppermute(values, ("seq", "batch"), pairs)


def after(value, *others):
    return lax.optimization_barrier((value, *others))[0]


def first_swap(values):
    return exchange(values, 1, 2)


def second_swap(values):
    return exchange(values, 2, 1)


def split_sum(lower, arrived):
    rows = lower.shape[0] // 2
    total = lower.astype(F32) + arrived.astype(F32)
    return total[:rows], total[rows:].astype(BF16)


def swap_halves(values):
    lane = lax.broadcasted_iota(jnp.int32, values.shape, 1)
    ahead = pltpu.roll(values, values.shape[1] - HD // 2, 1)
    behind = pltpu.roll(values, HD // 2, 1)
    return jnp.where(lane % HD < HD // 2, ahead, behind)


def padded_keys(keys_values):
    lane = lax.broadcasted_iota(jnp.int32, keys_values.shape, 1)
    zero = jnp.zeros_like(keys_values)
    left = jnp.where(lane < HD, keys_values, zero)
    right = pltpu.roll(left, HD, 1)
    return jnp.concatenate([left, right], axis=0)


def padded_values(keys_values):
    lane = lax.broadcasted_iota(jnp.int32, keys_values.shape, 1)
    zero = jnp.zeros_like(keys_values)
    right = jnp.where(lane >= HD, keys_values, zero)
    left = pltpu.roll(right, HD, 1)
    return jnp.concatenate([left, right], axis=0)


def attention_forward_kernel(
    first, info, query_ref, kv_ref, cos_ref, sin_ref, cos_all, sin_all,
    attended_ref, rotated_ref, kv_out, lse_ref, keys_s, values_s, acc_s, max_s,
):
    step = pl.program_id(0) + first
    rows = query_ref.shape[0]
    pairs = query_ref.shape[1] // 128
    blocks = kv_ref.shape[0] // rows

    @pl.when(step == first)
    def _():
        for part in range(blocks):
            here = pl.ds(part * rows, rows)
            kv = kv_ref[here, :]
            lane = lax.broadcasted_iota(jnp.int32, kv.shape, 1)
            turned = kv * cos_all[here, :] + swap_halves(kv) * sin_all[here, :]
            kv = jnp.where(lane < HD, turned, kv).astype(BF16).astype(F32)
            kv_out[here, :] = kv.astype(BF16)
            keys_s[part] = (padded_keys(kv) * (1.0 / math.sqrt(HD))).astype(BF16)
            both = jnp.transpose(padded_values(kv))
            feature = lax.broadcasted_iota(jnp.int32, both.shape, 0)
            key = lax.broadcasted_iota(jnp.int32, both.shape, 1)
            ones = jnp.where((feature < HD) == (key < rows), 1.0, 0.0)
            values_s[part] = jnp.concatenate([both, ones], axis=0).astype(BF16)

    own = info[step]
    low = info[2 * blocks + step]
    key_index = lax.broadcasted_iota(jnp.int32, (2 * rows, rows), 0) % rows
    query_index = lax.broadcasted_iota(jnp.int32, (2 * rows, rows), 1)
    allowed = key_index <= query_index
    at = info[blocks + own]

    def spread(upper, lower, height):
        return jnp.concatenate(
            [jnp.broadcast_to(upper, (height, rows)), jnp.broadcast_to(lower, (height, rows))], axis=0
        )

    for pair in range(pairs):
        cols = pl.ds(pair * 128, 128)
        query = query_ref[:, cols]
        query = (query * cos_ref[...] + swap_halves(query) * sin_ref[...]).astype(BF16)
        rotated_ref[:, cols] = query
        scores = jnp.where(allowed, mm_nt(keys_s[at], query), NEG)
        tops = [jnp.max(scores[i * rows : (i + 1) * rows], axis=0, keepdims=True) for i in range(2)]
        probs = jnp.exp(scores - spread(*tops, rows)).astype(BF16)
        for i in range(2):
            max_s[2 * pair + i : 2 * pair + i + 1, :] = tops[i]
        acc_s[pair] = mm(values_s[at], probs)

    for back in range(1, blocks):

        @pl.when(own - back >= low)
        def _():
            there = info[blocks + jnp.maximum(own - back, 0)]
            for pair in range(pairs):
                query = rotated_ref[:, pl.ds(pair * 128, 128)]
                scores = mm_nt(keys_s[there], query)
                tops, scales = [], []
                for i in range(2):
                    before = max_s[2 * pair + i : 2 * pair + i + 1, :]
                    top = jnp.maximum(
                        before, jnp.max(scores[i * rows : (i + 1) * rows], axis=0, keepdims=True)
                    )
                    tops.append(top)
                    scales.append(jnp.exp(before - top))
                    max_s[2 * pair + i : 2 * pair + i + 1, :] = top
                probs = jnp.exp(scores - spread(*tops, rows)).astype(BF16)
                factor = spread(*scales, HD)
                factor = jnp.concatenate([factor, factor], axis=0)
                acc_s[pair] = acc_s[pair] * factor + mm(values_s[there], probs)

    for pair in range(pairs):
        total = acc_s[pair][128:, :]
        result = acc_s[pair][:128, :] / total
        attended_ref[:, pl.ds(pair * 128, 128)] = jnp.transpose(result).astype(BF16)
        for i in range(2):
            spot = slice(2 * pair + i, 2 * pair + i + 1)
            lse_ref[spot, :] = max_s[spot, :] + jnp.log(total[i * HD : i * HD + 1, :])


def attention_forward(info, qkv, cosine, sine, rows, first, count):
    total, width = qkv.shape
    blocks = total // rows
    query_width = width - 2 * HD
    pairs = query_width // 128
    last = query_width // 128
    return pl.pallas_call(
        functools.partial(attention_forward_kernel, first),
        grid_spec=pltpu.PrefetchScalarGridSpec(
            num_scalar_prefetch=1,
            grid=(count,),
            in_specs=[
                pl.BlockSpec((rows, query_width), lambda j, info: (j + first, 0)),
                pl.BlockSpec((total, 128), lambda j, info: (0, last)),
                pl.BlockSpec((rows, 128), lambda j, info: (j + first, 0)),
                pl.BlockSpec((rows, 128), lambda j, info: (j + first, 0)),
                pl.BlockSpec((total, 128), lambda j, info: (0, 0)),
                pl.BlockSpec((total, 128), lambda j, info: (0, 0)),
            ],
            out_specs=[
                pl.BlockSpec((rows, query_width), lambda j, info: (j, 0)),
                pl.BlockSpec((rows, query_width), lambda j, info: (j, 0)),
                pl.BlockSpec((total, 128), lambda j, info: (0, 0)),
                pl.BlockSpec((2 * pairs, rows), lambda j, info: (0, j)),
            ],
            scratch_shapes=[
                pltpu.VMEM((blocks, 2 * rows, 128), BF16),
                pltpu.VMEM((blocks, 256, 2 * rows), BF16),
                pltpu.VMEM((pairs, 256, rows), F32),
                pltpu.VMEM((2 * pairs, rows), F32),
            ],
        ),
        cost_estimate=pl.CostEstimate(flops=count * 4 * 10**9, bytes_accessed=count * 10**6, transcendentals=0),
        out_shape=[
            jax.ShapeDtypeStruct((count * rows, query_width), BF16),
            jax.ShapeDtypeStruct((count * rows, query_width), BF16),
            jax.ShapeDtypeStruct((total, 128), BF16),
            jax.ShapeDtypeStruct((2 * pairs, count * rows), F32),
        ],
        name="attention_forward",
    )(info, qkv, qkv, cosine, sine, cosine, sine)


def attention_backward_kernel(
    first, final, info, query_ref, att_ref, grad_ref, lse_ref, kv_ref, cos_ref, sin_ref, cos_all, sin_all, *refs
):
    if first:
        refs = refs[1:]
        key_in, value_in = refs[:2]
        refs = refs[2:]
    else:
        key_in = value_in = None
    out_ref, key_acc, value_acc = refs[:3]
    refs = refs[3:]
    if final:
        kv_out = refs[0]
        refs = refs[1:]
    keys_s, values_s, query_acc, delta_s = refs
    step = pl.program_id(0) + first
    rows = query_ref.shape[0]
    query_width = query_ref.shape[1]
    pairs = query_width // 128
    blocks = kv_ref.shape[0] // rows

    @pl.when(step == first)
    def _():
        for part in range(blocks):
            kv = kv_ref[pl.ds(part * rows, rows), :].astype(F32)
            keys_s[part] = (padded_keys(kv) * (1.0 / math.sqrt(HD))).astype(BF16)
            values_s[part] = padded_values(kv).astype(BF16)
        if first:
            key_acc[...] = key_in[...]
            value_acc[...] = value_in[...]
        else:
            key_acc[...] = jnp.zeros_like(key_acc)
            value_acc[...] = jnp.zeros_like(value_acc)

    own = info[step]
    low = info[2 * blocks + step]
    at = info[blocks + own]
    key_index = lax.broadcasted_iota(jnp.int32, (2 * rows, rows), 0) % rows
    query_index = lax.broadcasted_iota(jnp.int32, (2 * rows, rows), 1)
    allowed = key_index <= query_index
    top_half = lax.broadcasted_iota(jnp.int32, (2 * rows, rows), 0) < rows

    products = att_ref[...].astype(F32) * grad_ref[...].astype(F32)
    head_row = lax.broadcasted_iota(jnp.int32, (2 * pairs, query_width), 0)
    head_col = lax.broadcasted_iota(jnp.int32, (2 * pairs, query_width), 1) // HD
    picker = jnp.where(head_row == head_col, 1.0, 0.0)
    delta_s[...] = lax.dot_general(
        picker, products, (((1,), (1,)), ((), ())),
        precision=lax.Precision.HIGHEST, preferred_element_type=F32,
    )

    def one_block(where_, masked):
        keys = keys_s[where_]
        values = values_s[where_]
        for pair in range(pairs):
            cols = pl.ds(pair * 128, 128)
            query = query_ref[:, cols]
            grad = grad_ref[:, cols]
            lse = jnp.where(
                top_half, lse_ref[2 * pair : 2 * pair + 1, :], lse_ref[2 * pair + 1 : 2 * pair + 2, :]
            )
            delta = jnp.where(
                top_half, delta_s[2 * pair : 2 * pair + 1, :], delta_s[2 * pair + 1 : 2 * pair + 2, :]
            )
            scores = mm_nt(keys, query) - lse
            if masked:
                scores = jnp.where(allowed, scores, NEG)
            probs = jnp.exp(scores)
            grad_probs = mm_nt(values, grad)
            grad_scores = (probs * (grad_probs - delta)).astype(BF16)
            value_acc[where_] += mm(probs.astype(BF16), grad)
            key_acc[where_] += mm(grad_scores, query)
            part = mm_tn(grad_scores, keys)
            if masked:
                query_acc[:, cols] = part
            else:
                query_acc[:, cols] += part

    one_block(at, True)
    for back in range(1, blocks):

        @pl.when(own - back >= low)
        def _():
            one_block(info[blocks + jnp.maximum(own - back, 0)], False)

    for pair in range(pairs):
        cols = pl.ds(pair * 128, 128)
        grad = query_acc[:, cols].astype(BF16).astype(F32)
        out_ref[:, cols] = (grad * cos_ref[...] - swap_halves(grad) * sin_ref[...]).astype(BF16)

    if final:

        @pl.when(step == first + pl.num_programs(0) - 1)
        def _():
            lane = lax.broadcasted_iota(jnp.int32, (rows, 128), 1)
            for part in range(blocks):
                spot = pl.ds(part * rows, rows)
                key_grad = key_acc[part]
                key_grad = key_grad[:rows] + pltpu.roll(key_grad[rows:], HD, 1)
                key_grad = (key_grad * (1.0 / math.sqrt(HD))).astype(BF16).astype(F32)
                value_grad = value_acc[part]
                value_grad = pltpu.roll(value_grad[:rows], HD, 1) + value_grad[rows:]
                turned = key_grad * cos_all[spot, :] - swap_halves(key_grad) * sin_all[spot, :]
                kv_out[spot, :] = jnp.where(lane < HD, turned, value_grad).astype(BF16)


def attention_backward(info, query, attended, grad, lse, kv, cosine, sine, rows, first, count, carried):
    total, query_width = query.shape
    blocks = total // rows
    pairs = query_width // 128
    final = first + count == blocks
    row_block = pl.BlockSpec((rows, query_width), lambda j, info: (j + first, 0))
    table_block = pl.BlockSpec((rows, 128), lambda j, info: (j + first, 0))
    whole = pl.BlockSpec((total, 128), lambda j, info: (0, 0))
    sums = pl.BlockSpec((blocks, 2 * rows, 128), lambda j, info: (0, 0, 0))
    sums_shape = jax.ShapeDtypeStruct((blocks, 2 * rows, 128), F32)
    in_specs = [
        row_block, row_block,
        pl.BlockSpec((rows, query_width), lambda j, info: (j, 0)),
        pl.BlockSpec((2 * pairs, rows), lambda j, info: (0, j + first)),
        whole, table_block, table_block, whole, whole,
    ]
    operands = [info, query, attended, grad, lse, kv, cosine, sine, cosine, sine]
    aliases = {}
    if first:
        aliases = {len(operands): 0, len(operands) + 1: 1, len(operands) + 2: 2}
        operands += carried
        in_specs += [pl.BlockSpec(memory_space=pl.ANY), sums, sums]
    out_specs = [row_block, sums, sums]
    out_shape = [jax.ShapeDtypeStruct((total, query_width + 128), BF16), sums_shape, sums_shape]
    if final:
        out_specs.append(whole)
        out_shape.append(jax.ShapeDtypeStruct((total, 128), BF16))
    return pl.pallas_call(
        functools.partial(attention_backward_kernel, first, final),
        grid_spec=pltpu.PrefetchScalarGridSpec(
            num_scalar_prefetch=1,
            grid=(count,),
            in_specs=in_specs,
            out_specs=out_specs,
            scratch_shapes=[
                pltpu.VMEM((blocks, 2 * rows, 128), BF16),
                pltpu.VMEM((blocks, 2 * rows, 128), BF16),
                pltpu.VMEM((rows, query_width), F32),
                pltpu.VMEM((2 * pairs, rows), F32),
            ],
        ),
        out_shape=out_shape,
        input_output_aliases=aliases,
        cost_estimate=pl.CostEstimate(flops=count * 6 * 10**9, bytes_accessed=count * 10**6, transcendentals=0),
        name="attention_backward",
    )(*operands)


def feed_forward_kernel(parts, *refs):
    values_refs = refs[:parts]
    grad_ref, gate_w, up_w = refs[parts : parts + 3]
    rows_out, mixed_ref, slopes_ref = refs[-3 - parts : -parts]
    back_refs = refs[-parts:]
    rows, width = values_refs[0].shape
    hidden = gate_w.shape[1]
    for i in range(parts):
        rows_out[pl.ds(i * rows, rows), :] = values_refs[i][...]

    def columns(first, size):
        cols = pl.ds(first, size)
        values = rows_out[...]
        gate = mm(values, gate_w[:, cols])
        upward = mm(values, up_w[:, cols])
        grad = grad_ref[:, cols]
        sigma = 1.0 / (1.0 + jnp.exp(-gate))
        activated = gate * sigma
        mixed_ref[:, cols] = (activated * upward).astype(BF16)
        slopes_ref[:, cols] = (grad * upward * sigma * (1.0 + gate * (1.0 - sigma))).astype(BF16)
        slopes_ref[:, pl.ds(hidden + first, size)] = (grad * activated).astype(BF16)

    step = min(256, hidden)

    @pl.loop(0, hidden // step)
    def _(index):
        columns(pl.multiple_of(index * step, 128), step)

    if hidden % step:
        columns(hidden - hidden % step, hidden % step)

    part = min(256, width)

    @pl.loop(0, width // part)
    def _(index):
        here = pl.ds(pl.multiple_of(index * part, part), part)
        result = mm_nt(slopes_ref[:, :hidden], gate_w[here, :]) + mm_nt(slopes_ref[:, hidden:], up_w[here, :])
        for i in range(parts):
            back_refs[i][:, here] = result[i * rows : (i + 1) * rows].astype(BF16)


def feed_forward(values, grad_mixed, gate_weight, up_weight, first, carried):
    parts = len(values)
    rows, width = values[0].shape
    total, hidden = grad_mixed.shape
    size = parts * rows
    block = first // size
    resident = pl.BlockSpec(memory_space=pltpu.VMEM)
    operands = [*values, grad_mixed, gate_weight, up_weight, *carried]
    single = pl.BlockSpec((rows, width), lambda i: (0, 0))
    here = pl.BlockSpec((size, hidden), lambda i: (block, 0))
    return pl.pallas_call(
        functools.partial(feed_forward_kernel, parts),
        grid=(1,),
        in_specs=[
            *[single] * parts, here, resident, resident,
            *[pl.BlockSpec(memory_space=pl.ANY)] * len(carried),
        ],
        out_specs=[
            pl.BlockSpec((size, width), lambda i: (block, 0)), here,
            pl.BlockSpec((size, 2 * hidden), lambda i: (block, 0)), *[single] * parts,
        ],
        out_shape=[
            jax.ShapeDtypeStruct((total, width), BF16),
            jax.ShapeDtypeStruct((total, hidden), BF16),
            jax.ShapeDtypeStruct((total, 2 * hidden), BF16),
            *[jax.ShapeDtypeStruct((rows, width), BF16)] * parts,
        ],
        input_output_aliases={parts + 3 + i: i for i in range(len(carried))},
        cost_estimate=pl.CostEstimate(flops=parts * 6 * 10**9, bytes_accessed=10**6, transcendentals=0),
        name="feed_forward",
    )(*operands)


def weight_gradient_kernel(values_ref, grad_ref, out_ref):
    out_ref[...] = mm_tn(values_ref[...], grad_ref[...]).astype(BF16)


def weight_gradient(values, grad):
    total, features = values.shape
    outputs = grad.shape[1]
    tile = min(512, features)
    return pl.pallas_call(
        weight_gradient_kernel,
        grid=(features // tile,),
        in_specs=[
            pl.BlockSpec((total, tile), lambda i: (0, i)),
            pl.BlockSpec((total, outputs), lambda i: (0, 0)),
        ],
        out_specs=pl.BlockSpec((tile, outputs), lambda i: (i, 0)),
        out_shape=jax.ShapeDtypeStruct((features, outputs), BF16),
        cost_estimate=pl.CostEstimate(
            flops=2 * total * features * outputs, bytes_accessed=10**6, transcendentals=0
        ),
        name="weight_gradient",
    )(values, grad)


def norm_scale(values):
    return lax.rsqrt(jnp.mean(values * values, axis=-1, keepdims=True) + EPS)


def norm_backward(values, scale, gain, grads):
    weighted = grads * gain
    gain_grad = jnp.sum(grads * values * scale, axis=0)
    cubed = scale * scale * scale
    value_grad = scale * weighted - values * cubed * jnp.mean(weighted * values, axis=-1, keepdims=True)
    return gain_grad, value_grad


def over_batch(term):
    return lax.psum_scatter(term, "batch", scatter_dimension=0, tiled=True)


def pick(parts, index, axis):
    return lax.dynamic_index_in_dim(parts, index, axis, keepdims=False)


def line_sum(term):
    batch_parts = lax.axis_size("batch")
    line = batch_parts // 2
    index = lax.axis_index("batch")
    core, place = index % 2, index // 2
    parts = term.reshape(line, 2, term.shape[0] // batch_parts, term.shape[1])
    swap = [(i, i ^ 1) for i in range(batch_parts)]
    arrived = lax.ppermute(pick(parts, 1 - core, 1), "batch", swap)
    parts = (pick(parts, core, 1).astype(F32) + arrived.astype(F32)).astype(BF16)
    up = down = None
    for step in range(1, line):
        rising = pick(parts, jnp.minimum(place + line - step, line - 1), 0)
        falling = pick(parts, jnp.maximum(place - line + step, 0), 0)
        if up is not None:
            rising = (rising.astype(F32) + up.astype(F32)).astype(BF16)
            falling = (falling.astype(F32) + down.astype(F32)).astype(BF16)
        up = lax.ppermute(rising, "batch", [(i, i + 2) for i in range(2 * step)])
        down = lax.ppermute(
            falling, "batch", [(i, i - 2) for i in range(batch_parts - 2 * step, batch_parts)]
        )
    total = pick(parts, place, 0).astype(F32)
    if up is not None:
        total = total + up.astype(F32) + down.astype(F32)
    return total


def shards(
    tokens, seq_count, query_weight, key_weight, value_weight, out_weight,
    gate_weight, up_weight, down_weight, attention_gain, feedforward_gain, cotangent,
):
    seq_parts = lax.axis_size("seq")
    batch_parts = lax.axis_size("batch")
    part = lax.axis_index("seq")
    parity = lax.axis_index("batch") % 2
    rows = tokens.shape[1]
    group_rows = rows * seq_parts
    width = tokens.shape[2]

    order = jnp.arange(seq_parts, dtype=jnp.int32)
    swapped = ((order & 1) << 1) | (order >> 1)
    masks = jnp.where(parity == 0, order, swapped)
    owners = part ^ masks
    other = part ^ order
    spots = jnp.where(parity == 0, other, ((other & 1) << 1) | (other >> 1))
    seq_length = group_rows // seq_count[0]
    firsts = (owners * rows) // seq_length * seq_length // rows
    info = jnp.concatenate([owners, spots, firsts]).astype(jnp.int32)

    index = (owners[:, None] * rows + jnp.arange(rows, dtype=jnp.int32)[None, :]).reshape(-1)
    places = index - index // seq_length * seq_length
    lane = jnp.arange(128, dtype=jnp.int32)
    inverse = jnp.exp((lane % (HD // 2)).astype(F32) * (-2.0 * math.log(10000.0) / HD))
    angles = places.astype(F32)[:, None] * inverse[None, :]
    cosine = jnp.cos(angles)
    sine = jnp.sin(angles) * jnp.where(lane % HD < HD // 2, -1.0, 1.0)[None, :]

    inputs = tokens[0].astype(F32)
    scale_one = norm_scale(inputs)
    normed_one = (inputs * scale_one * attention_gain).astype(BF16)
    qkv_weight = jnp.concatenate([query_weight, key_weight, value_weight], axis=1)
    half = group_rows // 2

    near = first_swap(normed_one)
    side = second_swap(normed_one)
    qkv_own = mm(normed_one, qkv_weight)
    far = second_swap(after(near, qkv_own))
    normed_one_blocks = [normed_one, near, side, far]
    qkv = jnp.concatenate([qkv_own, *(mm(block, qkv_weight) for block in normed_one_blocks[1:])], axis=0)

    grad_ffn = after(cotangent[0], far)
    grad_near = first_swap(grad_ffn)
    grad_side = second_swap(grad_ffn)

    att_upper, query_upper, kv, lse_upper = attention_forward(info, qkv, cosine, sine, rows, seq_parts // 2, seq_parts // 2)
    branch_upper = mm(att_upper, out_weight).astype(BF16)
    arrived = second_swap(branch_upper)
    later_qkv, grad_near, grad_side = lax.optimization_barrier((after(qkv, branch_upper), grad_near, grad_side))
    grad_far = second_swap(grad_near)
    att_lower, query_lower, _, lse_lower = attention_forward(info, later_qkv, cosine, sine, rows, 0, seq_parts // 2)
    branch_lower = mm(att_lower, out_weight).astype(BF16)
    attended = jnp.concatenate([att_lower, att_upper], axis=0)
    query = jnp.concatenate([query_lower, query_upper], axis=0)
    lse = jnp.concatenate([lse_lower, lse_upper], axis=1)
    branch, passed = split_sum(branch_lower, after(arrived, branch_lower))
    passed = first_swap(after(passed, grad_far))
    grad_rows = jnp.concatenate([grad_near, grad_side, grad_far, cotangent[0]], axis=0)
    grad_mixed = mm_nt(grad_rows, down_weight)
    hidden = inputs + branch + after(passed, grad_mixed).astype(F32)

    scale_two = norm_scale(hidden)
    normed_two = (hidden * scale_two * feedforward_gain).astype(BF16)
    near = first_swap(normed_two)
    side = second_swap(normed_two)
    *carried, back_own = feed_forward([normed_two], grad_mixed, gate_weight, up_weight, 3 * rows, [])
    near, side, *carried = lax.optimization_barrier((near, side, *carried))
    far = second_swap(near)
    *carried, back_near, back_side = feed_forward([near, side], grad_mixed, gate_weight, up_weight, 0, carried)
    sum_side = second_swap(back_side)
    *carried, back_far = feed_forward([far], grad_mixed, gate_weight, up_weight, 2 * rows, carried)
    normed_two_rows, mixed, slopes = carried
    sum_far = second_swap(back_far)
    down_term = mm_tn(mixed, after(grad_rows, sum_side)).astype(BF16)
    near_sum = (back_near.astype(F32) + after(sum_far, down_term).astype(F32)).astype(BF16)
    passed = first_swap(near_sum)
    gate_up_term = weight_gradient(normed_two_rows, after(slopes, near_sum))
    grad_normed_two = back_own.astype(F32) + sum_side.astype(F32) + after(passed, gate_up_term).astype(F32)
    down_grad = over_batch(after(down_term, sum_far))
    gate_up_grad = over_batch(after(gate_up_term, passed))

    grad_out = cotangent[0].astype(F32)
    feed_gain_term, grad_hidden_norm = norm_backward(hidden, scale_two, feedforward_gain, grad_normed_two)
    grad_hidden = grad_out + grad_hidden_norm
    grad_branch = grad_hidden.astype(BF16)
    near = first_swap(grad_branch)
    side = second_swap(grad_branch)

    def attended_grad(block):
        return mm_nt(block, out_weight).astype(BF16)

    def backward(grad, first, count, carried):
        return attention_backward(
            info, query, attended, grad, lse, kv, cosine, sine, rows, first, count, carried
        )

    ffn_upper = mm(after(mixed, grad_branch)[rows : 3 * rows], down_weight).astype(BF16)
    carried = backward(after(attended_grad(grad_branch), ffn_upper), 0, 1, [])
    near, side, *carried = lax.optimization_barrier((near, side, *carried))
    far = second_swap(near)
    middle = attended_grad(jnp.concatenate([near, side], axis=0))
    carried = backward(middle, 1, 2, carried)
    far = after(far, *carried)
    ffn_arrived = second_swap(after(ffn_upper, far))
    grad_branch_rows = jnp.concatenate([grad_branch, near, side, far], axis=0)
    out_term = mm_tn(attended, grad_branch_rows).astype(BF16)
    grad_qkv, _, _, grad_kv = backward(attended_grad(after(far, out_term)), 3, 1, carried)
    grad_qkv = lax.dynamic_update_slice(grad_qkv, grad_kv, (0, grad_qkv.shape[1] - grad_kv.shape[1]))
    upper = mm_nt(after(grad_qkv, down_grad)[half:], qkv_weight).astype(BF16)
    arrived = second_swap(after(upper, ffn_arrived))
    lower = mm_nt(grad_qkv[:half], qkv_weight).astype(BF16)
    normed_one_rows = jnp.concatenate(normed_one_blocks, axis=0)
    qkv_term = mm_tn(normed_one_rows, after(grad_qkv, upper)).astype(BF16)
    out_grad = line_sum(out_term)
    qkv_grad = line_sum(qkv_term)
    kept, passed = split_sum(lower, after(arrived, qkv_term, lower))
    passed = first_swap(passed)
    later_mixed = after(mixed, upper)
    ffn_passed = mm(later_mixed[:rows], down_weight) + ffn_arrived[rows:].astype(F32)
    ffn_passed = first_swap(ffn_passed.astype(BF16))
    ffn_kept = mm(later_mixed[3 * rows :], down_weight) + ffn_arrived[:rows].astype(F32)
    grad_normed_one = kept + passed.astype(F32)
    attention_gain_term, grad_inputs_norm = norm_backward(inputs, scale_one, attention_gain, grad_normed_one)
    input_grad = grad_hidden + grad_inputs_norm
    layer_out = (hidden + ffn_kept + ffn_passed.astype(F32)).astype(BF16)

    devices = seq_parts * batch_parts
    gains = jnp.concatenate(
        [attention_gain_term.reshape(devices, -1), feed_gain_term.reshape(devices, -1)], axis=1
    )
    gains = jnp.sum(lax.all_to_all(gains, ("seq", "batch"), 0, 0, tiled=True), axis=0)
    gate_up_grad = after(gate_up_grad, gains, qkv_grad, out_grad)
    hidden_width = gate_weight.shape[1]
    share = width // devices
    query_width = query_weight.shape[1]
    key_width = key_weight.shape[1]
    return (
        layer_out[None],
        input_grad[None],
        qkv_grad[:, :query_width],
        qkv_grad[:, query_width : query_width + key_width],
        qkv_grad[:, query_width + key_width :],
        out_grad,
        gate_up_grad[:, :hidden_width].astype(F32),
        gate_up_grad[:, hidden_width:].astype(F32),
        down_grad.astype(F32),
        gains[:share],
        gains[share:],
    )


def solution(mesh):
    return jax.shard_map(
        shards,
        mesh=mesh,
        in_specs=(
            P("batch", "seq", None),
            P("batch"),
            P(None, "seq"),
            P(None, "seq"),
            P(None, "seq"),
            P("seq", None),
            P(None, "seq"),
            P(None, "seq"),
            P("seq", None),
            P(),
            P(),
            P("batch", "seq", None),
        ),
        out_specs=(
            P("batch", "seq", None),
            P("batch", "seq", None),
            P("batch", "seq"),
            P("batch", "seq"),
            P("batch", "seq"),
            P(("seq", "batch"), None),
            P("batch", "seq"),
            P("batch", "seq"),
            P(("seq", "batch"), None),
            P(("seq", "batch")),
            P(("seq", "batch")),
        ),
        check_vma=False,
    )
```

```python
import functools
import math

import jax
import jax.numpy as jnp
from jax import lax
from jax.experimental import pallas as pl
from jax.experimental.pallas import tpu as pltpu
from jax.sharding import PartitionSpec as P

HD = 64
EPS = 1e-05
NEG = -1e30
F32 = jnp.float32
BF16 = jnp.bfloat16


def mm(a, b):
    return lax.dot_general(a, b, (((1,), (0,)), ((), ())), preferred_element_type=F32)


def mm_nt(a, b):
    return lax.dot_general(a, b, (((1,), (1,)), ((), ())), preferred_element_type=F32)


def mm_tn(a, b):
    return lax.dot_general(a, b, (((0,), (0,)), ((), ())), preferred_element_type=F32)


def exchange(values, even_mask, odd_mask):
    seq_parts = lax.axis_size("seq")
    batch_parts = lax.axis_size("batch")
    pairs = []
    for part in range(seq_parts):
        for group in range(batch_parts):
            mask = even_mask if group % 2 == 0 else odd_mask
            pairs.append((part * batch_parts + group, (part ^ mask) * batch_parts + group))
    return lax.ppermute(values, ("seq", "batch"), pairs)


def after(value, *others):
    return lax.optimization_barrier((value, *others))[0]


def first_swap(values):
    return exchange(values, 1, 2)


def second_swap(values):
    return exchange(values, 2, 1)


def split_sum(lower, arrived):
    rows = lower.shape[0] // 2
    total = lower.astype(F32) + arrived.astype(F32)
    return total[:rows], total[rows:].astype(BF16)


def swap_halves(values):
    lane = lax.broadcasted_iota(jnp.int32, values.shape, 1)
    ahead = pltpu.roll(values, values.shape[1] - HD // 2, 1)
    behind = pltpu.roll(values, HD // 2, 1)
    return jnp.where(lane % HD < HD // 2, ahead, behind)


def padded_keys(keys_values):
    lane = lax.broadcasted_iota(jnp.int32, keys_values.shape, 1)
    zero = jnp.zeros_like(keys_values)
    left = jnp.where(lane < HD, keys_values, zero)
    right = pltpu.roll(left, HD, 1)
    return jnp.concatenate([left, right], axis=0)


def padded_values(keys_values):
    lane = lax.broadcasted_iota(jnp.int32, keys_values.shape, 1)
    zero = jnp.zeros_like(keys_values)
    right = jnp.where(lane >= HD, keys_values, zero)
    left = pltpu.roll(right, HD, 1)
    return jnp.concatenate([left, right], axis=0)


def attention_forward_kernel(
    first, info, query_ref, kv_ref, cos_ref, sin_ref, cos_all, sin_all,
    attended_ref, rotated_ref, kv_out, lse_ref, keys_s, values_s, acc_s, max_s,
):
    step = pl.program_id(0) + first
    rows = query_ref.shape[0]
    pairs = query_ref.shape[1] // 128
    blocks = kv_ref.shape[0] // rows

    @pl.when(step == first)
    def _():
        for part in range(blocks):
            here = pl.ds(part * rows, rows)
            kv = kv_ref[here, :]
            lane = lax.broadcasted_iota(jnp.int32, kv.shape, 1)
            turned = kv * cos_all[here, :] + swap_halves(kv) * sin_all[here, :]
            kv = jnp.where(lane < HD, turned, kv).astype(BF16).astype(F32)
            kv_out[here, :] = kv.astype(BF16)
            keys_s[part] = (padded_keys(kv) * (1.0 / math.sqrt(HD))).astype(BF16)
            both = jnp.transpose(padded_values(kv))
            feature = lax.broadcasted_iota(jnp.int32, both.shape, 0)
            key = lax.broadcasted_iota(jnp.int32, both.shape, 1)
            ones = jnp.where((feature < HD) == (key < rows), 1.0, 0.0)
            values_s[part] = jnp.concatenate([both, ones], axis=0).astype(BF16)

    own = info[step]
    low = info[2 * blocks + step]
    key_index = lax.broadcasted_iota(jnp.int32, (2 * rows, rows), 0) % rows
    query_index = lax.broadcasted_iota(jnp.int32, (2 * rows, rows), 1)
    allowed = key_index <= query_index
    at = info[blocks + own]

    def spread(upper, lower, height):
        return jnp.concatenate(
            [jnp.broadcast_to(upper, (height, rows)), jnp.broadcast_to(lower, (height, rows))], axis=0
        )

    for pair in range(pairs):
        cols = pl.ds(pair * 128, 128)
        query = query_ref[:, cols]
        query = (query * cos_ref[...] + swap_halves(query) * sin_ref[...]).astype(BF16)
        rotated_ref[:, cols] = query
        scores = jnp.where(allowed, mm_nt(keys_s[at], query), NEG)
        tops = [jnp.max(scores[i * rows : (i + 1) * rows], axis=0, keepdims=True) for i in range(2)]
        probs = jnp.exp(scores - spread(*tops, rows)).astype(BF16)
        for i in range(2):
            max_s[2 * pair + i : 2 * pair + i + 1, :] = tops[i]
        acc_s[pair] = mm(values_s[at], probs)

    for back in range(1, blocks):

        @pl.when(own - back >= low)
        def _():
            there = info[blocks + jnp.maximum(own - back, 0)]
            for pair in range(pairs):
                query = rotated_ref[:, pl.ds(pair * 128, 128)]
                scores = mm_nt(keys_s[there], query)
                tops, scales = [], []
                for i in range(2):
                    before = max_s[2 * pair + i : 2 * pair + i + 1, :]
                    top = jnp.maximum(
                        before, jnp.max(scores[i * rows : (i + 1) * rows], axis=0, keepdims=True)
                    )
                    tops.append(top)
                    scales.append(jnp.exp(before - top))
                    max_s[2 * pair + i : 2 * pair + i + 1, :] = top
                probs = jnp.exp(scores - spread(*tops, rows)).astype(BF16)
                factor = spread(*scales, HD)
                factor = jnp.concatenate([factor, factor], axis=0)
                acc_s[pair] = acc_s[pair] * factor + mm(values_s[there], probs)

    for pair in range(pairs):
        total = acc_s[pair][128:, :]
        result = acc_s[pair][:128, :] / total
        attended_ref[:, pl.ds(pair * 128, 128)] = jnp.transpose(result).astype(BF16)
        for i in range(2):
            spot = slice(2 * pair + i, 2 * pair + i + 1)
            lse_ref[spot, :] = max_s[spot, :] + jnp.log(total[i * HD : i * HD + 1, :])


def attention_forward(info, qkv, cosine, sine, rows, first, count):
    total, width = qkv.shape
    blocks = total // rows
    query_width = width - 2 * HD
    pairs = query_width // 128
    last = query_width // 128
    return pl.pallas_call(
        functools.partial(attention_forward_kernel, first),
        grid_spec=pltpu.PrefetchScalarGridSpec(
            num_scalar_prefetch=1,
            grid=(count,),
            in_specs=[
                pl.BlockSpec((rows, query_width), lambda j, info: (j + first, 0)),
                pl.BlockSpec((total, 128), lambda j, info: (0, last)),
                pl.BlockSpec((rows, 128), lambda j, info: (j + first, 0)),
                pl.BlockSpec((rows, 128), lambda j, info: (j + first, 0)),
                pl.BlockSpec((total, 128), lambda j, info: (0, 0)),
                pl.BlockSpec((total, 128), lambda j, info: (0, 0)),
            ],
            out_specs=[
                pl.BlockSpec((rows, query_width), lambda j, info: (j, 0)),
                pl.BlockSpec((rows, query_width), lambda j, info: (j, 0)),
                pl.BlockSpec((total, 128), lambda j, info: (0, 0)),
                pl.BlockSpec((2 * pairs, rows), lambda j, info: (0, j)),
            ],
            scratch_shapes=[
                pltpu.VMEM((blocks, 2 * rows, 128), BF16),
                pltpu.VMEM((blocks, 256, 2 * rows), BF16),
                pltpu.VMEM((pairs, 256, rows), F32),
                pltpu.VMEM((2 * pairs, rows), F32),
            ],
        ),
        cost_estimate=pl.CostEstimate(flops=count * 4 * 10**9, bytes_accessed=count * 10**6, transcendentals=0),
        out_shape=[
            jax.ShapeDtypeStruct((count * rows, query_width), BF16),
            jax.ShapeDtypeStruct((count * rows, query_width), BF16),
            jax.ShapeDtypeStruct((total, 128), BF16),
            jax.ShapeDtypeStruct((2 * pairs, count * rows), F32),
        ],
        name="attention_forward",
    )(info, qkv, qkv, cosine, sine, cosine, sine)


def attention_backward_kernel(
    first, final, info, query_ref, att_ref, grad_ref, lse_ref, kv_ref, cos_ref, sin_ref, cos_all, sin_all, *refs
):
    if first:
        refs = refs[1:]
        key_in, value_in = refs[:2]
        refs = refs[2:]
    else:
        key_in = value_in = None
    out_ref, key_acc, value_acc = refs[:3]
    refs = refs[3:]
    if final:
        kv_out = refs[0]
        refs = refs[1:]
    keys_s, values_s, query_acc, delta_s = refs
    step = pl.program_id(0) + first
    rows = query_ref.shape[0]
    query_width = query_ref.shape[1]
    pairs = query_width // 128
    blocks = kv_ref.shape[0] // rows

    @pl.when(step == first)
    def _():
        for part in range(blocks):
            kv = kv_ref[pl.ds(part * rows, rows), :].astype(F32)
            keys_s[part] = (padded_keys(kv) * (1.0 / math.sqrt(HD))).astype(BF16)
            values_s[part] = padded_values(kv).astype(BF16)
        if first:
            key_acc[...] = key_in[...]
            value_acc[...] = value_in[...]
        else:
            key_acc[...] = jnp.zeros_like(key_acc)
            value_acc[...] = jnp.zeros_like(value_acc)

    own = info[step]
    low = info[2 * blocks + step]
    at = info[blocks + own]
    key_index = lax.broadcasted_iota(jnp.int32, (2 * rows, rows), 0) % rows
    query_index = lax.broadcasted_iota(jnp.int32, (2 * rows, rows), 1)
    allowed = key_index <= query_index
    top_half = lax.broadcasted_iota(jnp.int32, (2 * rows, rows), 0) < rows

    products = att_ref[...].astype(F32) * grad_ref[...].astype(F32)
    head_row = lax.broadcasted_iota(jnp.int32, (2 * pairs, query_width), 0)
    head_col = lax.broadcasted_iota(jnp.int32, (2 * pairs, query_width), 1) // HD
    picker = jnp.where(head_row == head_col, 1.0, 0.0)
    delta_s[...] = lax.dot_general(
        picker, products, (((1,), (1,)), ((), ())),
        precision=lax.Precision.HIGHEST, preferred_element_type=F32,
    )

    def one_block(where_, masked):
        keys = keys_s[where_]
        values = values_s[where_]
        for pair in range(pairs):
            cols = pl.ds(pair * 128, 128)
            query = query_ref[:, cols]
            grad = grad_ref[:, cols]
            lse = jnp.where(
                top_half, lse_ref[2 * pair : 2 * pair + 1, :], lse_ref[2 * pair + 1 : 2 * pair + 2, :]
            )
            delta = jnp.where(
                top_half, delta_s[2 * pair : 2 * pair + 1, :], delta_s[2 * pair + 1 : 2 * pair + 2, :]
            )
            scores = mm_nt(keys, query) - lse
            if masked:
                scores = jnp.where(allowed, scores, NEG)
            probs = jnp.exp(scores)
            grad_probs = mm_nt(values, grad)
            grad_scores = (probs * (grad_probs - delta)).astype(BF16)
            value_acc[where_] += mm(probs.astype(BF16), grad)
            key_acc[where_] += mm(grad_scores, query)
            part = mm_tn(grad_scores, keys)
            if masked:
                query_acc[:, cols] = part
            else:
                query_acc[:, cols] += part

    one_block(at, True)
    for back in range(1, blocks):

        @pl.when(own - back >= low)
        def _():
            one_block(info[blocks + jnp.maximum(own - back, 0)], False)

    for pair in range(pairs):
        cols = pl.ds(pair * 128, 128)
        grad = query_acc[:, cols].astype(BF16).astype(F32)
        out_ref[:, cols] = (grad * cos_ref[...] - swap_halves(grad) * sin_ref[...]).astype(BF16)

    if final:

        @pl.when(step == first + pl.num_programs(0) - 1)
        def _():
            lane = lax.broadcasted_iota(jnp.int32, (rows, 128), 1)
            for part in range(blocks):
                spot = pl.ds(part * rows, rows)
                key_grad = key_acc[part]
                key_grad = key_grad[:rows] + pltpu.roll(key_grad[rows:], HD, 1)
                key_grad = (key_grad * (1.0 / math.sqrt(HD))).astype(BF16).astype(F32)
                value_grad = value_acc[part]
                value_grad = pltpu.roll(value_grad[:rows], HD, 1) + value_grad[rows:]
                turned = key_grad * cos_all[spot, :] - swap_halves(key_grad) * sin_all[spot, :]
                kv_out[spot, :] = jnp.where(lane < HD, turned, value_grad).astype(BF16)


def attention_backward(info, query, attended, grad, lse, kv, cosine, sine, rows, first, count, carried):
    total, query_width = query.shape
    blocks = total // rows
    pairs = query_width // 128
    final = first + count == blocks
    row_block = pl.BlockSpec((rows, query_width), lambda j, info: (j + first, 0))
    table_block = pl.BlockSpec((rows, 128), lambda j, info: (j + first, 0))
    whole = pl.BlockSpec((total, 128), lambda j, info: (0, 0))
    sums = pl.BlockSpec((blocks, 2 * rows, 128), lambda j, info: (0, 0, 0))
    sums_shape = jax.ShapeDtypeStruct((blocks, 2 * rows, 128), F32)
    in_specs = [
        row_block, row_block,
        pl.BlockSpec((rows, query_width), lambda j, info: (j, 0)),
        pl.BlockSpec((2 * pairs, rows), lambda j, info: (0, j + first)),
        whole, table_block, table_block, whole, whole,
    ]
    operands = [info, query, attended, grad, lse, kv, cosine, sine, cosine, sine]
    aliases = {}
    if first:
        aliases = {len(operands): 0, len(operands) + 1: 1, len(operands) + 2: 2}
        operands += carried
        in_specs += [pl.BlockSpec(memory_space=pl.ANY), sums, sums]
    out_specs = [row_block, sums, sums]
    out_shape = [jax.ShapeDtypeStruct((total, query_width + 128), BF16), sums_shape, sums_shape]
    if final:
        out_specs.append(whole)
        out_shape.append(jax.ShapeDtypeStruct((total, 128), BF16))
    return pl.pallas_call(
        functools.partial(attention_backward_kernel, first, final),
        grid_spec=pltpu.PrefetchScalarGridSpec(
            num_scalar_prefetch=1,
            grid=(count,),
            in_specs=in_specs,
            out_specs=out_specs,
            scratch_shapes=[
                pltpu.VMEM((blocks, 2 * rows, 128), BF16),
                pltpu.VMEM((blocks, 2 * rows, 128), BF16),
                pltpu.VMEM((rows, query_width), F32),
                pltpu.VMEM((2 * pairs, rows), F32),
            ],
        ),
        out_shape=out_shape,
        input_output_aliases=aliases,
        cost_estimate=pl.CostEstimate(flops=count * 6 * 10**9, bytes_accessed=count * 10**6, transcendentals=0),
        name="attention_backward",
    )(*operands)


def feed_forward_kernel(parts, first_row, *refs):
    values_refs = refs[:parts]
    grad_ref, gate_all, up_all = refs[parts : parts + 3]
    back_refs = refs[-7 - parts : -7]
    rows_all, mixed_all, slopes_all = refs[-10 - parts : -7 - parts]
    gate_w, up_w, rows_s, mixed_s, slopes_s, arrived, stored = refs[-7:]
    rows, width = values_refs[0].shape
    hidden = gate_w.shape[1]
    step = min(256, hidden)
    count, rest = divmod(hidden, step)

    def weight_copies(index, first, size):
        cols = pl.ds(first, size)
        return (
            pltpu.make_async_copy(gate_all.at[:, cols], gate_w.at[:, cols], arrived.at[0, index]),
            pltpu.make_async_copy(up_all.at[:, cols], up_w.at[:, cols], arrived.at[1, index]),
        )

    for index in range(count + (rest > 0)):
        for copy in weight_copies(index, index * step, step if index < count else rest):
            copy.start()
    for i in range(parts):
        rows_s[pl.ds(i * rows, rows), :] = values_refs[i][...]
    here = pl.ds(first_row, parts * rows)
    outs = [
        pltpu.make_async_copy(scratch, whole.at[here, :], stored.at[i])
        for i, (scratch, whole) in enumerate(((rows_s, rows_all), (mixed_s, mixed_all), (slopes_s, slopes_all)))
    ]
    outs[0].start()

    def columns(index, first, size):
        for copy in weight_copies(index, first, size):
            copy.wait()
        cols = pl.ds(first, size)
        values = rows_s[...]
        gate = mm(values, gate_w[:, cols])
        upward = mm(values, up_w[:, cols])
        grad = grad_ref[:, cols]
        sigma = 1.0 / (1.0 + jnp.exp(-gate))
        activated = gate * sigma
        mixed_s[:, cols] = (activated * upward).astype(BF16)
        slopes_s[:, cols] = (grad * upward * sigma * (1.0 + gate * (1.0 - sigma))).astype(BF16)
        slopes_s[:, pl.ds(hidden + first, size)] = (grad * activated).astype(BF16)

    @pl.loop(0, count)
    def _(index):
        columns(index, pl.multiple_of(index * step, 128), step)

    if rest:
        columns(count, hidden - rest, rest)
    outs[1].start()
    outs[2].start()

    part = min(256, width)

    @pl.loop(0, width // part)
    def _(index):
        here = pl.ds(pl.multiple_of(index * part, part), part)
        result = mm_nt(slopes_s[:, :hidden], gate_w[here, :]) + mm_nt(slopes_s[:, hidden:], up_w[here, :])
        for i in range(parts):
            back_refs[i][:, here] = result[i * rows : (i + 1) * rows].astype(BF16)

    for copy in outs:
        copy.wait()


def feed_forward(values, grad_mixed, gate_weight, up_weight, first, carried):
    parts = len(values)
    rows, width = values[0].shape
    total, hidden = grad_mixed.shape
    size = parts * rows
    block = first // size
    anywhere = pl.BlockSpec(memory_space=pl.ANY)
    operands = [*values, grad_mixed, gate_weight, up_weight, *carried]
    single = pl.BlockSpec((rows, width), lambda i: (0, 0))
    here = pl.BlockSpec((size, hidden), lambda i: (block, 0))
    return pl.pallas_call(
        functools.partial(feed_forward_kernel, parts, first),
        grid=(1,),
        in_specs=[*[single] * parts, here, *[anywhere] * (2 + len(carried))],
        out_specs=[*[anywhere] * 3, *[single] * parts],
        scratch_shapes=[
            pltpu.VMEM((width, hidden), BF16),
            pltpu.VMEM((width, hidden), BF16),
            pltpu.VMEM((size, width), BF16),
            pltpu.VMEM((size, hidden), BF16),
            pltpu.VMEM((size, 2 * hidden), BF16),
            pltpu.SemaphoreType.DMA((2, -(-hidden // 256))),
            pltpu.SemaphoreType.DMA((3,)),
        ],
        out_shape=[
            jax.ShapeDtypeStruct((total, width), BF16),
            jax.ShapeDtypeStruct((total, hidden), BF16),
            jax.ShapeDtypeStruct((total, 2 * hidden), BF16),
            *[jax.ShapeDtypeStruct((rows, width), BF16)] * parts,
        ],
        input_output_aliases={parts + 3 + i: i for i in range(len(carried))},
        cost_estimate=pl.CostEstimate(flops=parts * 6 * 10**9, bytes_accessed=10**6, transcendentals=0),
        name="feed_forward",
    )(*operands)


def weight_gradient_kernel(values_ref, grad_ref, out_ref):
    out_ref[...] = mm_tn(values_ref[...], grad_ref[...]).astype(BF16)


def weight_gradient(values, grad):
    total, features = values.shape
    outputs = grad.shape[1]
    tile = math.gcd(512, features)
    return pl.pallas_call(
        weight_gradient_kernel,
        grid=(features // tile,),
        in_specs=[
            pl.BlockSpec((total, tile), lambda i: (0, i)),
            pl.BlockSpec((total, outputs), lambda i: (0, 0)),
        ],
        out_specs=pl.BlockSpec((tile, outputs), lambda i: (i, 0)),
        out_shape=jax.ShapeDtypeStruct((features, outputs), BF16),
        cost_estimate=pl.CostEstimate(
            flops=2 * total * features * outputs, bytes_accessed=10**6, transcendentals=0
        ),
        name="weight_gradient",
    )(values, grad)


def norm_scale(values):
    return lax.rsqrt(jnp.mean(values * values, axis=-1, keepdims=True) + EPS)


def norm_backward(values, scale, gain, grads):
    weighted = grads * gain
    gain_grad = jnp.sum(grads * values * scale, axis=0)
    cubed = scale * scale * scale
    value_grad = scale * weighted - values * cubed * jnp.mean(weighted * values, axis=-1, keepdims=True)
    return gain_grad, value_grad


def over_batch(term):
    return lax.psum_scatter(term, "batch", scatter_dimension=0, tiled=True)


def pick(parts, index, axis):
    return lax.dynamic_index_in_dim(parts, index, axis, keepdims=False)


def line_sum(term, waits):
    batch_parts = lax.axis_size("batch")
    line = batch_parts // 2
    index = lax.axis_index("batch")
    core, place = index % 2, index // 2
    parts = term.reshape(line, 2, term.shape[0] // batch_parts, term.shape[1])
    swap = [(i, i ^ 1) for i in range(batch_parts)]
    arrived = lax.ppermute(pick(parts, 1 - core, 1), "batch", swap)
    parts = (pick(parts, core, 1).astype(F32) + arrived.astype(F32)).astype(BF16)
    up = down = None
    for step in range(1, line):
        parts, up, down = lax.optimization_barrier((parts, up, down, *waits.get(step, ())))[:3]
        rising = pick(parts, jnp.minimum(place + line - step, line - 1), 0)
        falling = pick(parts, jnp.maximum(place - line + step, 0), 0)
        if up is not None:
            rising = (rising.astype(F32) + up.astype(F32)).astype(BF16)
            falling = (falling.astype(F32) + down.astype(F32)).astype(BF16)
        up = lax.ppermute(rising, "batch", [(i, i + 2) for i in range(2 * step)])
        down = lax.ppermute(
            falling, "batch", [(i, i - 2) for i in range(batch_parts - 2 * step, batch_parts)]
        )
    return pick(after(parts, *waits.get(line, ())), place, 0), up, down


def split_total_kernel(own_ref, up_ref, down_ref, *out_refs):
    total = own_ref[...].astype(F32) + up_ref[...].astype(F32) + down_ref[...].astype(F32)
    first = 0
    for out_ref in out_refs:
        size = out_ref.shape[1]
        out_ref[...] = total[:, first : first + size]
        first += size


def split_total(terms, sizes):
    rows = terms[0].shape[0]
    return pl.pallas_call(
        split_total_kernel,
        out_shape=[jax.ShapeDtypeStruct((rows, size), F32) for size in sizes],
        cost_estimate=pl.CostEstimate(flops=10**8, bytes_accessed=10**6, transcendentals=0),
        name="split_total",
    )(*terms)


def shards(
    tokens, seq_count, query_weight, key_weight, value_weight, out_weight,
    gate_weight, up_weight, down_weight, attention_gain, feedforward_gain, cotangent,
):
    seq_parts = lax.axis_size("seq")
    batch_parts = lax.axis_size("batch")
    part = lax.axis_index("seq")
    parity = lax.axis_index("batch") % 2
    rows = tokens.shape[1]
    group_rows = rows * seq_parts
    width = tokens.shape[2]

    order = jnp.arange(seq_parts, dtype=jnp.int32)
    swapped = ((order & 1) << 1) | (order >> 1)
    masks = jnp.where(parity == 0, order, swapped)
    owners = part ^ masks
    other = part ^ order
    spots = jnp.where(parity == 0, other, ((other & 1) << 1) | (other >> 1))
    seq_length = group_rows // seq_count[0]
    firsts = (owners * rows) // seq_length * seq_length // rows
    info = jnp.concatenate([owners, spots, firsts]).astype(jnp.int32)

    index = (owners[:, None] * rows + jnp.arange(rows, dtype=jnp.int32)[None, :]).reshape(-1)
    places = index - index // seq_length * seq_length
    lane = jnp.arange(128, dtype=jnp.int32)
    inverse = jnp.exp((lane % (HD // 2)).astype(F32) * (-2.0 * math.log(10000.0) / HD))
    angles = places.astype(F32)[:, None] * inverse[None, :]
    cosine = jnp.cos(angles)
    sine = jnp.sin(angles) * jnp.where(lane % HD < HD // 2, -1.0, 1.0)[None, :]

    inputs = tokens[0].astype(F32)
    scale_one = norm_scale(inputs)
    normed_one = (inputs * scale_one * attention_gain).astype(BF16)
    qkv_weight = jnp.concatenate([query_weight, key_weight, value_weight], axis=1)
    half = group_rows // 2

    near = first_swap(normed_one)
    side = second_swap(normed_one)
    qkv_own = mm(normed_one, qkv_weight)
    far = second_swap(after(near, qkv_own))
    normed_one_blocks = [normed_one, near, side, far]
    qkv = jnp.concatenate([qkv_own, *(mm(block, qkv_weight) for block in normed_one_blocks[1:])], axis=0)

    grad_ffn = after(cotangent[0], far)
    grad_near = first_swap(grad_ffn)
    grad_side = second_swap(grad_ffn)

    att_upper, query_upper, kv, lse_upper = attention_forward(info, qkv, cosine, sine, rows, seq_parts // 2, seq_parts // 2)
    branch_upper = mm(att_upper, out_weight).astype(BF16)
    arrived = second_swap(branch_upper)
    later_qkv, grad_near, grad_side = lax.optimization_barrier((after(qkv, branch_upper), grad_near, grad_side))
    grad_far = second_swap(grad_near)
    att_lower, query_lower, _, lse_lower = attention_forward(info, later_qkv, cosine, sine, rows, 0, seq_parts // 2)
    branch_lower = mm(att_lower, out_weight).astype(BF16)
    attended = jnp.concatenate([att_lower, att_upper], axis=0)
    query = jnp.concatenate([query_lower, query_upper], axis=0)
    lse = jnp.concatenate([lse_lower, lse_upper], axis=1)
    branch, passed = split_sum(branch_lower, after(arrived, branch_lower))
    passed = first_swap(after(passed, grad_far))
    grad_rows = jnp.concatenate([grad_near, grad_side, grad_far, cotangent[0]], axis=0)
    grad_mixed = mm_nt(grad_rows, down_weight)
    hidden = inputs + branch + after(passed, grad_mixed).astype(F32)

    scale_two = norm_scale(hidden)
    normed_two = (hidden * scale_two * feedforward_gain).astype(BF16)
    near = first_swap(normed_two)
    side = second_swap(normed_two)
    *carried, back_own = feed_forward([normed_two], grad_mixed, gate_weight, up_weight, 3 * rows, [])
    normed_one_rows = jnp.concatenate(normed_one_blocks, axis=0)
    near, side, normed_one_rows, grad_rows, attended, query, lse, *carried = lax.optimization_barrier(
        (near, side, normed_one_rows, grad_rows, attended, query, lse, *carried)
    )
    far = second_swap(near)
    *carried, back_near, back_side = feed_forward([near, side], grad_mixed, gate_weight, up_weight, 0, carried)
    sum_side = second_swap(after(back_side, far))
    *carried, back_far = feed_forward([far], grad_mixed, gate_weight, up_weight, 2 * rows, carried)
    normed_two_rows, mixed, slopes = carried
    sum_far = second_swap(back_far)
    down_term = mm_tn(mixed, after(grad_rows, sum_side)).astype(BF16)
    near_sum = (back_near.astype(F32) + after(sum_far, down_term).astype(F32)).astype(BF16)
    passed = first_swap(near_sum)
    gate_up_term = weight_gradient(normed_two_rows, after(slopes, near_sum))
    grad_normed_two = back_own.astype(F32) + sum_side.astype(F32) + after(passed, gate_up_term).astype(F32)
    down_grad = over_batch(after(down_term, sum_far))
    gate_up_grad = over_batch(after(gate_up_term, passed))

    grad_out = cotangent[0].astype(F32)
    feed_gain_term, grad_hidden_norm = norm_backward(hidden, scale_two, feedforward_gain, grad_normed_two)
    grad_hidden = grad_out + grad_hidden_norm
    grad_branch = grad_hidden.astype(BF16)
    near = first_swap(grad_branch)
    side = second_swap(grad_branch)

    def attended_grad(block):
        return mm_nt(block, out_weight).astype(BF16)

    def backward(grad, first, count, carried):
        return attention_backward(
            info, query, attended, grad, lse, kv, cosine, sine, rows, first, count, carried
        )

    ffn_upper = mm(after(mixed, grad_branch)[rows : 3 * rows], down_weight).astype(BF16)
    carried = backward(after(attended_grad(grad_branch), ffn_upper), 0, 1, [])
    near, side, *carried = lax.optimization_barrier((near, side, *carried))
    far = second_swap(near)
    middle = attended_grad(jnp.concatenate([near, side], axis=0))
    carried = backward(middle, 1, 2, carried)
    far = after(far, *carried)
    ffn_arrived = second_swap(after(ffn_upper, far))
    grad_branch_rows = jnp.concatenate([grad_branch, near, side, far], axis=0)
    out_term = mm_tn(attended, grad_branch_rows).astype(BF16)
    grad_qkv, _, _, grad_kv = backward(attended_grad(after(far, out_term)), 3, 1, carried)
    grad_qkv = lax.dynamic_update_slice(grad_qkv, grad_kv, (0, grad_qkv.shape[1] - grad_kv.shape[1]))
    upper = mm_nt(after(grad_qkv, down_grad, ffn_arrived)[half:], qkv_weight).astype(BF16)
    arrived = second_swap(upper)
    lower = mm_nt(after(grad_qkv, upper)[:half], qkv_weight).astype(BF16)
    qkv_term = weight_gradient(normed_one_rows, after(grad_qkv, upper))
    kept, passed = split_sum(lower, after(arrived, qkv_term, lower))
    arrived_passed = first_swap(passed)
    later_mixed = after(mixed, upper)
    ffn_passed = mm(later_mixed[:rows], down_weight) + ffn_arrived[rows:].astype(F32)
    ffn_passed = first_swap(ffn_passed.astype(BF16))
    ffn_kept = mm(later_mixed[3 * rows :], down_weight) + ffn_arrived[:rows].astype(F32)
    grad_normed_one = kept + arrived_passed.astype(F32)
    attention_gain_term, grad_inputs_norm = norm_backward(inputs, scale_one, attention_gain, grad_normed_one)
    input_grad = grad_hidden + grad_inputs_norm
    layer_out = (hidden + ffn_kept + ffn_passed.astype(F32)).astype(BF16)

    devices = seq_parts * batch_parts
    gains = jnp.concatenate(
        [attention_gain_term.reshape(devices, -1), feed_gain_term.reshape(devices, -1)], axis=1
    )
    gains = jnp.sum(lax.all_to_all(gains, ("seq", "batch"), 0, 0, tiled=True), axis=0)
    share = width // devices
    query_width = query_weight.shape[1]
    key_width = key_weight.shape[1]
    line = batch_parts // 2
    out_terms = line_sum(out_term, {1: (qkv_term,), 2: (lower,), 3: (passed,)})
    out_grad = sum(term.astype(F32) for term in out_terms)
    qkv_terms = line_sum(qkv_term, {1: (lower,), 2: (passed,), 3: (arrived_passed,), line: (gains,)})
    query_grad, key_grad, value_grad = split_total(qkv_terms, (query_width, key_width, key_width))
    gate_up_grad = after(gate_up_grad, gains, query_grad, out_grad)
    hidden_width = gate_weight.shape[1]
    return (
        layer_out[None],
        input_grad[None],
        query_grad,
        key_grad,
        value_grad,
        out_grad,
        gate_up_grad[:, :hidden_width].astype(F32),
        gate_up_grad[:, hidden_width:].astype(F32),
        down_grad.astype(F32),
        gains[:share],
        gains[share:],
    )


def solution(mesh):
    return jax.shard_map(
        shards,
        mesh=mesh,
        in_specs=(
            P("batch", "seq", None),
            P("batch"),
            P(None, "seq"),
            P(None, "seq"),
            P(None, "seq"),
            P("seq", None),
            P(None, "seq"),
            P(None, "seq"),
            P("seq", None),
            P(),
            P(),
            P("batch", "seq", None),
        ),
        out_specs=(
            P("batch", "seq", None),
            P("batch", "seq", None),
            P("batch", "seq"),
            P("batch", "seq"),
            P("batch", "seq"),
            P(("seq", "batch"), None),
            P("batch", "seq"),
            P("batch", "seq"),
            P(("seq", "batch"), None),
            P(("seq", "batch")),
            P(("seq", "batch")),
        ),
        check_vma=False,
    )
```

```python
import functools
import math

import jax
import jax.numpy as jnp
from jax import lax
from jax.experimental import pallas as pl
from jax.experimental.pallas import tpu as pltpu
from jax.sharding import PartitionSpec as P

HD = 64
EPS = 1e-05
NEG = -1e30
F32 = jnp.float32
BF16 = jnp.bfloat16


def mm(a, b):
    return lax.dot_general(a, b, (((1,), (0,)), ((), ())), preferred_element_type=F32)


def mm_nt(a, b):
    return lax.dot_general(a, b, (((1,), (1,)), ((), ())), preferred_element_type=F32)


def mm_tn(a, b):
    return lax.dot_general(a, b, (((0,), (0,)), ((), ())), preferred_element_type=F32)


def exchange(values, even_mask, odd_mask):
    seq_parts = lax.axis_size("seq")
    batch_parts = lax.axis_size("batch")
    pairs = []
    for part in range(seq_parts):
        for group in range(batch_parts):
            mask = even_mask if group % 2 == 0 else odd_mask
            pairs.append((part * batch_parts + group, (part ^ mask) * batch_parts + group))
    return lax.ppermute(values, ("seq", "batch"), pairs)


def after(value, *others):
    return lax.optimization_barrier((value, *others))[0]


def first_swap(values):
    return exchange(values, 1, 2)


def second_swap(values):
    return exchange(values, 2, 1)


def split_sum(lower, arrived):
    rows = lower.shape[0] // 2
    total = lower.astype(F32) + arrived.astype(F32)
    return total[:rows], total[rows:].astype(BF16)


def norm_project_kernel(rows_ref, gain_ref, weight_ref, *refs):
    normed_ref, out_ref = refs[-2:]
    values = rows_ref[...].astype(F32)
    scale = lax.rsqrt(jnp.mean(values * values, axis=-1, keepdims=True) + EPS)
    normed_ref[...] = (values * scale * gain_ref[...]).astype(BF16)
    out_ref[...] = mm(normed_ref[...], weight_ref[...])


def norm_project(block, gain, weight, place, total, carried):
    rows, width = block.shape
    outputs = weight.shape[1]
    return pl.pallas_call(
        norm_project_kernel,
        grid=(1,),
        in_specs=[
            pl.BlockSpec((rows, width), lambda i: (0, 0)),
            pl.BlockSpec((1, width), lambda i: (0, 0)),
            pl.BlockSpec((width, outputs), lambda i: (0, 0)),
            *[pl.BlockSpec(memory_space=pl.ANY)] * len(carried),
        ],
        out_specs=[
            pl.BlockSpec((rows, width), lambda i: (place, 0)),
            pl.BlockSpec((rows, outputs), lambda i: (place, 0)),
        ],
        out_shape=[jax.ShapeDtypeStruct((total, width), BF16), jax.ShapeDtypeStruct((total, outputs), F32)],
        input_output_aliases={3 + i: i for i in range(len(carried))},
        cost_estimate=pl.CostEstimate(flops=10**9, bytes_accessed=10**6, transcendentals=0),
        name="norm_project",
    )(block, gain[None], weight, *carried)


def swap_halves(values):
    lane = lax.broadcasted_iota(jnp.int32, values.shape, 1)
    ahead = pltpu.roll(values, values.shape[1] - HD // 2, 1)
    behind = pltpu.roll(values, HD // 2, 1)
    return jnp.where(lane % HD < HD // 2, ahead, behind)


def padded_keys(keys_values):
    lane = lax.broadcasted_iota(jnp.int32, keys_values.shape, 1)
    zero = jnp.zeros_like(keys_values)
    left = jnp.where(lane < HD, keys_values, zero)
    right = pltpu.roll(left, HD, 1)
    return jnp.concatenate([left, right], axis=0)


def padded_values(keys_values):
    lane = lax.broadcasted_iota(jnp.int32, keys_values.shape, 1)
    zero = jnp.zeros_like(keys_values)
    right = jnp.where(lane >= HD, keys_values, zero)
    left = pltpu.roll(right, HD, 1)
    return jnp.concatenate([left, right], axis=0)


def attention_forward_kernel(
    first, info, query_ref, kv_ref, cos_ref, sin_ref, cos_all, sin_all,
    attended_ref, rotated_ref, kv_out, lse_ref, keys_s, values_s, acc_s, max_s,
):
    step = pl.program_id(0) + first
    rows = query_ref.shape[0]
    pairs = query_ref.shape[1] // 128
    blocks = kv_ref.shape[0] // rows

    @pl.when(step == first)
    def _():
        for part in range(blocks):
            here = pl.ds(part * rows, rows)
            kv = kv_ref[here, :]
            lane = lax.broadcasted_iota(jnp.int32, kv.shape, 1)
            turned = kv * cos_all[here, :] + swap_halves(kv) * sin_all[here, :]
            kv = jnp.where(lane < HD, turned, kv).astype(BF16).astype(F32)
            kv_out[here, :] = kv.astype(BF16)
            keys_s[part] = (padded_keys(kv) * (1.0 / math.sqrt(HD))).astype(BF16)
            both = jnp.transpose(padded_values(kv))
            feature = lax.broadcasted_iota(jnp.int32, both.shape, 0)
            key = lax.broadcasted_iota(jnp.int32, both.shape, 1)
            ones = jnp.where((feature < HD) == (key < rows), 1.0, 0.0)
            values_s[part] = jnp.concatenate([both, ones], axis=0).astype(BF16)

    own = info[step]
    low = info[2 * blocks + step]
    key_index = lax.broadcasted_iota(jnp.int32, (2 * rows, rows), 0) % rows
    query_index = lax.broadcasted_iota(jnp.int32, (2 * rows, rows), 1)
    allowed = key_index <= query_index
    at = info[blocks + own]

    def spread(upper, lower, height):
        return jnp.concatenate(
            [jnp.broadcast_to(upper, (height, rows)), jnp.broadcast_to(lower, (height, rows))], axis=0
        )

    for pair in range(pairs):
        cols = pl.ds(pair * 128, 128)
        query = query_ref[:, cols]
        query = (query * cos_ref[...] + swap_halves(query) * sin_ref[...]).astype(BF16)
        rotated_ref[:, cols] = query
        scores = jnp.where(allowed, mm_nt(keys_s[at], query), NEG)
        tops = [jnp.max(scores[i * rows : (i + 1) * rows], axis=0, keepdims=True) for i in range(2)]
        probs = jnp.exp(scores - spread(*tops, rows)).astype(BF16)
        for i in range(2):
            max_s[2 * pair + i : 2 * pair + i + 1, :] = tops[i]
        acc_s[pair] = mm(values_s[at], probs)

    for back in range(1, blocks):

        @pl.when(own - back >= low)
        def _():
            there = info[blocks + jnp.maximum(own - back, 0)]
            for pair in range(pairs):
                query = rotated_ref[:, pl.ds(pair * 128, 128)]
                scores = mm_nt(keys_s[there], query)
                tops, scales = [], []
                for i in range(2):
                    before = max_s[2 * pair + i : 2 * pair + i + 1, :]
                    top = jnp.maximum(
                        before, jnp.max(scores[i * rows : (i + 1) * rows], axis=0, keepdims=True)
                    )
                    tops.append(top)
                    scales.append(jnp.exp(before - top))
                    max_s[2 * pair + i : 2 * pair + i + 1, :] = top
                probs = jnp.exp(scores - spread(*tops, rows)).astype(BF16)
                factor = spread(*scales, HD)
                factor = jnp.concatenate([factor, factor], axis=0)
                acc_s[pair] = acc_s[pair] * factor + mm(values_s[there], probs)

    for pair in range(pairs):
        total = acc_s[pair][128:, :]
        result = acc_s[pair][:128, :] / total
        attended_ref[:, pl.ds(pair * 128, 128)] = jnp.transpose(result).astype(BF16)
        for i in range(2):
            spot = slice(2 * pair + i, 2 * pair + i + 1)
            lse_ref[spot, :] = max_s[spot, :] + jnp.log(total[i * HD : i * HD + 1, :])


def attention_forward(info, qkv, cosine, sine, rows, first, count):
    total, width = qkv.shape
    blocks = total // rows
    query_width = width - 2 * HD
    pairs = query_width // 128
    last = query_width // 128
    return pl.pallas_call(
        functools.partial(attention_forward_kernel, first),
        grid_spec=pltpu.PrefetchScalarGridSpec(
            num_scalar_prefetch=1,
            grid=(count,),
            in_specs=[
                pl.BlockSpec((rows, query_width), lambda j, info: (j + first, 0)),
                pl.BlockSpec((total, 128), lambda j, info: (0, last)),
                pl.BlockSpec((rows, 128), lambda j, info: (j + first, 0)),
                pl.BlockSpec((rows, 128), lambda j, info: (j + first, 0)),
                pl.BlockSpec((total, 128), lambda j, info: (0, 0)),
                pl.BlockSpec((total, 128), lambda j, info: (0, 0)),
            ],
            out_specs=[
                pl.BlockSpec((rows, query_width), lambda j, info: (j, 0)),
                pl.BlockSpec((rows, query_width), lambda j, info: (j, 0)),
                pl.BlockSpec((total, 128), lambda j, info: (0, 0)),
                pl.BlockSpec((2 * pairs, rows), lambda j, info: (0, j)),
            ],
            scratch_shapes=[
                pltpu.VMEM((blocks, 2 * rows, 128), BF16),
                pltpu.VMEM((blocks, 256, 2 * rows), BF16),
                pltpu.VMEM((pairs, 256, rows), F32),
                pltpu.VMEM((2 * pairs, rows), F32),
            ],
        ),
        cost_estimate=pl.CostEstimate(flops=count * 4 * 10**9, bytes_accessed=count * 10**6, transcendentals=0),
        out_shape=[
            jax.ShapeDtypeStruct((count * rows, query_width), BF16),
            jax.ShapeDtypeStruct((count * rows, query_width), BF16),
            jax.ShapeDtypeStruct((total, 128), BF16),
            jax.ShapeDtypeStruct((2 * pairs, count * rows), F32),
        ],
        name="attention_forward",
    )(info, qkv, qkv, cosine, sine, cosine, sine)


def attention_backward_kernel(
    first, final, info, query_ref, att_ref, grad_ref, lse_ref, kv_ref, cos_ref, sin_ref, cos_all, sin_all, *refs
):
    if first:
        refs = refs[1:]
        key_in, value_in = refs[:2]
        refs = refs[2:]
    else:
        key_in = value_in = None
    out_ref, key_acc, value_acc = refs[:3]
    refs = refs[3:]
    if final:
        kv_out = refs[0]
        refs = refs[1:]
    keys_s, values_s, query_acc, delta_s = refs
    step = pl.program_id(0) + first
    rows = query_ref.shape[0]
    query_width = query_ref.shape[1]
    pairs = query_width // 128
    blocks = kv_ref.shape[0] // rows

    @pl.when(step == first)
    def _():
        for part in range(blocks):
            kv = kv_ref[pl.ds(part * rows, rows), :].astype(F32)
            keys_s[part] = (padded_keys(kv) * (1.0 / math.sqrt(HD))).astype(BF16)
            values_s[part] = padded_values(kv).astype(BF16)
        if first:
            key_acc[...] = key_in[...]
            value_acc[...] = value_in[...]
        else:
            key_acc[...] = jnp.zeros_like(key_acc)
            value_acc[...] = jnp.zeros_like(value_acc)

    own = info[step]
    low = info[2 * blocks + step]
    at = info[blocks + own]
    key_index = lax.broadcasted_iota(jnp.int32, (2 * rows, rows), 0) % rows
    query_index = lax.broadcasted_iota(jnp.int32, (2 * rows, rows), 1)
    allowed = key_index <= query_index
    top_half = lax.broadcasted_iota(jnp.int32, (2 * rows, rows), 0) < rows

    products = att_ref[...].astype(F32) * grad_ref[...].astype(F32)
    head_row = lax.broadcasted_iota(jnp.int32, (2 * pairs, query_width), 0)
    head_col = lax.broadcasted_iota(jnp.int32, (2 * pairs, query_width), 1) // HD
    picker = jnp.where(head_row == head_col, 1.0, 0.0)
    delta_s[...] = lax.dot_general(
        picker, products, (((1,), (1,)), ((), ())),
        precision=lax.Precision.HIGHEST, preferred_element_type=F32,
    )

    def one_block(where_, masked):
        keys = keys_s[where_]
        values = values_s[where_]
        for pair in range(pairs):
            cols = pl.ds(pair * 128, 128)
            query = query_ref[:, cols]
            grad = grad_ref[:, cols]
            lse = jnp.where(
                top_half, lse_ref[2 * pair : 2 * pair + 1, :], lse_ref[2 * pair + 1 : 2 * pair + 2, :]
            )
            delta = jnp.where(
                top_half, delta_s[2 * pair : 2 * pair + 1, :], delta_s[2 * pair + 1 : 2 * pair + 2, :]
            )
            scores = mm_nt(keys, query) - lse
            if masked:
                scores = jnp.where(allowed, scores, NEG)
            probs = jnp.exp(scores)
            grad_probs = mm_nt(values, grad)
            grad_scores = (probs * (grad_probs - delta)).astype(BF16)
            value_acc[where_] += mm(probs.astype(BF16), grad)
            key_acc[where_] += mm(grad_scores, query)
            part = mm_tn(grad_scores, keys)
            if masked:
                query_acc[:, cols] = part
            else:
                query_acc[:, cols] += part

    one_block(at, True)
    for back in range(1, blocks):

        @pl.when(own - back >= low)
        def _():
            one_block(info[blocks + jnp.maximum(own - back, 0)], False)

    for pair in range(pairs):
        cols = pl.ds(pair * 128, 128)
        grad = query_acc[:, cols].astype(BF16).astype(F32)
        out_ref[:, cols] = (grad * cos_ref[...] - swap_halves(grad) * sin_ref[...]).astype(BF16)

    if final:

        @pl.when(step == first + pl.num_programs(0) - 1)
        def _():
            lane = lax.broadcasted_iota(jnp.int32, (rows, 128), 1)
            for part in range(blocks):
                spot = pl.ds(part * rows, rows)
                key_grad = key_acc[part]
                key_grad = key_grad[:rows] + pltpu.roll(key_grad[rows:], HD, 1)
                key_grad = (key_grad * (1.0 / math.sqrt(HD))).astype(BF16).astype(F32)
                value_grad = value_acc[part]
                value_grad = pltpu.roll(value_grad[:rows], HD, 1) + value_grad[rows:]
                turned = key_grad * cos_all[spot, :] - swap_halves(key_grad) * sin_all[spot, :]
                kv_out[spot, :] = jnp.where(lane < HD, turned, value_grad).astype(BF16)


def attention_backward(info, query, attended, grad, lse, kv, cosine, sine, rows, first, count, carried):
    total, query_width = query.shape
    blocks = total // rows
    pairs = query_width // 128
    final = first + count == blocks
    row_block = pl.BlockSpec((rows, query_width), lambda j, info: (j + first, 0))
    table_block = pl.BlockSpec((rows, 128), lambda j, info: (j + first, 0))
    whole = pl.BlockSpec((total, 128), lambda j, info: (0, 0))
    sums = pl.BlockSpec((blocks, 2 * rows, 128), lambda j, info: (0, 0, 0))
    sums_shape = jax.ShapeDtypeStruct((blocks, 2 * rows, 128), F32)
    in_specs = [
        row_block, row_block,
        pl.BlockSpec((rows, query_width), lambda j, info: (j, 0)),
        pl.BlockSpec((2 * pairs, rows), lambda j, info: (0, j + first)),
        whole, table_block, table_block, whole, whole,
    ]
    operands = [info, query, attended, grad, lse, kv, cosine, sine, cosine, sine]
    aliases = {}
    if first:
        aliases = {len(operands): 0, len(operands) + 1: 1, len(operands) + 2: 2}
        operands += carried
        in_specs += [pl.BlockSpec(memory_space=pl.ANY), sums, sums]
    out_specs = [row_block, sums, sums]
    out_shape = [jax.ShapeDtypeStruct((total, query_width + 128), BF16), sums_shape, sums_shape]
    if final:
        out_specs.append(whole)
        out_shape.append(jax.ShapeDtypeStruct((total, 128), BF16))
    return pl.pallas_call(
        functools.partial(attention_backward_kernel, first, final),
        grid_spec=pltpu.PrefetchScalarGridSpec(
            num_scalar_prefetch=1,
            grid=(count,),
            in_specs=in_specs,
            out_specs=out_specs,
            scratch_shapes=[
                pltpu.VMEM((blocks, 2 * rows, 128), BF16),
                pltpu.VMEM((blocks, 2 * rows, 128), BF16),
                pltpu.VMEM((rows, query_width), F32),
                pltpu.VMEM((2 * pairs, rows), F32),
            ],
        ),
        out_shape=out_shape,
        input_output_aliases=aliases,
        cost_estimate=pl.CostEstimate(flops=count * 6 * 10**9, bytes_accessed=count * 10**6, transcendentals=0),
        name="attention_backward",
    )(*operands)


def feed_forward_kernel(parts, first_row, *refs):
    values_refs = refs[:parts]
    grad_ref, gate_all, up_all = refs[parts : parts + 3]
    back_refs = refs[-7 - parts : -7]
    rows_all, mixed_all, slopes_all = refs[-10 - parts : -7 - parts]
    gate_w, up_w, rows_s, mixed_s, slopes_s, arrived, stored = refs[-7:]
    rows, width = values_refs[0].shape
    hidden = gate_w.shape[1]
    step = min(256, hidden)
    count, rest = divmod(hidden, step)

    def weight_copies(index, first, size):
        cols = pl.ds(first, size)
        return (
            pltpu.make_async_copy(gate_all.at[:, cols], gate_w.at[:, cols], arrived.at[0, index]),
            pltpu.make_async_copy(up_all.at[:, cols], up_w.at[:, cols], arrived.at[1, index]),
        )

    for index in range(count + (rest > 0)):
        for copy in weight_copies(index, index * step, step if index < count else rest):
            copy.start()
    for i in range(parts):
        rows_s[pl.ds(i * rows, rows), :] = values_refs[i][...]
    here = pl.ds(first_row, parts * rows)
    outs = [
        pltpu.make_async_copy(scratch, whole.at[here, :], stored.at[i])
        for i, (scratch, whole) in enumerate(((rows_s, rows_all), (mixed_s, mixed_all), (slopes_s, slopes_all)))
    ]
    outs[0].start()

    def columns(index, first, size):
        for copy in weight_copies(index, first, size):
            copy.wait()
        cols = pl.ds(first, size)
        values = rows_s[...]
        gate = mm(values, gate_w[:, cols])
        upward = mm(values, up_w[:, cols])
        grad = grad_ref[:, cols]
        sigma = 1.0 / (1.0 + jnp.exp(-gate))
        activated = gate * sigma
        mixed_s[:, cols] = (activated * upward).astype(BF16)
        slopes_s[:, cols] = (grad * upward * sigma * (1.0 + gate * (1.0 - sigma))).astype(BF16)
        slopes_s[:, pl.ds(hidden + first, size)] = (grad * activated).astype(BF16)

    @pl.loop(0, count)
    def _(index):
        columns(index, pl.multiple_of(index * step, 128), step)

    if rest:
        columns(count, hidden - rest, rest)
    outs[1].start()
    outs[2].start()

    part = min(256, width)

    @pl.loop(0, width // part)
    def _(index):
        here = pl.ds(pl.multiple_of(index * part, part), part)
        result = mm_nt(slopes_s[:, :hidden], gate_w[here, :]) + mm_nt(slopes_s[:, hidden:], up_w[here, :])
        for i in range(parts):
            back_refs[i][:, here] = result[i * rows : (i + 1) * rows].astype(BF16)

    for copy in outs:
        copy.wait()


def feed_forward(values, grad_mixed, gate_weight, up_weight, first, carried):
    parts = len(values)
    rows, width = values[0].shape
    total, hidden = grad_mixed.shape
    size = parts * rows
    block = first // size
    anywhere = pl.BlockSpec(memory_space=pl.ANY)
    operands = [*values, grad_mixed, gate_weight, up_weight, *carried]
    single = pl.BlockSpec((rows, width), lambda i: (0, 0))
    here = pl.BlockSpec((size, hidden), lambda i: (block, 0))
    return pl.pallas_call(
        functools.partial(feed_forward_kernel, parts, first),
        grid=(1,),
        in_specs=[*[single] * parts, here, *[anywhere] * (2 + len(carried))],
        out_specs=[*[anywhere] * 3, *[single] * parts],
        scratch_shapes=[
            pltpu.VMEM((width, hidden), BF16),
            pltpu.VMEM((width, hidden), BF16),
            pltpu.VMEM((size, width), BF16),
            pltpu.VMEM((size, hidden), BF16),
            pltpu.VMEM((size, 2 * hidden), BF16),
            pltpu.SemaphoreType.DMA((2, -(-hidden // 256))),
            pltpu.SemaphoreType.DMA((3,)),
        ],
        out_shape=[
            jax.ShapeDtypeStruct((total, width), BF16),
            jax.ShapeDtypeStruct((total, hidden), BF16),
            jax.ShapeDtypeStruct((total, 2 * hidden), BF16),
            *[jax.ShapeDtypeStruct((rows, width), BF16)] * parts,
        ],
        input_output_aliases={parts + 3 + i: i for i in range(len(carried))},
        cost_estimate=pl.CostEstimate(flops=parts * 6 * 10**9, bytes_accessed=10**6, transcendentals=0),
        name="feed_forward",
    )(*operands)


def weight_gradient_kernel(values_ref, grad_ref, out_ref):
    out_ref[...] = mm_tn(values_ref[...], grad_ref[...]).astype(BF16)


def weight_gradient(values, grad):
    total, features = values.shape
    outputs = grad.shape[1]
    tile = math.gcd(512, features)
    return pl.pallas_call(
        weight_gradient_kernel,
        grid=(features // tile,),
        in_specs=[
            pl.BlockSpec((total, tile), lambda i: (0, i)),
            pl.BlockSpec((total, outputs), lambda i: (0, 0)),
        ],
        out_specs=pl.BlockSpec((tile, outputs), lambda i: (i, 0)),
        out_shape=jax.ShapeDtypeStruct((features, outputs), BF16),
        cost_estimate=pl.CostEstimate(
            flops=2 * total * features * outputs, bytes_accessed=10**6, transcendentals=0
        ),
        name="weight_gradient",
    )(values, grad)


def norm_scale(values):
    return lax.rsqrt(jnp.mean(values * values, axis=-1, keepdims=True) + EPS)


def norm_backward(values, scale, gain, grads):
    weighted = grads * gain
    gain_grad = jnp.sum(grads * values * scale, axis=0)
    cubed = scale * scale * scale
    value_grad = scale * weighted - values * cubed * jnp.mean(weighted * values, axis=-1, keepdims=True)
    return gain_grad, value_grad


def over_batch(term):
    return lax.psum_scatter(term, "batch", scatter_dimension=0, tiled=True)


def pick(parts, index, axis):
    return lax.dynamic_index_in_dim(parts, index, axis, keepdims=False)


def line_sum(term, waits):
    batch_parts = lax.axis_size("batch")
    line = batch_parts // 2
    index = lax.axis_index("batch")
    core, place = index % 2, index // 2
    parts = term.reshape(line, 2, term.shape[0] // batch_parts, term.shape[1])
    swap = [(i, i ^ 1) for i in range(batch_parts)]
    arrived = lax.ppermute(pick(parts, 1 - core, 1), "batch", swap)
    parts = (pick(parts, core, 1).astype(F32) + arrived.astype(F32)).astype(BF16)
    up = down = None
    for step in range(1, line):
        parts, up, down = lax.optimization_barrier((parts, up, down, *waits.get(step, ())))[:3]
        rising = pick(parts, jnp.minimum(place + line - step, line - 1), 0)
        falling = pick(parts, jnp.maximum(place - line + step, 0), 0)
        if up is not None:
            rising = (rising.astype(F32) + up.astype(F32)).astype(BF16)
            falling = (falling.astype(F32) + down.astype(F32)).astype(BF16)
        up = lax.ppermute(rising, "batch", [(i, i + 2) for i in range(2 * step)])
        down = lax.ppermute(
            falling, "batch", [(i, i - 2) for i in range(batch_parts - 2 * step, batch_parts)]
        )
    return pick(after(parts, *waits.get(line, ())), place, 0), up, down


def split_total_kernel(own_ref, up_ref, down_ref, *out_refs):
    total = own_ref[...].astype(F32) + up_ref[...].astype(F32) + down_ref[...].astype(F32)
    first = 0
    for out_ref in out_refs:
        size = out_ref.shape[1]
        out_ref[...] = total[:, first : first + size]
        first += size


def split_total(terms, sizes):
    rows = terms[0].shape[0]
    return pl.pallas_call(
        split_total_kernel,
        out_shape=[jax.ShapeDtypeStruct((rows, size), F32) for size in sizes],
        cost_estimate=pl.CostEstimate(flops=10**8, bytes_accessed=10**6, transcendentals=0),
        name="split_total",
    )(*terms)


def shards(
    tokens, seq_count, query_weight, key_weight, value_weight, out_weight,
    gate_weight, up_weight, down_weight, attention_gain, feedforward_gain, cotangent,
):
    seq_parts = lax.axis_size("seq")
    batch_parts = lax.axis_size("batch")
    part = lax.axis_index("seq")
    parity = lax.axis_index("batch") % 2
    rows = tokens.shape[1]
    group_rows = rows * seq_parts
    width = tokens.shape[2]

    order = jnp.arange(seq_parts, dtype=jnp.int32)
    swapped = ((order & 1) << 1) | (order >> 1)
    masks = jnp.where(parity == 0, order, swapped)
    owners = part ^ masks
    other = part ^ order
    spots = jnp.where(parity == 0, other, ((other & 1) << 1) | (other >> 1))
    seq_length = group_rows // seq_count[0]
    firsts = (owners * rows) // seq_length * seq_length // rows
    info = jnp.concatenate([owners, spots, firsts]).astype(jnp.int32)

    index = (owners[:, None] * rows + jnp.arange(rows, dtype=jnp.int32)[None, :]).reshape(-1)
    places = index - index // seq_length * seq_length
    lane = jnp.arange(128, dtype=jnp.int32)
    inverse = jnp.exp((lane % (HD // 2)).astype(F32) * (-2.0 * math.log(10000.0) / HD))
    angles = places.astype(F32)[:, None] * inverse[None, :]
    cosine = jnp.cos(angles)
    sine = jnp.sin(angles) * jnp.where(lane % HD < HD // 2, -1.0, 1.0)[None, :]

    inputs = tokens[0].astype(F32)
    scale_one = norm_scale(inputs)
    qkv_weight = jnp.concatenate([query_weight, key_weight, value_weight], axis=1)
    half = group_rows // 2

    def project(block, place, carried):
        return norm_project(block, attention_gain, qkv_weight, place, group_rows, carried)

    near = first_swap(tokens[0])
    side = second_swap(tokens[0])
    carried = project(tokens[0], 0, [])
    near, side, *carried = lax.optimization_barrier((near, side, *carried))
    far = second_swap(near)
    carried = project(side, 2, project(near, 1, carried))
    normed_one_rows, qkv = project(far, 3, carried)

    grad_ffn = after(cotangent[0], far)
    grad_near = first_swap(grad_ffn)
    grad_side = second_swap(grad_ffn)

    att_upper, query_upper, kv, lse_upper = attention_forward(info, qkv, cosine, sine, rows, seq_parts // 2, seq_parts // 2)
    branch_upper = mm(att_upper, out_weight).astype(BF16)
    arrived = second_swap(branch_upper)
    later_qkv, grad_near, grad_side = lax.optimization_barrier((after(qkv, branch_upper), grad_near, grad_side))
    grad_far = second_swap(grad_near)
    att_lower, query_lower, _, lse_lower = attention_forward(info, later_qkv, cosine, sine, rows, 0, seq_parts // 2)
    branch_lower = mm(att_lower, out_weight).astype(BF16)
    attended = jnp.concatenate([att_lower, att_upper], axis=0)
    query = jnp.concatenate([query_lower, query_upper], axis=0)
    lse = jnp.concatenate([lse_lower, lse_upper], axis=1)
    branch, passed = split_sum(branch_lower, after(arrived, branch_lower))
    passed = first_swap(after(passed, grad_far))
    grad_rows = jnp.concatenate([grad_near, grad_side, grad_far, cotangent[0]], axis=0)
    grad_mixed = mm_nt(grad_rows, down_weight)
    hidden = inputs + branch + after(passed, grad_mixed).astype(F32)

    scale_two = norm_scale(hidden)
    normed_two = (hidden * scale_two * feedforward_gain).astype(BF16)
    near = first_swap(normed_two)
    side = second_swap(normed_two)
    *carried, back_own = feed_forward([normed_two], grad_mixed, gate_weight, up_weight, 3 * rows, [])
    near, side, grad_rows, attended, query, lse, *carried = lax.optimization_barrier(
        (near, side, grad_rows, attended, query, lse, *carried)
    )
    far = second_swap(near)
    *carried, back_near, back_side = feed_forward([near, side], grad_mixed, gate_weight, up_weight, 0, carried)
    sum_side = second_swap(after(back_side, far))
    *carried, back_far = feed_forward([far], grad_mixed, gate_weight, up_weight, 2 * rows, carried)
    normed_two_rows, mixed, slopes = carried
    sum_far = second_swap(back_far)
    down_term = mm_tn(mixed, after(grad_rows, sum_side)).astype(BF16)
    near_sum = (back_near.astype(F32) + after(sum_far, down_term).astype(F32)).astype(BF16)
    passed = first_swap(near_sum)
    gate_up_term = weight_gradient(normed_two_rows, after(slopes, near_sum))
    grad_normed_two = back_own.astype(F32) + sum_side.astype(F32) + after(passed, gate_up_term).astype(F32)
    down_grad = over_batch(after(down_term, sum_far))
    gate_up_grad = over_batch(after(gate_up_term, passed))

    grad_out = cotangent[0].astype(F32)
    feed_gain_term, grad_hidden_norm = norm_backward(hidden, scale_two, feedforward_gain, grad_normed_two)
    grad_hidden = grad_out + grad_hidden_norm
    grad_branch = grad_hidden.astype(BF16)
    near = first_swap(grad_branch)
    side = second_swap(grad_branch)

    def attended_grad(block):
        return mm_nt(block, out_weight).astype(BF16)

    def backward(grad, first, count, carried):
        return attention_backward(
            info, query, attended, grad, lse, kv, cosine, sine, rows, first, count, carried
        )

    ffn_upper = mm(after(mixed, grad_branch)[rows : 3 * rows], down_weight).astype(BF16)
    carried = backward(after(attended_grad(grad_branch), ffn_upper), 0, 1, [])
    near, side, *carried = lax.optimization_barrier((near, side, *carried))
    far = second_swap(near)
    middle = attended_grad(jnp.concatenate([near, side], axis=0))
    carried = backward(middle, 1, 2, carried)
    far = after(far, *carried)
    ffn_arrived = second_swap(after(ffn_upper, far))
    grad_branch_rows = jnp.concatenate([grad_branch, near, side, far], axis=0)
    out_term = mm_tn(attended, grad_branch_rows).astype(BF16)
    grad_qkv, _, _, grad_kv = backward(attended_grad(after(far, out_term)), 3, 1, carried)
    grad_qkv = lax.dynamic_update_slice(grad_qkv, grad_kv, (0, grad_qkv.shape[1] - grad_kv.shape[1]))
    upper = mm_nt(after(grad_qkv, down_grad, ffn_arrived)[half:], qkv_weight).astype(BF16)
    arrived = second_swap(upper)
    lower = mm_nt(after(grad_qkv, upper)[:half], qkv_weight).astype(BF16)
    qkv_term = weight_gradient(normed_one_rows, after(grad_qkv, upper))
    kept, passed = split_sum(lower, after(arrived, qkv_term, lower))
    arrived_passed = first_swap(passed)
    later_mixed = after(mixed, upper)
    ffn_passed = mm(later_mixed[:rows], down_weight) + ffn_arrived[rows:].astype(F32)
    ffn_passed = first_swap(ffn_passed.astype(BF16))
    ffn_kept = mm(later_mixed[3 * rows :], down_weight) + ffn_arrived[:rows].astype(F32)
    grad_normed_one = kept + arrived_passed.astype(F32)
    attention_gain_term, grad_inputs_norm = norm_backward(inputs, scale_one, attention_gain, grad_normed_one)
    input_grad = grad_hidden + grad_inputs_norm
    layer_out = (hidden + ffn_kept + ffn_passed.astype(F32)).astype(BF16)

    devices = seq_parts * batch_parts
    gains = jnp.concatenate(
        [attention_gain_term.reshape(devices, -1), feed_gain_term.reshape(devices, -1)], axis=1
    )
    gains = jnp.sum(lax.all_to_all(gains, ("seq", "batch"), 0, 0, tiled=True), axis=0)
    share = width // devices
    query_width = query_weight.shape[1]
    key_width = key_weight.shape[1]
    line = batch_parts // 2
    out_terms = line_sum(out_term, {1: (qkv_term,), 2: (lower,), 3: (passed,)})
    out_grad = sum(term.astype(F32) for term in out_terms)
    qkv_terms = line_sum(qkv_term, {1: (lower,), 2: (passed,), 3: (arrived_passed,), line: (gains,)})
    query_grad, key_grad, value_grad = split_total(qkv_terms, (query_width, key_width, key_width))
    gate_up_grad = after(gate_up_grad, gains, query_grad, out_grad)
    hidden_width = gate_weight.shape[1]
    return (
        layer_out[None],
        input_grad[None],
        query_grad,
        key_grad,
        value_grad,
        out_grad,
        gate_up_grad[:, :hidden_width].astype(F32),
        gate_up_grad[:, hidden_width:].astype(F32),
        down_grad.astype(F32),
        gains[:share],
        gains[share:],
    )


def solution(mesh):
    return jax.shard_map(
        shards,
        mesh=mesh,
        in_specs=(
            P("batch", "seq", None),
            P("batch"),
            P(None, "seq"),
            P(None, "seq"),
            P(None, "seq"),
            P("seq", None),
            P(None, "seq"),
            P(None, "seq"),
            P("seq", None),
            P(),
            P(),
            P("batch", "seq", None),
        ),
        out_specs=(
            P("batch", "seq", None),
            P("batch", "seq", None),
            P("batch", "seq"),
            P("batch", "seq"),
            P("batch", "seq"),
            P(("seq", "batch"), None),
            P("batch", "seq"),
            P("batch", "seq"),
            P(("seq", "batch"), None),
            P(("seq", "batch")),
            P(("seq", "batch")),
        ),
        check_vma=False,
    )
```

```python
import functools
import math

import jax
import jax.numpy as jnp
from jax import lax
from jax.experimental import pallas as pl
from jax.experimental.pallas import tpu as pltpu
from jax.sharding import PartitionSpec as P

HD = 64
EPS = 1e-05
NEG = -1e30
F32 = jnp.float32
BF16 = jnp.bfloat16


def mm(a, b):
    return lax.dot_general(a, b, (((1,), (0,)), ((), ())), preferred_element_type=F32)


def mm_nt(a, b):
    return lax.dot_general(a, b, (((1,), (1,)), ((), ())), preferred_element_type=F32)


def mm_tn(a, b):
    return lax.dot_general(a, b, (((0,), (0,)), ((), ())), preferred_element_type=F32)


def exchange(values, even_mask, odd_mask):
    seq_parts = lax.axis_size("seq")
    batch_parts = lax.axis_size("batch")
    pairs = []
    for part in range(seq_parts):
        for group in range(batch_parts):
            mask = even_mask if group % 2 == 0 else odd_mask
            pairs.append((part * batch_parts + group, (part ^ mask) * batch_parts + group))
    return lax.ppermute(values, ("seq", "batch"), pairs)


def after(value, *others):
    return lax.optimization_barrier((value, *others))[0]


def first_swap(values):
    return exchange(values, 1, 2)


def second_swap(values):
    return exchange(values, 2, 1)


def split_sum(lower, arrived):
    rows = lower.shape[0] // 2
    total = lower.astype(F32) + arrived.astype(F32)
    return total[:rows], total[rows:].astype(BF16)


def norm_project_kernel(rows_ref, gain_ref, weight_ref, *refs):
    normed_ref, out_ref = refs[-2:]
    values = rows_ref[...].astype(F32)
    scale = lax.rsqrt(jnp.mean(values * values, axis=-1, keepdims=True) + EPS)
    normed_ref[...] = (values * scale * gain_ref[...]).astype(BF16)
    out_ref[...] = mm(normed_ref[...], weight_ref[...])


def norm_project(block, gain, weight, place, total, carried):
    rows, width = block.shape
    outputs = weight.shape[1]
    return pl.pallas_call(
        norm_project_kernel,
        grid=(1,),
        in_specs=[
            pl.BlockSpec((rows, width), lambda i: (0, 0)),
            pl.BlockSpec((1, width), lambda i: (0, 0)),
            pl.BlockSpec((width, outputs), lambda i: (0, 0)),
            *[pl.BlockSpec(memory_space=pl.ANY)] * len(carried),
        ],
        out_specs=[
            pl.BlockSpec((rows, width), lambda i: (place, 0)),
            pl.BlockSpec((rows, outputs), lambda i: (place, 0)),
        ],
        out_shape=[jax.ShapeDtypeStruct((total, width), BF16), jax.ShapeDtypeStruct((total, outputs), F32)],
        input_output_aliases={3 + i: i for i in range(len(carried))},
        cost_estimate=pl.CostEstimate(flops=10**9, bytes_accessed=10**6, transcendentals=0),
        name="norm_project",
    )(block, gain[None], weight, *carried)


def swap_halves(values):
    lane = lax.broadcasted_iota(jnp.int32, values.shape, 1)
    ahead = pltpu.roll(values, values.shape[1] - HD // 2, 1)
    behind = pltpu.roll(values, HD // 2, 1)
    return jnp.where(lane % HD < HD // 2, ahead, behind)


def padded_keys(keys_values):
    lane = lax.broadcasted_iota(jnp.int32, keys_values.shape, 1)
    zero = jnp.zeros_like(keys_values)
    left = jnp.where(lane < HD, keys_values, zero)
    right = pltpu.roll(left, HD, 1)
    return jnp.concatenate([left, right], axis=0)


def padded_values(keys_values):
    lane = lax.broadcasted_iota(jnp.int32, keys_values.shape, 1)
    zero = jnp.zeros_like(keys_values)
    right = jnp.where(lane >= HD, keys_values, zero)
    left = pltpu.roll(right, HD, 1)
    return jnp.concatenate([left, right], axis=0)


def attention_forward_kernel(
    first, info, query_ref, kv_ref, cos_ref, sin_ref, cos_all, sin_all,
    attended_ref, rotated_ref, kv_out, lse_ref, keys_s, values_s, acc_s, max_s,
):
    step = pl.program_id(0) + first
    rows = query_ref.shape[0]
    pairs = query_ref.shape[1] // 128
    blocks = kv_ref.shape[0] // rows

    @pl.when(step == first)
    def _():
        for part in range(blocks):
            here = pl.ds(part * rows, rows)
            kv = kv_ref[here, :]
            lane = lax.broadcasted_iota(jnp.int32, kv.shape, 1)
            turned = kv * cos_all[here, :] + swap_halves(kv) * sin_all[here, :]
            kv = jnp.where(lane < HD, turned, kv).astype(BF16).astype(F32)
            kv_out[here, :] = kv.astype(BF16)
            keys_s[part] = (padded_keys(kv) * (1.0 / math.sqrt(HD))).astype(BF16)
            both = jnp.transpose(padded_values(kv))
            feature = lax.broadcasted_iota(jnp.int32, both.shape, 0)
            key = lax.broadcasted_iota(jnp.int32, both.shape, 1)
            ones = jnp.where((feature < HD) == (key < rows), 1.0, 0.0)
            values_s[part] = jnp.concatenate([both, ones], axis=0).astype(BF16)

    own = info[step]
    low = info[2 * blocks + step]
    key_index = lax.broadcasted_iota(jnp.int32, (2 * rows, rows), 0) % rows
    query_index = lax.broadcasted_iota(jnp.int32, (2 * rows, rows), 1)
    allowed = key_index <= query_index
    at = info[blocks + own]

    def spread(upper, lower, height):
        return jnp.concatenate(
            [jnp.broadcast_to(upper, (height, rows)), jnp.broadcast_to(lower, (height, rows))], axis=0
        )

    for pair in range(pairs):
        cols = pl.ds(pair * 128, 128)
        query = query_ref[:, cols]
        query = (query * cos_ref[...] + swap_halves(query) * sin_ref[...]).astype(BF16)
        rotated_ref[:, cols] = query
        scores = jnp.where(allowed, mm_nt(keys_s[at], query), NEG)
        tops = [jnp.max(scores[i * rows : (i + 1) * rows], axis=0, keepdims=True) for i in range(2)]
        probs = jnp.exp(scores - spread(*tops, rows)).astype(BF16)
        for i in range(2):
            max_s[2 * pair + i : 2 * pair + i + 1, :] = tops[i]
        acc_s[pair] = mm(values_s[at], probs)

    for back in range(1, blocks):

        @pl.when(own - back >= low)
        def _():
            there = info[blocks + jnp.maximum(own - back, 0)]
            for pair in range(pairs):
                query = rotated_ref[:, pl.ds(pair * 128, 128)]
                scores = mm_nt(keys_s[there], query)
                tops, scales = [], []
                for i in range(2):
                    before = max_s[2 * pair + i : 2 * pair + i + 1, :]
                    top = jnp.maximum(
                        before, jnp.max(scores[i * rows : (i + 1) * rows], axis=0, keepdims=True)
                    )
                    tops.append(top)
                    scales.append(jnp.exp(before - top))
                    max_s[2 * pair + i : 2 * pair + i + 1, :] = top
                probs = jnp.exp(scores - spread(*tops, rows)).astype(BF16)
                factor = spread(*scales, HD)
                factor = jnp.concatenate([factor, factor], axis=0)
                acc_s[pair] = acc_s[pair] * factor + mm(values_s[there], probs)

    for pair in range(pairs):
        total = acc_s[pair][128:, :]
        result = acc_s[pair][:128, :] / total
        attended_ref[:, pl.ds(pair * 128, 128)] = jnp.transpose(result).astype(BF16)
        for i in range(2):
            spot = slice(2 * pair + i, 2 * pair + i + 1)
            lse_ref[spot, :] = max_s[spot, :] + jnp.log(total[i * HD : i * HD + 1, :])


def attention_forward(info, qkv, cosine, sine, rows, first, count):
    total, width = qkv.shape
    blocks = total // rows
    query_width = width - 2 * HD
    pairs = query_width // 128
    last = query_width // 128
    return pl.pallas_call(
        functools.partial(attention_forward_kernel, first),
        grid_spec=pltpu.PrefetchScalarGridSpec(
            num_scalar_prefetch=1,
            grid=(count,),
            in_specs=[
                pl.BlockSpec((rows, query_width), lambda j, info: (j + first, 0)),
                pl.BlockSpec((total, 128), lambda j, info: (0, last)),
                pl.BlockSpec((rows, 128), lambda j, info: (j + first, 0)),
                pl.BlockSpec((rows, 128), lambda j, info: (j + first, 0)),
                pl.BlockSpec((total, 128), lambda j, info: (0, 0)),
                pl.BlockSpec((total, 128), lambda j, info: (0, 0)),
            ],
            out_specs=[
                pl.BlockSpec((rows, query_width), lambda j, info: (j, 0)),
                pl.BlockSpec((rows, query_width), lambda j, info: (j, 0)),
                pl.BlockSpec((total, 128), lambda j, info: (0, 0)),
                pl.BlockSpec((2 * pairs, rows), lambda j, info: (0, j)),
            ],
            scratch_shapes=[
                pltpu.VMEM((blocks, 2 * rows, 128), BF16),
                pltpu.VMEM((blocks, 256, 2 * rows), BF16),
                pltpu.VMEM((pairs, 256, rows), F32),
                pltpu.VMEM((2 * pairs, rows), F32),
            ],
        ),
        cost_estimate=pl.CostEstimate(flops=count * 4 * 10**9, bytes_accessed=count * 10**6, transcendentals=0),
        out_shape=[
            jax.ShapeDtypeStruct((count * rows, query_width), BF16),
            jax.ShapeDtypeStruct((count * rows, query_width), BF16),
            jax.ShapeDtypeStruct((total, 128), BF16),
            jax.ShapeDtypeStruct((2 * pairs, count * rows), F32),
        ],
        name="attention_forward",
    )(info, qkv, qkv, cosine, sine, cosine, sine)


def attention_backward_kernel(
    first, final, info, query_ref, att_ref, grad_ref, lse_ref, kv_ref, cos_ref, sin_ref, cos_all, sin_all, *refs
):
    if first:
        refs = refs[1:]
        key_in, value_in = refs[:2]
        refs = refs[2:]
    else:
        key_in = value_in = None
    out_ref, key_acc, value_acc = refs[:3]
    refs = refs[3:]
    if final:
        kv_out = refs[0]
        refs = refs[1:]
    keys_s, values_s, query_acc, delta_s = refs
    step = pl.program_id(0) + first
    rows = query_ref.shape[0]
    query_width = query_ref.shape[1]
    pairs = query_width // 128
    blocks = kv_ref.shape[0] // rows

    @pl.when(step == first)
    def _():
        for part in range(blocks):
            kv = kv_ref[pl.ds(part * rows, rows), :].astype(F32)
            keys_s[part] = (padded_keys(kv) * (1.0 / math.sqrt(HD))).astype(BF16)
            values_s[part] = padded_values(kv).astype(BF16)
        if first:
            key_acc[...] = key_in[...]
            value_acc[...] = value_in[...]
        else:
            key_acc[...] = jnp.zeros_like(key_acc)
            value_acc[...] = jnp.zeros_like(value_acc)

    own = info[step]
    low = info[2 * blocks + step]
    at = info[blocks + own]
    key_index = lax.broadcasted_iota(jnp.int32, (2 * rows, rows), 0) % rows
    query_index = lax.broadcasted_iota(jnp.int32, (2 * rows, rows), 1)
    allowed = key_index <= query_index
    top_half = lax.broadcasted_iota(jnp.int32, (2 * rows, rows), 0) < rows

    products = att_ref[...].astype(F32) * grad_ref[...].astype(F32)
    head_row = lax.broadcasted_iota(jnp.int32, (2 * pairs, query_width), 0)
    head_col = lax.broadcasted_iota(jnp.int32, (2 * pairs, query_width), 1) // HD
    picker = jnp.where(head_row == head_col, 1.0, 0.0)
    delta_s[...] = lax.dot_general(
        picker, products, (((1,), (1,)), ((), ())),
        precision=lax.Precision.HIGHEST, preferred_element_type=F32,
    )

    def one_block(where_, masked):
        keys = keys_s[where_]
        values = values_s[where_]
        for pair in range(pairs):
            cols = pl.ds(pair * 128, 128)
            query = query_ref[:, cols]
            grad = grad_ref[:, cols]
            lse = jnp.where(
                top_half, lse_ref[2 * pair : 2 * pair + 1, :], lse_ref[2 * pair + 1 : 2 * pair + 2, :]
            )
            delta = jnp.where(
                top_half, delta_s[2 * pair : 2 * pair + 1, :], delta_s[2 * pair + 1 : 2 * pair + 2, :]
            )
            scores = mm_nt(keys, query) - lse
            if masked:
                scores = jnp.where(allowed, scores, NEG)
            probs = jnp.exp(scores)
            grad_probs = mm_nt(values, grad)
            grad_scores = (probs * (grad_probs - delta)).astype(BF16)
            value_acc[where_] += mm(probs.astype(BF16), grad)
            key_acc[where_] += mm(grad_scores, query)
            part = mm_tn(grad_scores, keys)
            if masked:
                query_acc[:, cols] = part
            else:
                query_acc[:, cols] += part

    one_block(at, True)
    for back in range(1, blocks):

        @pl.when(own - back >= low)
        def _():
            one_block(info[blocks + jnp.maximum(own - back, 0)], False)

    for pair in range(pairs):
        cols = pl.ds(pair * 128, 128)
        grad = query_acc[:, cols].astype(BF16).astype(F32)
        out_ref[:, cols] = (grad * cos_ref[...] - swap_halves(grad) * sin_ref[...]).astype(BF16)

    if final:

        @pl.when(step == first + pl.num_programs(0) - 1)
        def _():
            lane = lax.broadcasted_iota(jnp.int32, (rows, 128), 1)
            for part in range(blocks):
                spot = pl.ds(part * rows, rows)
                key_grad = key_acc[part]
                key_grad = key_grad[:rows] + pltpu.roll(key_grad[rows:], HD, 1)
                key_grad = (key_grad * (1.0 / math.sqrt(HD))).astype(BF16).astype(F32)
                value_grad = value_acc[part]
                value_grad = pltpu.roll(value_grad[:rows], HD, 1) + value_grad[rows:]
                turned = key_grad * cos_all[spot, :] - swap_halves(key_grad) * sin_all[spot, :]
                kv_out[spot, :] = jnp.where(lane < HD, turned, value_grad).astype(BF16)


def attention_backward(info, query, attended, grad, lse, kv, cosine, sine, rows, first, count, carried):
    total, query_width = query.shape
    blocks = total // rows
    pairs = query_width // 128
    final = first + count == blocks
    row_block = pl.BlockSpec((rows, query_width), lambda j, info: (j + first, 0))
    table_block = pl.BlockSpec((rows, 128), lambda j, info: (j + first, 0))
    whole = pl.BlockSpec((total, 128), lambda j, info: (0, 0))
    sums = pl.BlockSpec((blocks, 2 * rows, 128), lambda j, info: (0, 0, 0))
    sums_shape = jax.ShapeDtypeStruct((blocks, 2 * rows, 128), F32)
    in_specs = [
        row_block, row_block,
        pl.BlockSpec((rows, query_width), lambda j, info: (j, 0)),
        pl.BlockSpec((2 * pairs, rows), lambda j, info: (0, j + first)),
        whole, table_block, table_block, whole, whole,
    ]
    operands = [info, query, attended, grad, lse, kv, cosine, sine, cosine, sine]
    aliases = {}
    if first:
        aliases = {len(operands): 0, len(operands) + 1: 1, len(operands) + 2: 2}
        operands += carried
        in_specs += [pl.BlockSpec(memory_space=pl.ANY), sums, sums]
    out_specs = [row_block, sums, sums]
    out_shape = [jax.ShapeDtypeStruct((total, query_width + 128), BF16), sums_shape, sums_shape]
    if final:
        out_specs.append(whole)
        out_shape.append(jax.ShapeDtypeStruct((total, 128), BF16))
    return pl.pallas_call(
        functools.partial(attention_backward_kernel, first, final),
        grid_spec=pltpu.PrefetchScalarGridSpec(
            num_scalar_prefetch=1,
            grid=(count,),
            in_specs=in_specs,
            out_specs=out_specs,
            scratch_shapes=[
                pltpu.VMEM((blocks, 2 * rows, 128), BF16),
                pltpu.VMEM((blocks, 2 * rows, 128), BF16),
                pltpu.VMEM((rows, query_width), F32),
                pltpu.VMEM((2 * pairs, rows), F32),
            ],
        ),
        out_shape=out_shape,
        input_output_aliases=aliases,
        cost_estimate=pl.CostEstimate(flops=count * 6 * 10**9, bytes_accessed=count * 10**6, transcendentals=0),
        name="attention_backward",
    )(*operands)


def feed_forward_kernel(parts, first_row, *refs):
    values_refs = refs[:parts]
    cotangent_refs = refs[parts : 2 * parts]
    grad_ref, gate_all, up_all = refs[2 * parts : 2 * parts + 3]
    back_refs = refs[-7 - parts : -7]
    rows_all, mixed_all, slopes_all, cotangents_all = refs[-11 - parts : -7 - parts]
    gate_w, up_w, rows_s, mixed_s, slopes_s, arrived, stored = refs[-7:]
    rows, width = values_refs[0].shape
    hidden = gate_w.shape[1]
    step = min(256, hidden)
    count, rest = divmod(hidden, step)

    def weight_copies(index, first, size):
        cols = pl.ds(first, size)
        return (
            pltpu.make_async_copy(gate_all.at[:, cols], gate_w.at[:, cols], arrived.at[0, index]),
            pltpu.make_async_copy(up_all.at[:, cols], up_w.at[:, cols], arrived.at[1, index]),
        )

    for index in range(count + (rest > 0)):
        for copy in weight_copies(index, index * step, step if index < count else rest):
            copy.start()
    for i in range(parts):
        rows_s[pl.ds(i * rows, rows), :] = values_refs[i][...]
    here = pl.ds(first_row, parts * rows)
    outs = [
        pltpu.make_async_copy(scratch, whole.at[here, :], stored.at[i])
        for i, (scratch, whole) in enumerate(((rows_s, rows_all), (mixed_s, mixed_all), (slopes_s, slopes_all)))
    ]
    outs[0].start()
    moves = [
        pltpu.make_async_copy(
            cotangent_refs[i], cotangents_all.at[pl.ds(first_row + i * rows, rows), :], stored.at[3 + i]
        )
        for i in range(parts)
    ]
    for copy in moves:
        copy.start()

    def columns(index, first, size):
        for copy in weight_copies(index, first, size):
            copy.wait()
        cols = pl.ds(first, size)
        values = rows_s[...]
        gate = mm(values, gate_w[:, cols])
        upward = mm(values, up_w[:, cols])
        grad = grad_ref[:, cols]
        sigma = 1.0 / (1.0 + jnp.exp(-gate))
        activated = gate * sigma
        mixed_s[:, cols] = (activated * upward).astype(BF16)
        slopes_s[:, cols] = (grad * upward * sigma * (1.0 + gate * (1.0 - sigma))).astype(BF16)
        slopes_s[:, pl.ds(hidden + first, size)] = (grad * activated).astype(BF16)

    @pl.loop(0, count)
    def _(index):
        columns(index, pl.multiple_of(index * step, 128), step)

    if rest:
        columns(count, hidden - rest, rest)
    outs[1].start()
    outs[2].start()

    part = min(256, width)

    @pl.loop(0, width // part)
    def _(index):
        here = pl.ds(pl.multiple_of(index * part, part), part)
        result = mm_nt(slopes_s[:, :hidden], gate_w[here, :]) + mm_nt(slopes_s[:, hidden:], up_w[here, :])
        for i in range(parts):
            back_refs[i][:, here] = result[i * rows : (i + 1) * rows].astype(BF16)

    for copy in outs + moves:
        copy.wait()


def feed_forward(values, cotangents, grad_mixed, grad_first, gate_weight, up_weight, first, total, carried):
    parts = len(values)
    rows, width = values[0].shape
    hidden = grad_mixed.shape[1]
    size = parts * rows
    block = grad_first // size
    anywhere = pl.BlockSpec(memory_space=pl.ANY)
    operands = [*values, *cotangents, grad_mixed, gate_weight, up_weight, *carried]
    single = pl.BlockSpec((rows, width), lambda i: (0, 0))
    here = pl.BlockSpec((size, hidden), lambda i: (block, 0))
    return pl.pallas_call(
        functools.partial(feed_forward_kernel, parts, first),
        grid=(1,),
        in_specs=[*[single] * (2 * parts), here, *[anywhere] * (2 + len(carried))],
        out_specs=[*[anywhere] * 4, *[single] * parts],
        scratch_shapes=[
            pltpu.VMEM((width, hidden), BF16),
            pltpu.VMEM((width, hidden), BF16),
            pltpu.VMEM((size, width), BF16),
            pltpu.VMEM((size, hidden), BF16),
            pltpu.VMEM((size, 2 * hidden), BF16),
            pltpu.SemaphoreType.DMA((2, -(-hidden // 256))),
            pltpu.SemaphoreType.DMA((3 + parts,)),
        ],
        out_shape=[
            jax.ShapeDtypeStruct((total, width), BF16),
            jax.ShapeDtypeStruct((total, hidden), BF16),
            jax.ShapeDtypeStruct((total, 2 * hidden), BF16),
            jax.ShapeDtypeStruct((total, width), BF16),
            *[jax.ShapeDtypeStruct((rows, width), BF16)] * parts,
        ],
        input_output_aliases={2 * parts + 3 + i: i for i in range(len(carried))},
        cost_estimate=pl.CostEstimate(flops=parts * 6 * 10**9, bytes_accessed=10**6, transcendentals=0),
        name="feed_forward",
    )(*operands)


def weight_gradient_kernel(values_ref, grad_ref, out_ref):
    out_ref[...] = mm_tn(values_ref[...], grad_ref[...]).astype(BF16)


def weight_gradient(values, grad):
    total, features = values.shape
    outputs = grad.shape[1]
    tile = math.gcd(512, features)
    return pl.pallas_call(
        weight_gradient_kernel,
        grid=(features // tile,),
        in_specs=[
            pl.BlockSpec((total, tile), lambda i: (0, i)),
            pl.BlockSpec((total, outputs), lambda i: (0, 0)),
        ],
        out_specs=pl.BlockSpec((tile, outputs), lambda i: (i, 0)),
        out_shape=jax.ShapeDtypeStruct((features, outputs), BF16),
        cost_estimate=pl.CostEstimate(
            flops=2 * total * features * outputs, bytes_accessed=10**6, transcendentals=0
        ),
        name="weight_gradient",
    )(values, grad)


def norm_scale(values):
    return lax.rsqrt(jnp.mean(values * values, axis=-1, keepdims=True) + EPS)


def norm_backward(values, scale, gain, grads):
    weighted = grads * gain
    gain_grad = jnp.sum(grads * values * scale, axis=0)
    cubed = scale * scale * scale
    value_grad = scale * weighted - values * cubed * jnp.mean(weighted * values, axis=-1, keepdims=True)
    return gain_grad, value_grad


def second_norm_backward_kernel(
    hidden_ref, gain_ref, cotangent_ref, first_ref, second_ref, third_ref, grad_ref, branch_ref, gain_grad_ref
):
    step = pl.program_id(0)
    values = hidden_ref[...]
    grads = first_ref[...].astype(F32) + second_ref[...].astype(F32) + third_ref[...].astype(F32)
    scale = lax.rsqrt(jnp.mean(values * values, axis=-1, keepdims=True) + EPS)
    weighted = grads * gain_ref[...]
    scaled = values * scale
    share = jnp.mean(weighted * values, axis=-1, keepdims=True) * (scale * scale)
    grad = cotangent_ref[...].astype(F32) + scale * weighted - scaled * share
    grad_ref[...] = grad
    branch_ref[...] = grad.astype(BF16)
    part = jnp.sum(grads * scaled, axis=0, keepdims=True)

    @pl.when(step == 0)
    def _():
        gain_grad_ref[...] = part

    @pl.when(step > 0)
    def _():
        gain_grad_ref[...] += part


def second_norm_backward(hidden, gain, cotangent, terms):
    rows, width = hidden.shape
    tile = math.gcd(64, rows)
    block = pl.BlockSpec((tile, width), lambda i: (i, 0))
    whole = pl.BlockSpec((1, width), lambda i: (0, 0))
    grad, branch, gain_grad = pl.pallas_call(
        second_norm_backward_kernel,
        grid=(rows // tile,),
        in_specs=[block, whole, *[block] * 4],
        out_specs=[block, block, whole],
        out_shape=[
            jax.ShapeDtypeStruct((rows, width), F32),
            jax.ShapeDtypeStruct((rows, width), BF16),
            jax.ShapeDtypeStruct((1, width), F32),
        ],
        cost_estimate=pl.CostEstimate(flops=10**9, bytes_accessed=10**6, transcendentals=0),
        name="second_norm_backward",
    )(hidden, gain[None], cotangent, *terms)
    return grad, branch, gain_grad[0]


def over_batch(term):
    return lax.psum_scatter(term, "batch", scatter_dimension=0, tiled=True)


def pick(parts, index, axis):
    return lax.dynamic_index_in_dim(parts, index, axis, keepdims=False)


def line_sum(term, waits):
    batch_parts = lax.axis_size("batch")
    line = batch_parts // 2
    index = lax.axis_index("batch")
    core, place = index % 2, index // 2
    parts = term.reshape(line, 2, term.shape[0] // batch_parts, term.shape[1])
    swap = [(i, i ^ 1) for i in range(batch_parts)]
    arrived = lax.ppermute(pick(parts, 1 - core, 1), "batch", swap)
    parts = (pick(parts, core, 1).astype(F32) + arrived.astype(F32)).astype(BF16)
    up = down = None
    for step in range(1, line):
        parts, up, down = lax.optimization_barrier((parts, up, down, *waits.get(step, ())))[:3]
        rising = pick(parts, jnp.minimum(place + line - step, line - 1), 0)
        falling = pick(parts, jnp.maximum(place - line + step, 0), 0)
        if up is not None:
            rising = (rising.astype(F32) + up.astype(F32)).astype(BF16)
            falling = (falling.astype(F32) + down.astype(F32)).astype(BF16)
        up = lax.ppermute(rising, "batch", [(i, i + 2) for i in range(2 * step)])
        down = lax.ppermute(
            falling, "batch", [(i, i - 2) for i in range(batch_parts - 2 * step, batch_parts)]
        )
    return pick(after(parts, *waits.get(line, ())), place, 0), up, down


def split_total_kernel(own_ref, up_ref, down_ref, *out_refs):
    total = own_ref[...].astype(F32) + up_ref[...].astype(F32) + down_ref[...].astype(F32)
    first = 0
    for out_ref in out_refs:
        size = out_ref.shape[1]
        out_ref[...] = total[:, first : first + size]
        first += size


def split_total(terms, sizes):
    rows = terms[0].shape[0]
    return pl.pallas_call(
        split_total_kernel,
        out_shape=[jax.ShapeDtypeStruct((rows, size), F32) for size in sizes],
        cost_estimate=pl.CostEstimate(flops=10**8, bytes_accessed=10**6, transcendentals=0),
        name="split_total",
    )(*terms)


def shards(
    tokens, seq_count, query_weight, key_weight, value_weight, out_weight,
    gate_weight, up_weight, down_weight, attention_gain, feedforward_gain, cotangent,
):
    seq_parts = lax.axis_size("seq")
    batch_parts = lax.axis_size("batch")
    part = lax.axis_index("seq")
    parity = lax.axis_index("batch") % 2
    rows = tokens.shape[1]
    group_rows = rows * seq_parts
    width = tokens.shape[2]

    order = jnp.arange(seq_parts, dtype=jnp.int32)
    swapped = ((order & 1) << 1) | (order >> 1)
    masks = jnp.where(parity == 0, order, swapped)
    owners = part ^ masks
    other = part ^ order
    spots = jnp.where(parity == 0, other, ((other & 1) << 1) | (other >> 1))
    seq_length = group_rows // seq_count[0]
    firsts = (owners * rows) // seq_length * seq_length // rows
    info = jnp.concatenate([owners, spots, firsts]).astype(jnp.int32)

    index = (owners[:, None] * rows + jnp.arange(rows, dtype=jnp.int32)[None, :]).reshape(-1)
    places = index - index // seq_length * seq_length
    lane = jnp.arange(128, dtype=jnp.int32)
    inverse = jnp.exp((lane % (HD // 2)).astype(F32) * (-2.0 * math.log(10000.0) / HD))
    angles = places.astype(F32)[:, None] * inverse[None, :]
    cosine = jnp.cos(angles)
    sine = jnp.sin(angles) * jnp.where(lane % HD < HD // 2, -1.0, 1.0)[None, :]

    inputs = tokens[0].astype(F32)
    scale_one = norm_scale(inputs)
    qkv_weight = jnp.concatenate([query_weight, key_weight, value_weight], axis=1)
    half = group_rows // 2

    def project(block, place, carried):
        return norm_project(block, attention_gain, qkv_weight, place, group_rows, carried)

    near = first_swap(tokens[0])
    side = second_swap(tokens[0])
    carried = project(tokens[0], 0, [])
    near, side, *carried = lax.optimization_barrier((near, side, *carried))
    far = second_swap(near)
    carried = project(side, 2, project(near, 1, carried))
    normed_one_rows, qkv = project(far, 3, carried)

    grad_ffn = after(cotangent[0], far)
    grad_near = first_swap(grad_ffn)
    grad_side = second_swap(grad_ffn)

    att_upper, query_upper, kv, lse_upper = attention_forward(info, qkv, cosine, sine, rows, seq_parts // 2, seq_parts // 2)
    branch_upper = mm(att_upper, out_weight).astype(BF16)
    arrived = second_swap(branch_upper)
    later_qkv, grad_near, grad_side = lax.optimization_barrier((after(qkv, branch_upper), grad_near, grad_side))
    att_lower, query_lower, _, lse_lower = attention_forward(info, later_qkv, cosine, sine, rows, 0, seq_parts // 2)
    branch_lower = mm(att_lower, out_weight).astype(BF16)
    attended = jnp.concatenate([att_lower, att_upper], axis=0)
    query = jnp.concatenate([query_lower, query_upper], axis=0)
    lse = jnp.concatenate([lse_lower, lse_upper], axis=1)
    branch, passed = split_sum(branch_lower, after(arrived, branch_lower))
    passed = first_swap(passed)
    grad_mixed = mm_nt(jnp.concatenate([grad_near, grad_side, cotangent[0]], axis=0), down_weight)
    hidden = inputs + branch + after(passed, grad_mixed).astype(F32)

    scale_two = norm_scale(hidden)
    normed_two = (hidden * scale_two * feedforward_gain).astype(BF16)
    near = first_swap(normed_two)
    side = second_swap(normed_two)

    def feed(values, cotangents, grads, grad_first, first, carried):
        return feed_forward(
            values, cotangents, grads, grad_first, gate_weight, up_weight, first, group_rows, carried
        )

    *carried, back_own = feed([normed_two], [cotangent[0]], grad_mixed, 2 * rows, 3 * rows, [])
    near, side, grad_near, attended, query, lse, *carried = lax.optimization_barrier(
        (near, side, grad_near, attended, query, lse, *carried)
    )
    far = second_swap(near)
    grad_far = second_swap(grad_near)
    *carried, back_near, back_side = feed([near, side], [grad_near, grad_side], grad_mixed, 0, 0, carried)
    sum_side = second_swap(after(back_side, far))
    grad_mixed_far = mm_nt(after(grad_far, back_side), down_weight)
    *carried, back_far = feed([far], [grad_far], grad_mixed_far, 0, 2 * rows, carried)
    normed_two_rows, mixed, slopes, grad_rows = carried
    sum_far = second_swap(back_far)
    down_term = mm_tn(mixed, after(grad_rows, sum_side)).astype(BF16)
    near_sum = (back_near.astype(F32) + after(sum_far, down_term).astype(F32)).astype(BF16)
    passed = first_swap(near_sum)
    gate_up_term = weight_gradient(normed_two_rows, after(slopes, near_sum))
    down_grad = over_batch(after(down_term, sum_far))
    gate_up_grad = over_batch(after(gate_up_term, passed))

    grad_hidden, grad_branch, feed_gain_term = second_norm_backward(
        hidden, feedforward_gain, cotangent[0], (back_own, sum_side, after(passed, gate_up_term))
    )
    near = first_swap(grad_branch)
    side = second_swap(grad_branch)

    def attended_grad(block):
        return mm_nt(block, out_weight).astype(BF16)

    def backward(grad, first, count, carried):
        return attention_backward(
            info, query, attended, grad, lse, kv, cosine, sine, rows, first, count, carried
        )

    ffn_upper = mm(after(mixed, grad_branch)[rows : 3 * rows], down_weight).astype(BF16)
    carried = backward(after(attended_grad(grad_branch), ffn_upper), 0, 1, [])
    near, side, *carried = lax.optimization_barrier((near, side, *carried))
    far = second_swap(near)
    middle = attended_grad(jnp.concatenate([near, side], axis=0))
    carried = backward(middle, 1, 2, carried)
    far = after(far, *carried)
    ffn_arrived = second_swap(after(ffn_upper, far))
    grad_branch_rows = jnp.concatenate([grad_branch, near, side, far], axis=0)
    out_term = mm_tn(attended, grad_branch_rows).astype(BF16)
    grad_qkv, _, _, grad_kv = backward(attended_grad(after(far, out_term)), 3, 1, carried)
    grad_qkv = lax.dynamic_update_slice(grad_qkv, grad_kv, (0, grad_qkv.shape[1] - grad_kv.shape[1]))
    upper = mm_nt(after(grad_qkv, down_grad, ffn_arrived)[half:], qkv_weight).astype(BF16)
    arrived = second_swap(upper)
    lower = mm_nt(after(grad_qkv, upper)[:half], qkv_weight).astype(BF16)
    qkv_term = weight_gradient(normed_one_rows, after(grad_qkv, upper))
    kept, passed = split_sum(lower, after(arrived, qkv_term, lower))
    arrived_passed = first_swap(passed)
    later_mixed = after(mixed, upper)
    ffn_passed = mm(later_mixed[:rows], down_weight) + ffn_arrived[rows:].astype(F32)
    ffn_passed = first_swap(ffn_passed.astype(BF16))
    ffn_kept = mm(later_mixed[3 * rows :], down_weight) + ffn_arrived[:rows].astype(F32)
    grad_normed_one = kept + arrived_passed.astype(F32)
    attention_gain_term, grad_inputs_norm = norm_backward(inputs, scale_one, attention_gain, grad_normed_one)
    input_grad = grad_hidden + grad_inputs_norm
    layer_out = (hidden + ffn_kept + ffn_passed.astype(F32)).astype(BF16)

    devices = seq_parts * batch_parts
    gains = jnp.concatenate(
        [attention_gain_term.reshape(devices, -1), feed_gain_term.reshape(devices, -1)], axis=1
    )
    gains = jnp.sum(lax.all_to_all(gains, ("seq", "batch"), 0, 0, tiled=True), axis=0)
    share = width // devices
    query_width = query_weight.shape[1]
    key_width = key_weight.shape[1]
    line = batch_parts // 2
    out_terms = line_sum(out_term, {1: (qkv_term,), 2: (lower,), 3: (passed,)})
    out_grad = sum(term.astype(F32) for term in out_terms)
    qkv_terms = line_sum(qkv_term, {1: (lower,), 2: (passed,), 3: (arrived_passed,), line: (gains,)})
    query_grad, key_grad, value_grad = split_total(qkv_terms, (query_width, key_width, key_width))
    gate_up_grad = after(gate_up_grad, gains, query_grad, out_grad)
    hidden_width = gate_weight.shape[1]
    return (
        layer_out[None],
        input_grad[None],
        query_grad,
        key_grad,
        value_grad,
        out_grad,
        gate_up_grad[:, :hidden_width].astype(F32),
        gate_up_grad[:, hidden_width:].astype(F32),
        down_grad.astype(F32),
        gains[:share],
        gains[share:],
    )


def solution(mesh):
    return jax.shard_map(
        shards,
        mesh=mesh,
        in_specs=(
            P("batch", "seq", None),
            P("batch"),
            P(None, "seq"),
            P(None, "seq"),
            P(None, "seq"),
            P("seq", None),
            P(None, "seq"),
            P(None, "seq"),
            P("seq", None),
            P(),
            P(),
            P("batch", "seq", None),
        ),
        out_specs=(
            P("batch", "seq", None),
            P("batch", "seq", None),
            P("batch", "seq"),
            P("batch", "seq"),
            P("batch", "seq"),
            P(("seq", "batch"), None),
            P("batch", "seq"),
            P("batch", "seq"),
            P(("seq", "batch"), None),
            P(("seq", "batch")),
            P(("seq", "batch")),
        ),
        check_vma=False,
    )
```

```python
import functools
import math

import jax
import jax.numpy as jnp
from jax import lax
from jax.experimental import pallas as pl
from jax.experimental.pallas import tpu as pltpu
from jax.sharding import PartitionSpec as P

HD = 64
EPS = 1e-05
NEG = -1e30
F32 = jnp.float32
BF16 = jnp.bfloat16


def mm(a, b):
    return lax.dot_general(a, b, (((1,), (0,)), ((), ())), preferred_element_type=F32)


def mm_nt(a, b):
    return lax.dot_general(a, b, (((1,), (1,)), ((), ())), preferred_element_type=F32)


def mm_tn(a, b):
    return lax.dot_general(a, b, (((0,), (0,)), ((), ())), preferred_element_type=F32)


def exchange(values, even_mask, odd_mask):
    seq_parts = lax.axis_size("seq")
    batch_parts = lax.axis_size("batch")
    pairs = []
    for part in range(seq_parts):
        for group in range(batch_parts):
            mask = even_mask if group % 2 == 0 else odd_mask
            pairs.append((part * batch_parts + group, (part ^ mask) * batch_parts + group))
    return lax.ppermute(values, ("seq", "batch"), pairs)


def after(value, *others):
    return lax.optimization_barrier((value, *others))[0]


def first_swap(values):
    return exchange(values, 1, 2)


def second_swap(values):
    return exchange(values, 2, 1)


def split_sum(lower, arrived):
    rows = lower.shape[0] // 2
    total = lower.astype(F32) + arrived.astype(F32)
    return total[:rows], total[rows:].astype(BF16)


def norm_project_kernel(rows_ref, gain_ref, weight_ref, *refs):
    normed_ref, out_ref = refs[-2:]
    values = rows_ref[...].astype(F32)
    scale = lax.rsqrt(jnp.mean(values * values, axis=-1, keepdims=True) + EPS)
    normed_ref[...] = (values * scale * gain_ref[...]).astype(BF16)
    out_ref[...] = mm(normed_ref[...], weight_ref[...])


def norm_project(block, gain, weight, place, total, carried):
    rows, width = block.shape
    outputs = weight.shape[1]
    return pl.pallas_call(
        norm_project_kernel,
        grid=(1,),
        in_specs=[
            pl.BlockSpec((rows, width), lambda i: (0, 0)),
            pl.BlockSpec((1, width), lambda i: (0, 0)),
            pl.BlockSpec((width, outputs), lambda i: (0, 0)),
            *[pl.BlockSpec(memory_space=pl.ANY)] * len(carried),
        ],
        out_specs=[
            pl.BlockSpec((rows, width), lambda i: (place, 0)),
            pl.BlockSpec((rows, outputs), lambda i: (place, 0)),
        ],
        out_shape=[jax.ShapeDtypeStruct((total, width), BF16), jax.ShapeDtypeStruct((total, outputs), F32)],
        input_output_aliases={3 + i: i for i in range(len(carried))},
        cost_estimate=pl.CostEstimate(flops=10**9, bytes_accessed=10**6, transcendentals=0),
        name="norm_project",
    )(block, gain[None], weight, *carried)


def swap_halves(values):
    lane = lax.broadcasted_iota(jnp.int32, values.shape, 1)
    ahead = pltpu.roll(values, values.shape[1] - HD // 2, 1)
    behind = pltpu.roll(values, HD // 2, 1)
    return jnp.where(lane % HD < HD // 2, ahead, behind)


def padded_keys(keys_values):
    lane = lax.broadcasted_iota(jnp.int32, keys_values.shape, 1)
    zero = jnp.zeros_like(keys_values)
    left = jnp.where(lane < HD, keys_values, zero)
    right = pltpu.roll(left, HD, 1)
    return jnp.concatenate([left, right], axis=0)


def padded_values(keys_values):
    lane = lax.broadcasted_iota(jnp.int32, keys_values.shape, 1)
    zero = jnp.zeros_like(keys_values)
    right = jnp.where(lane >= HD, keys_values, zero)
    left = pltpu.roll(right, HD, 1)
    return jnp.concatenate([left, right], axis=0)


def attention_forward_kernel(
    first, info, query_ref, kv_ref, cos_ref, sin_ref, cos_all, sin_all,
    attended_ref, rotated_ref, kv_out, lse_ref, keys_s, values_s, acc_s, max_s,
):
    step = pl.program_id(0) + first
    rows = query_ref.shape[0]
    pairs = query_ref.shape[1] // 128
    blocks = kv_ref.shape[0] // rows

    @pl.when(step == first)
    def _():
        for part in range(blocks):
            here = pl.ds(part * rows, rows)
            kv = kv_ref[here, :]
            lane = lax.broadcasted_iota(jnp.int32, kv.shape, 1)
            turned = kv * cos_all[here, :] + swap_halves(kv) * sin_all[here, :]
            kv = jnp.where(lane < HD, turned, kv).astype(BF16).astype(F32)
            kv_out[here, :] = kv.astype(BF16)
            keys_s[part] = (padded_keys(kv) * (1.0 / math.sqrt(HD))).astype(BF16)
            both = jnp.transpose(padded_values(kv))
            feature = lax.broadcasted_iota(jnp.int32, both.shape, 0)
            key = lax.broadcasted_iota(jnp.int32, both.shape, 1)
            ones = jnp.where((feature < HD) == (key < rows), 1.0, 0.0)
            values_s[part] = jnp.concatenate([both, ones], axis=0).astype(BF16)

    own = info[step]
    low = info[2 * blocks + step]
    key_index = lax.broadcasted_iota(jnp.int32, (2 * rows, rows), 0) % rows
    query_index = lax.broadcasted_iota(jnp.int32, (2 * rows, rows), 1)
    allowed = key_index <= query_index
    at = info[blocks + own]

    def spread(upper, lower, height):
        return jnp.concatenate(
            [jnp.broadcast_to(upper, (height, rows)), jnp.broadcast_to(lower, (height, rows))], axis=0
        )

    for pair in range(pairs):
        cols = pl.ds(pair * 128, 128)
        query = query_ref[:, cols]
        query = (query * cos_ref[...] + swap_halves(query) * sin_ref[...]).astype(BF16)
        rotated_ref[:, cols] = query
        scores = jnp.where(allowed, mm_nt(keys_s[at], query), NEG)
        tops = [jnp.max(scores[i * rows : (i + 1) * rows], axis=0, keepdims=True) for i in range(2)]
        probs = jnp.exp(scores - spread(*tops, rows)).astype(BF16)
        for i in range(2):
            max_s[2 * pair + i : 2 * pair + i + 1, :] = tops[i]
        acc_s[pair] = mm(values_s[at], probs)

    for back in range(1, blocks):

        @pl.when(own - back >= low)
        def _():
            there = info[blocks + jnp.maximum(own - back, 0)]
            for pair in range(pairs):
                query = rotated_ref[:, pl.ds(pair * 128, 128)]
                scores = mm_nt(keys_s[there], query)
                tops, scales = [], []
                for i in range(2):
                    before = max_s[2 * pair + i : 2 * pair + i + 1, :]
                    top = jnp.maximum(
                        before, jnp.max(scores[i * rows : (i + 1) * rows], axis=0, keepdims=True)
                    )
                    tops.append(top)
                    scales.append(jnp.exp(before - top))
                    max_s[2 * pair + i : 2 * pair + i + 1, :] = top
                probs = jnp.exp(scores - spread(*tops, rows)).astype(BF16)
                factor = spread(*scales, HD)
                factor = jnp.concatenate([factor, factor], axis=0)
                acc_s[pair] = acc_s[pair] * factor + mm(values_s[there], probs)

    for pair in range(pairs):
        total = acc_s[pair][128:, :]
        result = acc_s[pair][:128, :] / total
        attended_ref[:, pl.ds(pair * 128, 128)] = jnp.transpose(result).astype(BF16)
        for i in range(2):
            spot = slice(2 * pair + i, 2 * pair + i + 1)
            lse_ref[spot, :] = max_s[spot, :] + jnp.log(total[i * HD : i * HD + 1, :])


def attention_forward(info, qkv, cosine, sine, rows, first, count):
    total, width = qkv.shape
    blocks = total // rows
    query_width = width - 2 * HD
    pairs = query_width // 128
    last = query_width // 128
    return pl.pallas_call(
        functools.partial(attention_forward_kernel, first),
        grid_spec=pltpu.PrefetchScalarGridSpec(
            num_scalar_prefetch=1,
            grid=(count,),
            in_specs=[
                pl.BlockSpec((rows, query_width), lambda j, info: (j + first, 0)),
                pl.BlockSpec((total, 128), lambda j, info: (0, last)),
                pl.BlockSpec((rows, 128), lambda j, info: (j + first, 0)),
                pl.BlockSpec((rows, 128), lambda j, info: (j + first, 0)),
                pl.BlockSpec((total, 128), lambda j, info: (0, 0)),
                pl.BlockSpec((total, 128), lambda j, info: (0, 0)),
            ],
            out_specs=[
                pl.BlockSpec((rows, query_width), lambda j, info: (j, 0)),
                pl.BlockSpec((rows, query_width), lambda j, info: (j, 0)),
                pl.BlockSpec((total, 128), lambda j, info: (0, 0)),
                pl.BlockSpec((2 * pairs, rows), lambda j, info: (0, j)),
            ],
            scratch_shapes=[
                pltpu.VMEM((blocks, 2 * rows, 128), BF16),
                pltpu.VMEM((blocks, 256, 2 * rows), BF16),
                pltpu.VMEM((pairs, 256, rows), F32),
                pltpu.VMEM((2 * pairs, rows), F32),
            ],
        ),
        cost_estimate=pl.CostEstimate(flops=count * 4 * 10**9, bytes_accessed=count * 10**6, transcendentals=0),
        out_shape=[
            jax.ShapeDtypeStruct((count * rows, query_width), BF16),
            jax.ShapeDtypeStruct((count * rows, query_width), BF16),
            jax.ShapeDtypeStruct((total, 128), BF16),
            jax.ShapeDtypeStruct((2 * pairs, count * rows), F32),
        ],
        name="attention_forward",
    )(info, qkv, qkv, cosine, sine, cosine, sine)


def attention_backward_kernel(
    first, final, info, query_ref, att_ref, grad_ref, lse_ref, kv_ref, cos_ref, sin_ref, cos_all, sin_all, *refs
):
    if first:
        refs = refs[1:]
        key_in, value_in = refs[:2]
        refs = refs[2:]
    else:
        key_in = value_in = None
    out_ref, key_acc, value_acc = refs[:3]
    refs = refs[3:]
    if final:
        kv_out = refs[0]
        refs = refs[1:]
    keys_s, values_s, query_acc, delta_s = refs
    step = pl.program_id(0) + first
    rows = query_ref.shape[0]
    query_width = query_ref.shape[1]
    pairs = query_width // 128
    blocks = kv_ref.shape[0] // rows

    @pl.when(step == first)
    def _():
        for part in range(blocks):
            kv = kv_ref[pl.ds(part * rows, rows), :].astype(F32)
            keys_s[part] = (padded_keys(kv) * (1.0 / math.sqrt(HD))).astype(BF16)
            values_s[part] = padded_values(kv).astype(BF16)
        if first:
            key_acc[...] = key_in[...]
            value_acc[...] = value_in[...]
        else:
            key_acc[...] = jnp.zeros_like(key_acc)
            value_acc[...] = jnp.zeros_like(value_acc)

    own = info[step]
    low = info[2 * blocks + step]
    at = info[blocks + own]
    key_index = lax.broadcasted_iota(jnp.int32, (2 * rows, rows), 0) % rows
    query_index = lax.broadcasted_iota(jnp.int32, (2 * rows, rows), 1)
    allowed = key_index <= query_index
    top_half = lax.broadcasted_iota(jnp.int32, (2 * rows, rows), 0) < rows

    products = att_ref[...].astype(F32) * grad_ref[...].astype(F32)
    head_row = lax.broadcasted_iota(jnp.int32, (2 * pairs, query_width), 0)
    head_col = lax.broadcasted_iota(jnp.int32, (2 * pairs, query_width), 1) // HD
    picker = jnp.where(head_row == head_col, 1.0, 0.0)
    delta_s[...] = lax.dot_general(
        picker, products, (((1,), (1,)), ((), ())),
        precision=lax.Precision.HIGHEST, preferred_element_type=F32,
    )

    def one_block(where_, masked):
        keys = keys_s[where_]
        values = values_s[where_]
        for pair in range(pairs):
            cols = pl.ds(pair * 128, 128)
            query = query_ref[:, cols]
            grad = grad_ref[:, cols]
            lse = jnp.where(
                top_half, lse_ref[2 * pair : 2 * pair + 1, :], lse_ref[2 * pair + 1 : 2 * pair + 2, :]
            )
            delta = jnp.where(
                top_half, delta_s[2 * pair : 2 * pair + 1, :], delta_s[2 * pair + 1 : 2 * pair + 2, :]
            )
            scores = mm_nt(keys, query) - lse
            if masked:
                scores = jnp.where(allowed, scores, NEG)
            probs = jnp.exp(scores)
            grad_probs = mm_nt(values, grad)
            grad_scores = (probs * (grad_probs - delta)).astype(BF16)
            value_acc[where_] += mm(probs.astype(BF16), grad)
            key_acc[where_] += mm(grad_scores, query)
            part = mm_tn(grad_scores, keys)
            if masked:
                query_acc[:, cols] = part
            else:
                query_acc[:, cols] += part

    one_block(at, True)
    for back in range(1, blocks):

        @pl.when(own - back >= low)
        def _():
            one_block(info[blocks + jnp.maximum(own - back, 0)], False)

    for pair in range(pairs):
        cols = pl.ds(pair * 128, 128)
        grad = query_acc[:, cols].astype(BF16).astype(F32)
        out_ref[:, cols] = (grad * cos_ref[...] - swap_halves(grad) * sin_ref[...]).astype(BF16)

    if final:

        @pl.when(step == first + pl.num_programs(0) - 1)
        def _():
            lane = lax.broadcasted_iota(jnp.int32, (rows, 128), 1)
            for part in range(blocks):
                spot = pl.ds(part * rows, rows)
                key_grad = key_acc[part]
                key_grad = key_grad[:rows] + pltpu.roll(key_grad[rows:], HD, 1)
                key_grad = (key_grad * (1.0 / math.sqrt(HD))).astype(BF16).astype(F32)
                value_grad = value_acc[part]
                value_grad = pltpu.roll(value_grad[:rows], HD, 1) + value_grad[rows:]
                turned = key_grad * cos_all[spot, :] - swap_halves(key_grad) * sin_all[spot, :]
                kv_out[spot, :] = jnp.where(lane < HD, turned, value_grad).astype(BF16)


def attention_backward(info, query, attended, grad, lse, kv, cosine, sine, rows, first, count, carried):
    total, query_width = query.shape
    blocks = total // rows
    pairs = query_width // 128
    final = first + count == blocks
    row_block = pl.BlockSpec((rows, query_width), lambda j, info: (j + first, 0))
    table_block = pl.BlockSpec((rows, 128), lambda j, info: (j + first, 0))
    whole = pl.BlockSpec((total, 128), lambda j, info: (0, 0))
    sums = pl.BlockSpec((blocks, 2 * rows, 128), lambda j, info: (0, 0, 0))
    sums_shape = jax.ShapeDtypeStruct((blocks, 2 * rows, 128), F32)
    in_specs = [
        row_block, row_block,
        pl.BlockSpec((rows, query_width), lambda j, info: (j, 0)),
        pl.BlockSpec((2 * pairs, rows), lambda j, info: (0, j + first)),
        whole, table_block, table_block, whole, whole,
    ]
    operands = [info, query, attended, grad, lse, kv, cosine, sine, cosine, sine]
    aliases = {}
    if first:
        aliases = {len(operands): 0, len(operands) + 1: 1, len(operands) + 2: 2}
        operands += carried
        in_specs += [pl.BlockSpec(memory_space=pl.ANY), sums, sums]
    out_specs = [row_block, sums, sums]
    out_shape = [jax.ShapeDtypeStruct((total, query_width + 128), BF16), sums_shape, sums_shape]
    if final:
        out_specs.append(whole)
        out_shape.append(jax.ShapeDtypeStruct((total, 128), BF16))
    return pl.pallas_call(
        functools.partial(attention_backward_kernel, first, final),
        grid_spec=pltpu.PrefetchScalarGridSpec(
            num_scalar_prefetch=1,
            grid=(count,),
            in_specs=in_specs,
            out_specs=out_specs,
            scratch_shapes=[
                pltpu.VMEM((blocks, 2 * rows, 128), BF16),
                pltpu.VMEM((blocks, 2 * rows, 128), BF16),
                pltpu.VMEM((rows, query_width), F32),
                pltpu.VMEM((2 * pairs, rows), F32),
            ],
        ),
        out_shape=out_shape,
        input_output_aliases=aliases,
        cost_estimate=pl.CostEstimate(flops=count * 6 * 10**9, bytes_accessed=count * 10**6, transcendentals=0),
        name="attention_backward",
    )(*operands)


def feed_forward_kernel(parts, first_row, *refs):
    values_refs = refs[:parts]
    cotangent_refs = refs[parts : 2 * parts]
    grad_ref, gate_all, up_all = refs[2 * parts : 2 * parts + 3]
    back_refs = refs[-7 - parts : -7]
    rows_all, mixed_all, slopes_all, cotangents_all = refs[-11 - parts : -7 - parts]
    gate_w, up_w, rows_s, mixed_s, slopes_s, arrived, stored = refs[-7:]
    rows, width = values_refs[0].shape
    hidden = gate_w.shape[1]
    step = min(256, hidden)
    count, rest = divmod(hidden, step)

    def weight_copies(index, first, size):
        cols = pl.ds(first, size)
        return (
            pltpu.make_async_copy(gate_all.at[:, cols], gate_w.at[:, cols], arrived.at[0, index]),
            pltpu.make_async_copy(up_all.at[:, cols], up_w.at[:, cols], arrived.at[1, index]),
        )

    for index in range(count + (rest > 0)):
        for copy in weight_copies(index, index * step, step if index < count else rest):
            copy.start()
    for i in range(parts):
        rows_s[pl.ds(i * rows, rows), :] = values_refs[i][...]
    here = pl.ds(first_row, parts * rows)
    outs = [
        pltpu.make_async_copy(scratch, whole.at[here, :], stored.at[i])
        for i, (scratch, whole) in enumerate(((rows_s, rows_all), (mixed_s, mixed_all), (slopes_s, slopes_all)))
    ]
    outs[0].start()
    moves = [
        pltpu.make_async_copy(
            cotangent_refs[i], cotangents_all.at[pl.ds(first_row + i * rows, rows), :], stored.at[3 + i]
        )
        for i in range(parts)
    ]
    for copy in moves:
        copy.start()

    def columns(index, first, size):
        for copy in weight_copies(index, first, size):
            copy.wait()
        cols = pl.ds(first, size)
        values = rows_s[...]
        gate = mm(values, gate_w[:, cols])
        upward = mm(values, up_w[:, cols])
        grad = grad_ref[:, cols]
        sigma = 1.0 / (1.0 + jnp.exp(-gate))
        activated = gate * sigma
        mixed_s[:, cols] = (activated * upward).astype(BF16)
        slopes_s[:, cols] = (grad * upward * sigma * (1.0 + gate * (1.0 - sigma))).astype(BF16)
        slopes_s[:, pl.ds(hidden + first, size)] = (grad * activated).astype(BF16)

    @pl.loop(0, count)
    def _(index):
        columns(index, pl.multiple_of(index * step, 128), step)

    if rest:
        columns(count, hidden - rest, rest)
    outs[1].start()
    outs[2].start()

    part = min(256, width)

    @pl.loop(0, width // part)
    def _(index):
        here = pl.ds(pl.multiple_of(index * part, part), part)
        result = mm_nt(slopes_s[:, :hidden], gate_w[here, :]) + mm_nt(slopes_s[:, hidden:], up_w[here, :])
        for i in range(parts):
            back_refs[i][:, here] = result[i * rows : (i + 1) * rows].astype(BF16)

    for copy in outs + moves:
        copy.wait()


def feed_forward(values, cotangents, grad_mixed, grad_first, gate_weight, up_weight, first, total, carried):
    parts = len(values)
    rows, width = values[0].shape
    hidden = grad_mixed.shape[1]
    size = parts * rows
    block = grad_first // size
    anywhere = pl.BlockSpec(memory_space=pl.ANY)
    operands = [*values, *cotangents, grad_mixed, gate_weight, up_weight, *carried]
    single = pl.BlockSpec((rows, width), lambda i: (0, 0))
    here = pl.BlockSpec((size, hidden), lambda i: (block, 0))
    return pl.pallas_call(
        functools.partial(feed_forward_kernel, parts, first),
        grid=(1,),
        in_specs=[*[single] * (2 * parts), here, *[anywhere] * (2 + len(carried))],
        out_specs=[*[anywhere] * 4, *[single] * parts],
        scratch_shapes=[
            pltpu.VMEM((width, hidden), BF16),
            pltpu.VMEM((width, hidden), BF16),
            pltpu.VMEM((size, width), BF16),
            pltpu.VMEM((size, hidden), BF16),
            pltpu.VMEM((size, 2 * hidden), BF16),
            pltpu.SemaphoreType.DMA((2, -(-hidden // 256))),
            pltpu.SemaphoreType.DMA((3 + parts,)),
        ],
        out_shape=[
            jax.ShapeDtypeStruct((total, width), BF16),
            jax.ShapeDtypeStruct((total, hidden), BF16),
            jax.ShapeDtypeStruct((total, 2 * hidden), BF16),
            jax.ShapeDtypeStruct((total, width), BF16),
            *[jax.ShapeDtypeStruct((rows, width), BF16)] * parts,
        ],
        input_output_aliases={2 * parts + 3 + i: i for i in range(len(carried))},
        cost_estimate=pl.CostEstimate(flops=parts * 6 * 10**9, bytes_accessed=10**6, transcendentals=0),
        name="feed_forward",
    )(*operands)


def weight_gradient_kernel(values_ref, grad_ref, out_ref):
    out_ref[...] = mm_tn(values_ref[...], grad_ref[...]).astype(BF16)


def weight_gradient(values, grad):
    total, features = values.shape
    outputs = grad.shape[1]
    tile = math.gcd(512, features)
    return pl.pallas_call(
        weight_gradient_kernel,
        grid=(features // tile,),
        in_specs=[
            pl.BlockSpec((total, tile), lambda i: (0, i)),
            pl.BlockSpec((total, outputs), lambda i: (0, 0)),
        ],
        out_specs=pl.BlockSpec((tile, outputs), lambda i: (i, 0)),
        out_shape=jax.ShapeDtypeStruct((features, outputs), BF16),
        cost_estimate=pl.CostEstimate(
            flops=2 * total * features * outputs, bytes_accessed=10**6, transcendentals=0
        ),
        name="weight_gradient",
    )(values, grad)


def norm_scale(values):
    return lax.rsqrt(jnp.mean(values * values, axis=-1, keepdims=True) + EPS)


def norm_backward(values, scale, gain, grads):
    weighted = grads * gain
    gain_grad = jnp.sum(grads * values * scale, axis=0)
    cubed = scale * scale * scale
    value_grad = scale * weighted - values * cubed * jnp.mean(weighted * values, axis=-1, keepdims=True)
    return gain_grad, value_grad


def second_norm_backward_kernel(
    hidden_ref, gain_ref, cotangent_ref, first_ref, second_ref, third_ref, grad_ref, branch_ref, gain_grad_ref
):
    step = pl.program_id(0)
    values = hidden_ref[...]
    grads = first_ref[...].astype(F32) + second_ref[...].astype(F32) + third_ref[...].astype(F32)
    scale = lax.rsqrt(jnp.mean(values * values, axis=-1, keepdims=True) + EPS)
    weighted = grads * gain_ref[...]
    scaled = values * scale
    share = jnp.mean(weighted * values, axis=-1, keepdims=True) * (scale * scale)
    grad = cotangent_ref[...].astype(F32) + scale * weighted - scaled * share
    grad_ref[...] = grad
    branch_ref[...] = grad.astype(BF16)
    part = jnp.sum(grads * scaled, axis=0, keepdims=True)

    @pl.when(step == 0)
    def _():
        gain_grad_ref[...] = part

    @pl.when(step > 0)
    def _():
        gain_grad_ref[...] += part


def second_norm_backward(hidden, gain, cotangent, terms):
    rows, width = hidden.shape
    tile = math.gcd(128, rows)
    block = pl.BlockSpec((tile, width), lambda i: (i, 0))
    whole = pl.BlockSpec((1, width), lambda i: (0, 0))
    grad, branch, gain_grad = pl.pallas_call(
        second_norm_backward_kernel,
        grid=(rows // tile,),
        in_specs=[block, whole, *[block] * 4],
        out_specs=[block, block, whole],
        out_shape=[
            jax.ShapeDtypeStruct((rows, width), F32),
            jax.ShapeDtypeStruct((rows, width), BF16),
            jax.ShapeDtypeStruct((1, width), F32),
        ],
        cost_estimate=pl.CostEstimate(flops=10**9, bytes_accessed=10**6, transcendentals=0),
        name="second_norm_backward",
    )(hidden, gain[None], cotangent, *terms)
    return grad, branch, gain_grad[0]


def over_batch(term):
    return lax.psum_scatter(term, "batch", scatter_dimension=0, tiled=True)


def pick(parts, index, axis):
    return lax.dynamic_index_in_dim(parts, index, axis, keepdims=False)


def line_sum(term, waits):
    batch_parts = lax.axis_size("batch")
    line = batch_parts // 2
    index = lax.axis_index("batch")
    core, place = index % 2, index // 2
    parts = term.reshape(line, 2, term.shape[0] // batch_parts, term.shape[1])
    swap = [(i, i ^ 1) for i in range(batch_parts)]
    arrived = lax.ppermute(pick(parts, 1 - core, 1), "batch", swap)
    parts = (pick(parts, core, 1).astype(F32) + arrived.astype(F32)).astype(BF16)
    up = down = None
    for step in range(1, line):
        parts, up, down = lax.optimization_barrier((parts, up, down, *waits.get(step, ())))[:3]
        rising = pick(parts, jnp.minimum(place + line - step, line - 1), 0)
        falling = pick(parts, jnp.maximum(place - line + step, 0), 0)
        if up is not None:
            rising = (rising.astype(F32) + up.astype(F32)).astype(BF16)
            falling = (falling.astype(F32) + down.astype(F32)).astype(BF16)
        up = lax.ppermute(rising, "batch", [(i, i + 2) for i in range(2 * step)])
        down = lax.ppermute(
            falling, "batch", [(i, i - 2) for i in range(batch_parts - 2 * step, batch_parts)]
        )
    return pick(after(parts, *waits.get(line, ())), place, 0), up, down


def split_total_kernel(own_ref, up_ref, down_ref, *out_refs):
    total = own_ref[...].astype(F32) + up_ref[...].astype(F32) + down_ref[...].astype(F32)
    first = 0
    for out_ref in out_refs:
        size = out_ref.shape[1]
        out_ref[...] = total[:, first : first + size]
        first += size


def split_total(terms, sizes):
    rows = terms[0].shape[0]
    return pl.pallas_call(
        split_total_kernel,
        out_shape=[jax.ShapeDtypeStruct((rows, size), F32) for size in sizes],
        cost_estimate=pl.CostEstimate(flops=10**8, bytes_accessed=10**6, transcendentals=0),
        name="split_total",
    )(*terms)


def shards(
    tokens, seq_count, query_weight, key_weight, value_weight, out_weight,
    gate_weight, up_weight, down_weight, attention_gain, feedforward_gain, cotangent,
):
    seq_parts = lax.axis_size("seq")
    batch_parts = lax.axis_size("batch")
    part = lax.axis_index("seq")
    parity = lax.axis_index("batch") % 2
    rows = tokens.shape[1]
    group_rows = rows * seq_parts
    width = tokens.shape[2]

    order = jnp.arange(seq_parts, dtype=jnp.int32)
    swapped = ((order & 1) << 1) | (order >> 1)
    masks = jnp.where(parity == 0, order, swapped)
    owners = part ^ masks
    other = part ^ order
    spots = jnp.where(parity == 0, other, ((other & 1) << 1) | (other >> 1))
    seq_length = group_rows // seq_count[0]
    firsts = (owners * rows) // seq_length * seq_length // rows
    info = jnp.concatenate([owners, spots, firsts]).astype(jnp.int32)

    index = (owners[:, None] * rows + jnp.arange(rows, dtype=jnp.int32)[None, :]).reshape(-1)
    places = index - index // seq_length * seq_length
    lane = jnp.arange(128, dtype=jnp.int32)
    inverse = jnp.exp((lane % (HD // 2)).astype(F32) * (-2.0 * math.log(10000.0) / HD))
    angles = places.astype(F32)[:, None] * inverse[None, :]
    cosine = jnp.cos(angles)
    sine = jnp.sin(angles) * jnp.where(lane % HD < HD // 2, -1.0, 1.0)[None, :]

    inputs = tokens[0].astype(F32)
    scale_one = norm_scale(inputs)
    qkv_weight = jnp.concatenate([query_weight, key_weight, value_weight], axis=1)
    half = group_rows // 2

    def project(block, place, carried):
        return norm_project(block, attention_gain, qkv_weight, place, group_rows, carried)

    near = first_swap(tokens[0])
    side = second_swap(tokens[0])
    carried = project(tokens[0], 0, [])
    near, side, *carried = lax.optimization_barrier((near, side, *carried))
    far = second_swap(near)
    carried = project(side, 2, project(near, 1, carried))
    normed_one_rows, qkv = project(far, 3, carried)

    grad_ffn = after(cotangent[0], far)
    grad_near = first_swap(grad_ffn)
    grad_side = second_swap(grad_ffn)

    att_upper, query_upper, kv, lse_upper = attention_forward(info, qkv, cosine, sine, rows, seq_parts // 2, seq_parts // 2)
    branch_upper = mm(att_upper, out_weight).astype(BF16)
    arrived = second_swap(branch_upper)
    later_qkv, grad_near, grad_side = lax.optimization_barrier((after(qkv, branch_upper), grad_near, grad_side))
    att_lower, query_lower, _, lse_lower = attention_forward(info, later_qkv, cosine, sine, rows, 0, seq_parts // 2)
    branch_lower = mm(att_lower, out_weight).astype(BF16)
    attended = jnp.concatenate([att_lower, att_upper], axis=0)
    query = jnp.concatenate([query_lower, query_upper], axis=0)
    lse = jnp.concatenate([lse_lower, lse_upper], axis=1)
    branch, passed = split_sum(branch_lower, after(arrived, branch_lower))
    passed = first_swap(passed)
    grad_mixed = mm_nt(jnp.concatenate([grad_near, grad_side, cotangent[0]], axis=0), down_weight)
    hidden = inputs + branch + after(passed, grad_mixed).astype(F32)

    scale_two = norm_scale(hidden)
    normed_two = (hidden * scale_two * feedforward_gain).astype(BF16)
    near = first_swap(normed_two)
    side = second_swap(normed_two)

    def feed(values, cotangents, grads, grad_first, first, carried):
        return feed_forward(
            values, cotangents, grads, grad_first, gate_weight, up_weight, first, group_rows, carried
        )

    *carried, back_own = feed([normed_two], [cotangent[0]], grad_mixed, 2 * rows, 3 * rows, [])
    near, side, grad_near, attended, query, lse, *carried = lax.optimization_barrier(
        (near, side, grad_near, attended, query, lse, *carried)
    )
    far = second_swap(near)
    grad_far = second_swap(grad_near)
    *carried, back_near, back_side = feed([near, side], [grad_near, grad_side], grad_mixed, 0, 0, carried)
    sum_side = second_swap(after(back_side, far))
    grad_mixed_far = mm_nt(after(grad_far, back_side), down_weight)
    *carried, back_far = feed([far], [grad_far], grad_mixed_far, 0, 2 * rows, carried)
    normed_two_rows, mixed, slopes, grad_rows = carried
    sum_far = second_swap(back_far)
    down_term = mm_tn(mixed, after(grad_rows, sum_side)).astype(BF16)
    near_sum = (back_near.astype(F32) + after(sum_far, down_term).astype(F32)).astype(BF16)
    passed = first_swap(near_sum)
    gate_up_term = weight_gradient(normed_two_rows, after(slopes, near_sum))
    down_grad = over_batch(down_term)
    gate_up_grad = over_batch(after(gate_up_term, passed))

    grad_hidden, grad_branch, feed_gain_term = second_norm_backward(
        hidden, feedforward_gain, cotangent[0], (back_own, sum_side, after(passed, gate_up_term))
    )
    near = first_swap(grad_branch)
    side = second_swap(grad_branch)

    def attended_grad(block):
        return mm_nt(block, out_weight).astype(BF16)

    def backward(grad, first, count, carried):
        return attention_backward(
            info, query, attended, grad, lse, kv, cosine, sine, rows, first, count, carried
        )

    ffn_upper = mm(after(mixed, grad_branch)[rows : 3 * rows], down_weight).astype(BF16)
    carried = backward(after(attended_grad(grad_branch), ffn_upper), 0, 1, [])
    near, side, *carried = lax.optimization_barrier((near, side, *carried))
    far = second_swap(near)
    middle = attended_grad(jnp.concatenate([near, side], axis=0))
    carried = backward(middle, 1, 2, carried)
    far = after(far, *carried)
    ffn_arrived = second_swap(after(ffn_upper, far))
    grad_branch_rows = jnp.concatenate([grad_branch, near, side, far], axis=0)
    out_term = mm_tn(attended, grad_branch_rows).astype(BF16)
    grad_qkv, _, _, grad_kv = backward(attended_grad(after(far, out_term)), 3, 1, carried)
    grad_qkv = lax.dynamic_update_slice(grad_qkv, grad_kv, (0, grad_qkv.shape[1] - grad_kv.shape[1]))
    upper = mm_nt(after(grad_qkv, down_grad, ffn_arrived)[half:], qkv_weight).astype(BF16)
    arrived = second_swap(upper)
    lower = mm_nt(after(grad_qkv, upper)[:half], qkv_weight).astype(BF16)
    qkv_term = weight_gradient(normed_one_rows, after(grad_qkv, upper))
    kept, passed = split_sum(lower, after(arrived, qkv_term, lower))
    arrived_passed = first_swap(passed)
    later_mixed = after(mixed, upper)
    ffn_passed = mm(later_mixed[:rows], down_weight) + ffn_arrived[rows:].astype(F32)
    ffn_passed = first_swap(ffn_passed.astype(BF16))
    ffn_kept = mm(later_mixed[3 * rows :], down_weight) + ffn_arrived[:rows].astype(F32)
    grad_normed_one = kept + arrived_passed.astype(F32)
    attention_gain_term, grad_inputs_norm = norm_backward(inputs, scale_one, attention_gain, grad_normed_one)
    input_grad = grad_hidden + grad_inputs_norm
    layer_out = (hidden + ffn_kept + ffn_passed.astype(F32)).astype(BF16)

    devices = seq_parts * batch_parts
    gains = jnp.concatenate(
        [attention_gain_term.reshape(devices, -1), feed_gain_term.reshape(devices, -1)], axis=1
    )
    gains = jnp.sum(lax.all_to_all(gains, ("seq", "batch"), 0, 0, tiled=True), axis=0)
    share = width // devices
    query_width = query_weight.shape[1]
    key_width = key_weight.shape[1]
    line = batch_parts // 2
    out_terms = line_sum(out_term, {1: (qkv_term,), 2: (lower,), 3: (passed,)})
    out_grad = sum(term.astype(F32) for term in out_terms)
    qkv_terms = line_sum(qkv_term, {1: (lower,), 2: (passed,), 3: (arrived_passed,), line: (gains,)})
    query_grad, key_grad, value_grad = split_total(qkv_terms, (query_width, key_width, key_width))
    gate_up_grad = after(gate_up_grad, gains, query_grad, out_grad)
    hidden_width = gate_weight.shape[1]
    return (
        layer_out[None],
        input_grad[None],
        query_grad,
        key_grad,
        value_grad,
        out_grad,
        gate_up_grad[:, :hidden_width].astype(F32),
        gate_up_grad[:, hidden_width:].astype(F32),
        down_grad.astype(F32),
        gains[:share],
        gains[share:],
    )


def solution(mesh):
    return jax.shard_map(
        shards,
        mesh=mesh,
        in_specs=(
            P("batch", "seq", None),
            P("batch"),
            P(None, "seq"),
            P(None, "seq"),
            P(None, "seq"),
            P("seq", None),
            P(None, "seq"),
            P(None, "seq"),
            P("seq", None),
            P(),
            P(),
            P("batch", "seq", None),
        ),
        out_specs=(
            P("batch", "seq", None),
            P("batch", "seq", None),
            P("batch", "seq"),
            P("batch", "seq"),
            P("batch", "seq"),
            P(("seq", "batch"), None),
            P("batch", "seq"),
            P("batch", "seq"),
            P(("seq", "batch"), None),
            P(("seq", "batch")),
            P(("seq", "batch")),
        ),
        check_vma=False,
    )
```
